32 devices in a mesh: dp: 8 (over z, x), mp: 4 (over y, core).
Axes of the slice: x: 2, y: 2, z: 4, core: 2. Of those that a mesh axis runs over, the one named last changes fastest.
Arguments:
- tokens: bfloat16 [2, 8, 256, 2048], P(None, 'dp'), may hold values from -6 to 6
- cotangent: bfloat16 [2, 8, 256, 2048], P(None, 'dp'), may hold values from -6 to 6
- row_length: int32 [2, 8], P(None, 'dp'), may hold values from 64 to 256, as said below
- first_gain: bfloat16 [2048], P('dp'), may hold values from 0.5 to 1.5
- value_weight: bfloat16 [2048, 2816], P('dp', 'mp'), may hold values from -0.125 to 0.125
- gelu_weight: bfloat16 [2048, 2816], P('dp', 'mp'), may hold values from -0.125 to 0.125
- conv_weight: bfloat16 [4, 2816], P(None, 'mp'), may hold values from -3 to 3
- conv_bias: bfloat16 [2816], P('mp'), may hold values from -3 to 3
- input_gate: bfloat16 [2816, 176], P('mp'), may hold values from -0.4375 to 0.4375
- input_bias: bfloat16 [2816], P('mp'), may hold values from -4 to 4
- recur_gate: bfloat16 [2816, 176], P('mp'), may hold values from -0.4375 to 0.4375
- recur_bias: bfloat16 [2816], P('mp'), may hold values from -4 to 4
- decay_param: bfloat16 [2816], P('mp'), may hold values from 2 to 9
- output_weight: bfloat16 [2816, 2048], P('mp', 'dp'), may hold values from -0.21875 to 0.21875
- second_gain: bfloat16 [2048], P('dp'), may hold values from 0.5 to 1.5
- mlp_gate: bfloat16 [2048, 6144], P(None, 'mp'), may hold values from -0.125 to 0.125
- mlp_up: bfloat16 [2048, 6144], P(None, 'mp'), may hold values from -0.125 to 0.125
- mlp_down: bfloat16 [6144, 2048], P('mp'), may hold values from -0.15625 to 0.15625
Outputs:
- layer_out: float32 [2, 8, 256, 2048], P(None, 'dp')
- input_grad: float32 [2, 8, 256, 2048], P(None, 'dp')
- first_gain_grad: float32 [2048], P('dp')
- value_weight_grad: float32 [2048, 2816], P('dp', 'mp')
- gelu_weight_grad: float32 [2048, 2816], P('dp', 'mp')
- conv_weight_grad: float32 [4, 2816], P(None, 'mp')
- conv_bias_grad: float32 [2816], P('mp')
- input_gate_grad: float32 [2816, 176], P('mp')
- input_bias_grad: float32 [2816], P('mp')
- recur_gate_grad: float32 [2816, 176], P('mp')
- recur_bias_grad: float32 [2816], P('mp')
- decay_param_grad: float32 [2816], P('mp')
- output_weight_grad: float32 [2816, 2048], P('mp', 'dp')
- second_gain_grad: float32 [2048], P('dp')
- mlp_gate_grad: float32 [2048, 6144], P('dp', 'mp')
- mlp_up_grad: float32 [2048, 6144], P('dp', 'mp')
- mlp_down_grad: float32 [6144, 2048], P('mp', 'dp')
The draws below stay inside these ranges and needn't reach their ends.
Inputs may be any that keep to these rules, and one draw needn't show every extreme that they name: `row_length`: every row's length is 256 or 64; both occur in every draw.
All inputs are finite; a program needn't handle non-finite values.
Results may differ from the reference program's by a relative error of at most 0.017.
Values may be sent and summed in bfloat16 or wider, within the bound.
No kernel may reach another device: no remote copies, remote signals or barrier semaphores. Data moves between devices by JAX's collectives and lax.ppermute only.
A program may use at most 320 MiB of HBM per device.

```python
import jax
import jax.numpy as jnp
from jax import lax

D = 2048
R = 2816
H = 16
HD = 176
FF = 6144
CONV = 4
SUBS = 2
LONG = 256
SHORT = 64
ROWS = 8


def draw_row_length(key, part):
    picks = jax.random.randint(key, (SUBS, ROWS), 0, 2)
    picks = picks.at[0, 0].set(1).at[0, 1].set(0)
    return jnp.where(picks == 1, LONG, SHORT).astype(jnp.int32)


def block_scale(key, extent, pieces, low, top_value):
    def one(position, blocks):
        draws = jax.random.uniform(jax.random.fold_in(jax.random.fold_in(key, 6), position), (blocks,), jnp.float32, low / len(pieces), top_value / len(pieces))
        return jnp.repeat(jnp.exp(draws), extent[position] // blocks).reshape((-1,) + (1,) * (len(extent) - position - 1))

    gain = one(*pieces[0])
    for cut in pieces[1:]:
        gain = gain * one(*cut)
    return gain


def scatter_about(key, extent, scale, bound, pieces=(), held_as=jnp.bfloat16):
    array = scale * jax.random.normal(key, extent, jnp.float32)
    if pieces:
        array = array * block_scale(key, extent, pieces, -0.22, 0.18)
    return jnp.clip(array, -bound, bound).astype(held_as)


def setup_inputs(seed: int = 0) -> dict:
    seeds = jax.random.split(jax.random.key(seed), 19)
    tokens = scatter_about(seeds[0], (SUBS, ROWS, LONG, D), 1.0, 6.0, ((1, 8),))
    cotangent = scatter_about(seeds[1], (SUBS, ROWS, LONG, D), 1.0, 6.0, ((1, 8),))
    row_length = draw_row_length(jax.random.fold_in(seeds[18], 71), 0)
    first_gain = jnp.clip(1.0 + 0.1 * jax.random.normal(seeds[3], (D,), jnp.float32), 0.5, 1.5).astype(jnp.bfloat16)
    value_weight = scatter_about(seeds[4], (D, R), D ** -0.5, 0.125, ((0, 8), (1, 4)))
    gelu_weight = scatter_about(seeds[5], (D, R), D ** -0.5, 0.125, ((0, 8), (1, 4)))
    conv_weight = scatter_about(seeds[6], (CONV, R), CONV ** -0.5, 3.0, ((1, 4),))
    conv_bias = scatter_about(seeds[7], (R,), 0.5, 3.0, ((0, 4),))
    input_gate = scatter_about(seeds[8], (R, HD), HD ** -0.5, 0.4375, ((0, 4),))
    input_bias = scatter_about(seeds[9], (R,), 1.0, 4.0, ((0, 4),))
    recur_gate = scatter_about(seeds[10], (R, HD), HD ** -0.5, 0.4375, ((0, 4),))
    recur_bias = scatter_about(seeds[11], (R,), 1.0, 4.0, ((0, 4),))
    decay_param = jnp.clip(2.0 + 7.0 * jax.random.uniform(seeds[12], (R,), jnp.float32) ** block_scale(seeds[12], (R,), ((0, 4),), -0.2, 0.2), 2.0, 9.0).astype(jnp.bfloat16)
    output_weight = scatter_about(seeds[13], (R, D), (R // 4) ** -0.5, 0.21875, ((0, 4), (1, 8)))
    second_gain = jnp.clip(1.0 + 0.1 * jax.random.normal(seeds[14], (D,), jnp.float32), 0.5, 1.5).astype(jnp.bfloat16)
    mlp_gate = scatter_about(seeds[15], (D, FF), D ** -0.5, 0.125, ((1, 4),))
    mlp_up = scatter_about(seeds[16], (D, FF), D ** -0.5, 0.125, ((1, 4),))
    mlp_down = scatter_about(seeds[17], (FF, D), (FF // 4) ** -0.5, 0.15625, ((0, 4),))
    return {"tokens": tokens, "cotangent": cotangent, "row_length": row_length, "first_gain": first_gain, "value_weight": value_weight, "gelu_weight": gelu_weight, "conv_weight": conv_weight, "conv_bias": conv_bias, "input_gate": input_gate, "input_bias": input_bias, "recur_gate": recur_gate, "recur_bias": recur_bias, "decay_param": decay_param, "output_weight": output_weight, "second_gain": second_gain, "mlp_gate": mlp_gate, "mlp_up": mlp_up, "mlp_down": mlp_down}


@jax.custom_vjp
def low(v):
    return lax.optimization_barrier(v.astype(jnp.bfloat16)).astype(jnp.float32)

@jax.custom_vjp
def low_back(v):
    return v

def low_keep(v):
    return (low(v), None)

def low_pass(kept, grad):
    return (grad,)

def back_keep(v):
    return (v, None)

def back_low(kept, grad):
    return (low(grad),)
low.defvjp(low_keep, low_pass)
low_back.defvjp(back_keep, back_low)
EPSILON = 1e-06
DECAY_SCALE = 8.0

def rms_scale(values, weights):
    return values * lax.rsqrt(lax.optimization_barrier(jnp.mean(values * values, -1, keepdims=True)) + EPSILON) * weights

def linear_combine(earlier, later):
    return (earlier[0] * later[0], later[0] * earlier[1] + later[1])

def shift_earlier(values, steps):
    length = values.shape[1]
    return jnp.pad(values, ((0, 0), (steps, 0), (0, 0)))[:, :length]

def gate_piece(linear_input, linear_recur, mixed, input_shift, recur_shift, decay_full):
    input_open = jax.nn.sigmoid(linear_input + input_shift)
    recur_open = jax.nn.sigmoid(linear_recur + recur_shift)
    log_decay = -DECAY_SCALE * recur_open * jax.nn.softplus(-decay_full)
    decay = jnp.exp(log_decay)
    scaler = jnp.sqrt(-jnp.expm1(2.0 * log_decay))
    return (decay, scaler * input_open * mixed)

def gelu_product(gate_act, upward):
    return jax.nn.gelu(gate_act, approximate=True) * upward

def dense(left, right):
    return jnp.einsum('bld,de->ble', left, right, precision=lax.Precision.HIGHEST)

def block_apply(values, blocks):
    batch, length, width = values.shape
    split = values.reshape(batch, length, H, width // H)
    cube = blocks.reshape(H, width // H, width // H)
    return jnp.einsum('blhi,hij->blhj', split, cube, precision=lax.Precision.HIGHEST).reshape(batch, length, width)

def forward(layer_in, gain_first, value_full, gelu_full, conv_full, conv_shift, input_full, input_shift, recur_full, recur_shift, decay_full, output_full, gain_second, gate_full, upward_full, downward_full):
    normed = low(rms_scale(layer_in, gain_first))
    branch_value = low_back(dense(normed, value_full))
    branch_gelu = low_back(dense(normed, gelu_full))
    gelu_out = jax.nn.gelu(branch_gelu, approximate=True)
    mixed = conv_shift + sum((conv_full[k] * shift_earlier(branch_value, k) for k in range(CONV)))
    mixed = low(mixed)
    linear_input = low_back(block_apply(mixed, input_full))
    linear_recur = low_back(block_apply(mixed, recur_full))
    decay, driven = gate_piece(linear_input, linear_recur, mixed, input_shift, recur_shift, decay_full)
    hidden = lax.associative_scan(linear_combine, (decay, driven), axis=1)[1]
    product = low(hidden * gelu_out)
    residual = layer_in + low_back(dense(product, output_full))
    normed_two = low(rms_scale(residual, gain_second))
    gate_act = low_back(dense(normed_two, gate_full))
    upward = low_back(dense(normed_two, upward_full))
    inner = low(gelu_product(gate_act, upward))
    return residual + dense(inner, downward_full)

def reference(tokens, cotangent, row_length, first_gain, value_weight, gelu_weight, conv_weight, conv_bias, input_gate, input_bias, recur_gate, recur_bias, decay_param, output_weight, second_gain, mlp_gate, mlp_up, mlp_down):
    params = tuple((item.astype(jnp.float32) for item in (first_gain, value_weight, gelu_weight, conv_weight, conv_bias, input_gate, input_bias, recur_gate, recur_bias, decay_param, output_weight, second_gain, mlp_gate, mlp_up, mlp_down)))
    positions = jnp.arange(LONG, dtype=jnp.int32)
    valid = (positions[None, None, :] < row_length[:, :, None]).astype(jnp.float32)
    grads_in = cotangent.astype(jnp.float32) * valid[..., None]
    groups = SUBS * ROWS // 8
    layer_in = tokens.astype(jnp.float32).reshape(groups, 8, LONG, D)
    grads_in = grads_in.reshape(groups, 8, LONG, D)

    def group_step(totals, pair):
        values, grads = pair
        result, pull = jax.vjp(forward, values, *params)
        pulled = pull(grads)
        return (tuple((left + right for left, right in zip(totals, pulled[1:]))), (result, pulled[0]))
    start = tuple((jnp.zeros_like(item) for item in params))
    totals, (results, inputs_back) = lax.scan(group_step, start, (layer_in, grads_in))
    return (results.reshape(SUBS, ROWS, LONG, D), inputs_back.reshape(SUBS, ROWS, LONG, D), totals[0], totals[1], totals[2], totals[3], totals[4], totals[5], totals[6], totals[7], totals[8], totals[9], totals[10], totals[11], totals[12], totals[13], totals[14])
```

```python
import jax
import jax.numpy as jnp
from jax import lax
from jax.experimental import pallas as pl
from jax.experimental.pallas import tpu as pltpu
from jax.sharding import PartitionSpec as P

EPSILON = 1e-06
DECAY_SCALE = 8.0
GELU_A = 0.7978845608028654
GELU_B = 0.044715
BF16 = jnp.bfloat16
F32 = jnp.float32
STEP = 16
HALF = 8
SUMS = 8
TN = (((0,), (0,)), ((), ()))


def gelu(v):
    return 0.5 * v * (1.0 + jnp.tanh(GELU_A * (v + GELU_B * v * v * v)))


def gelu_both(v):
    squared = v * v
    bent = jnp.tanh(GELU_A * v * (1.0 + GELU_B * squared))
    value = 0.5 * v * (1.0 + bent)
    slope = 0.5 * (1.0 + bent) + 0.5 * v * (1.0 - bent * bent) * GELU_A * (
        1.0 + 3.0 * GELU_B * squared
    )
    return value, slope


def negative_expm1(z, exp_z):
    series = 1.0 + z * (1.0 / 7.0)
    for k in (6.0, 5.0, 4.0, 3.0, 2.0):
        series = 1.0 + z * (1.0 / k) * series
    return jnp.where(z > -0.25, -z * series, 1.0 - exp_z)


def rows_of(shape):
    return lax.broadcasted_iota(jnp.int32, shape, 0)


def earlier(now, before, k, rows):
    return jnp.where(rows < k, pltpu.roll(before, k, 0), pltpu.roll(now, k, 0))


def later(now, after, k, rows):
    size = now.shape[0]
    return jnp.where(
        rows >= size - k, pltpu.roll(after, size - k, 0), pltpu.roll(now, size - k, 0)
    )


def mixer_forward_kernel(
    seqs, bx, by, taps, tap_bias, blocks_i, blocks_r, bias_i, bias_r, soft, p_o, cx_o, lx_o, lr_o, h_o
):
    total, width = bx.shape
    length = total // seqs
    steps = length // STEP
    rows16 = rows_of((STEP, width))
    w = [jnp.broadcast_to(taps[k : k + 1, :], (STEP, width)) for k in range(taps.shape[0])]
    shift = jnp.broadcast_to(tap_bias[...], (STEP, width))
    for seq in range(seqs):

        def conv(i, before):
            at = pl.ds(pl.multiple_of(seq * length + i * STEP, STEP), STEP)
            now = bx[at, :]
            mixed = shift + w[0] * now
            for k in range(1, taps.shape[0]):
                mixed = mixed + w[k] * earlier(now, before, k, rows16)
            cx_o[at, :] = mixed.astype(BF16)
            return now

        lax.fori_loop(0, steps, conv, jnp.zeros((STEP, width), F32))
    lx_o[...] = jnp.dot(cx_o[...], blocks_i[...], preferred_element_type=F32) + bias_i[...]
    lr_o[...] = jnp.dot(cx_o[...], blocks_r[...], preferred_element_type=F32) + bias_r[...]
    rows8 = rows_of((HALF, width))
    soft8 = jnp.broadcast_to(-DECAY_SCALE * soft[...], (HALF, width))

    def scan(i, carries):
        out = []
        for seq in range(seqs):
            carry = carries[seq]
            base = seq * length + i * STEP
            at = pl.ds(pl.multiple_of(base, STEP), STEP)
            cx16 = cx_o[at, :].astype(F32)
            products = []
            for part in range(STEP // HALF):
                here = pl.ds(pl.multiple_of(base + part * HALF, HALF), HALF)
                cx = cx16[part * HALF : (part + 1) * HALF, :]
                ix = jax.nn.sigmoid(lx_o[here, :])
                la = soft8 * jax.nn.sigmoid(lr_o[here, :])
                a = jnp.exp(la)
                rest = negative_expm1(2.0 * la, a * a)
                m = jnp.where(rest > 0.0, rest * lax.rsqrt(rest), 0.0)
                u = m * ix * cx
                for s in (1, 2, 4):
                    keep = rows8 >= s
                    u = u + jnp.where(keep, a * pltpu.roll(u, s, 0), 0.0)
                    a = jnp.where(keep, a * pltpu.roll(a, s, 0), a)
                h = u + a * carry
                carry = jnp.broadcast_to(h[HALF - 1 : HALF, :], (HALF, width))
                h_o[here, :] = h
                products.append(h * gelu(by[here, :]))
            p_o[at, :] = jnp.concatenate(products, 0).astype(BF16)
            out.append(carry)
        return tuple(out)

    lax.fori_loop(0, steps, scan, tuple(jnp.zeros((HALF, width), F32) for _ in range(seqs)))


def mixer_forward(seqs, bx, by, taps, tap_bias, blocks_i, blocks_r, bias_i, bias_r, soft):
    total, width = bx.shape
    low = jax.ShapeDtypeStruct((total, width), BF16)
    full = jax.ShapeDtypeStruct((total, width), F32)
    return pl.pallas_call(
        lambda *refs: mixer_forward_kernel(seqs, *refs),
        out_shape=(low, low, full, full, full),
        compiler_params=pltpu.CompilerParams(vmem_limit_bytes=40 << 20),
        cost_estimate=pl.CostEstimate(
            flops=4 * total * width * width, bytes_accessed=total * width * 24, transcendentals=6 * total * width
        ),
        name="mixer_forward",
    )(bx, by, taps, tap_bias, blocks_i, blocks_r, bias_i, bias_r, soft)


def mixer_backward_kernel(seqs, head, ring_size, dhr, *refs):
    outputs = refs[:ring_size]
    bx, by, cx_i, lx_i, lr_i, h_i, taps, blocks_i, blocks_r, soft, gate_soft = refs[ring_size : ring_size + 11]
    dbx_o, dby_o, gate_i_o, gate_r_o, dlx_o, dlr_o, dcx_s, dp = refs[ring_size + 11 :]
    for o in range(ring_size):
        part = jnp.dot(dhr[o], outputs[o][...], preferred_element_type=F32)
        dp[...] = part if o == 0 else dp[...] + part
    total, width = bx.shape
    length = total // seqs
    steps = length // STEP
    rows8 = rows_of((HALF, width))
    soft8 = jnp.broadcast_to(-DECAY_SCALE * soft[...], (HALF, width))
    zero = jnp.zeros((HALF, width), F32)

    def scan(j, state):
        i = steps - 1 - j
        sums_i, sums_r, sums_d = state[0]
        out = []
        for seq in range(seqs):
            a_after, e_after = state[1][seq]
            base = seq * length + i * STEP
            at = pl.ds(pl.multiple_of(base, STEP), STEP)
            cx16 = cx_i[at, :].astype(F32)
            dby_parts, dlx_parts, dlr_parts = [None, None], [None, None], [None, None]
            for part in (1, 0):
                start = base + part * HALF
                here = pl.ds(pl.multiple_of(start, HALF), HALF)
                cx = cx16[part * HALF : (part + 1) * HALF, :]
                ix = jax.nn.sigmoid(lx_i[here, :])
                ra = jax.nn.sigmoid(lr_i[here, :])
                la = soft8 * ra
                a = jnp.exp(la)
                rest = negative_expm1(2.0 * la, a * a)
                inverse = lax.rsqrt(rest)
                m = rest * inverse
                h = h_i[here, :]
                first = (i == 0) if part == 0 else False
                back = jnp.maximum(start - HALF, 0)
                before = h_i[pl.ds(pl.multiple_of(back, HALF), HALF), :]
                if part == 0:
                    before = jnp.where(i == 0, 0.0, before)
                h_prev = earlier(h, before, 1, rows8)
                gy, slope = gelu_both(by[here, :])
                grad = dp[here, :]
                dby_parts[part] = grad * h * slope
                e = grad * gy
                f = later(a, a_after, 1, rows8)
                for s in (1, 2, 4):
                    keep = rows8 < HALF - s
                    e = e + jnp.where(keep, f * pltpu.roll(e, HALF - s, 0), 0.0)
                    f = jnp.where(keep, f * pltpu.roll(f, HALF - s, 0), f)
                e = e + f * e_after
                e_after = jnp.broadcast_to(e[0:1, :], (HALF, width))
                a_after = a
                eix = e * ix
                dla = (e * h_prev - eix * cx * a * inverse) * a
                dlx = eix * m * cx * (1.0 - ix)
                dlr = dla * la * (1.0 - ra)
                sums_i = sums_i + dlx
                sums_r = sums_r + dlr
                sums_d = sums_d + dla * ra
                dlx_parts[part], dlr_parts[part] = dlx, dlr
                dcx_s[here, :] = eix * m
            dby_o[at, :] = jnp.concatenate(dby_parts, 0).astype(BF16)
            dlx_o[at, :] = jnp.concatenate(dlx_parts, 0).astype(BF16)
            dlr_o[at, :] = jnp.concatenate(dlr_parts, 0).astype(BF16)
            out.append((a_after, e_after))
        return (sums_i, sums_r, sums_d), tuple(out)

    (sums_i, sums_r, sums_d), _ = lax.fori_loop(
        0, steps, scan, ((zero, zero, zero), tuple((zero, zero) for _ in range(seqs)))
    )
    transposed = (((1,), (1,)), ((), ()))
    dcx_s[...] += lax.dot_general(
        dlx_o[...], blocks_i[...], transposed, preferred_element_type=F32
    ) + lax.dot_general(dlr_o[...], blocks_r[...], transposed, preferred_element_type=F32)
    count = taps.shape[0]
    rows16 = rows_of((STEP, width))
    w = [jnp.broadcast_to(taps[k : k + 1, :], (STEP, width)) for k in range(count)]
    zero16 = jnp.zeros((STEP, width), F32)
    sums_t = tuple(zero16 for _ in range(count))
    sums_b = zero16
    for seq in range(seqs):

        def conv(j, state):
            after, tap_sums, shift_sum = state
            at = pl.ds(pl.multiple_of(seq * length + (steps - 1 - j) * STEP, STEP), STEP)
            now = dcx_s[at, :]
            source = bx[at, :]
            grad = w[0] * now
            new_sums = [tap_sums[0] + now * source]
            for k in range(1, count):
                moved = later(now, after, k, rows16)
                grad = grad + w[k] * moved
                new_sums.append(tap_sums[k] + moved * source)
            dbx_o[at, :] = grad.astype(BF16)
            return now, tuple(new_sums), shift_sum + now

        _, sums_t, sums_b = lax.fori_loop(0, steps, conv, (zero16, sums_t, sums_b))
    lines = [jnp.sum(item, 0, keepdims=True) for item in (*sums_t, sums_b, sums_i, sums_r)]
    lines.append(DECAY_SCALE * gate_soft[...] * jnp.sum(sums_d, 0, keepdims=True))
    for place, line in enumerate(lines):
        for i in range(width // head):
            gate_i_o[width + i * SUMS + place : width + i * SUMS + place + 1, :] = line[:, i * head : (i + 1) * head]
    for grads, out in ((dlx_o, gate_i_o), (dlr_o, gate_r_o)):
        whole = lax.dot_general(cx_i[...], grads[...], TN, preferred_element_type=F32)
        for i in range(width // head):
            at = slice(i * head, (i + 1) * head)
            out[at, :] = whole[at, at]


def mixer_backward(
    seqs, dhr, outputs, bx, by, cx, lx, lr, h, taps, blocks_i, blocks_r, soft, gate_soft, head
):
    total, width = bx.shape
    ring_size = len(outputs)
    low = jax.ShapeDtypeStruct((total, width), BF16)
    gate = jax.ShapeDtypeStruct((width, head), F32)
    gate_sums = jax.ShapeDtypeStruct((width + SUMS * (width // head), head), F32)
    return pl.pallas_call(
        lambda *refs: mixer_backward_kernel(seqs, head, ring_size, *refs),
        out_shape=(low, low, gate_sums, gate),
        scratch_shapes=[
            pltpu.VMEM((total, width), BF16),
            pltpu.VMEM((total, width), BF16),
            pltpu.VMEM((total, width), F32),
            pltpu.VMEM((total, width), F32),
        ],
        compiler_params=pltpu.CompilerParams(vmem_limit_bytes=40 << 20),
        cost_estimate=pl.CostEstimate(
            flops=14 * total * width * width, bytes_accessed=total * width * 36, transcendentals=8 * total * width
        ),
        name="mixer_backward",
    )(dhr, *outputs, bx, by, cx, lx, lr, h, taps, blocks_i, blocks_r, soft, gate_soft)


def smem():
    return pl.BlockSpec(memory_space=pltpu.SMEM)


def vmem(count):
    return [pl.BlockSpec(memory_space=pltpu.VMEM)] * count


def params():
    return pltpu.CompilerParams(vmem_limit_bytes=40 << 20)


def cost(flops, bytes_accessed, transcendentals=0):
    return pl.CostEstimate(flops=flops, bytes_accessed=bytes_accessed, transcendentals=transcendentals)


def shaped(shape, dtype):
    return jax.ShapeDtypeStruct(shape, dtype)


def prepare_kernel(scalars, slots, tokens, cotangent, x_o, g_o, flat_o, r_o):
    ring_size, total, block = x_o.shape
    half = total // 2
    row_count = (scalars.shape[0] - 1) // 2
    length = half // row_count
    rows = lax.broadcasted_iota(jnp.int32, (length, block), 0)
    for place in range(2):
        sub = scalars[0] if place == 0 else 1 - scalars[0]
        for row in range(row_count):
            at = slice(place * half + row * length, place * half + (row + 1) * length)
            source = pl.ds(row * length, length)
            valid = jnp.where(rows < scalars[1 + sub * row_count + row], 1.0, 0.0)
            squares = jnp.zeros((length, block), F32)
            for k in range(ring_size):
                columns = slice(k * block, (k + 1) * block)
                piece = tokens[sub, source, columns]
                wide = piece.astype(F32)
                squares = squares + wide * wide
                x_o[slots[k], at, :] = piece
                masked = (cotangent[sub, source, columns].astype(F32) * valid).astype(BF16)
                g_o[slots[k], at, :] = masked
                flat_o[at, columns] = masked
            mean = jnp.sum(squares, 1, keepdims=True) * (1.0 / (ring_size * block))
            r_o[at, :] = lax.rsqrt(mean + EPSILON)


def prepare(scalars, slots, tokens, cotangent, ring_size):
    subs, half, model = tokens.shape
    total = subs * half
    rel = shaped((ring_size, total, model // ring_size), BF16)
    return pl.pallas_call(
        prepare_kernel,
        in_specs=[smem(), smem(), *vmem(2)],
        out_shape=(rel, rel, shaped((total, model), BF16), shaped((total, 1), F32)),
        compiler_params=params(),
        cost_estimate=cost(8 * total * model, 10 * total * model),
        name="prepare",
    )(scalars, slots, tokens, cotangent)


def project_kernel(offsets, first, width, *refs):
    count = len(offsets)
    x, r1 = refs[:2]
    value, gelu_w = refs[2 : 2 + count], refs[2 + count : 2 + 2 * count]
    rest = refs[2 + 2 * count :]
    if not first:
        before = rest[:2]
        rest = rest[2:]
    bx, by, n1_o, gains_o = rest
    block = x.shape[2]
    spare = value[0].shape[1] - width
    lines = block // spare
    scale = r1[...]
    for i, o in enumerate(offsets):
        slab = value[i][0:16, width:].astype(F32)
        gains = [
            jnp.concatenate([slab[g * lines + k : g * lines + k + 1, :] for k in range(lines)], 1)
            for g in range(2)
        ]
        gains_o[i, 0:1, :] = gains[0]
        gains_o[i, 1:2, :] = gains[1]
        n1 = (x[o].astype(F32) * scale * gains[0]).astype(BF16)
        n1_o[i] = n1
        for out, weight, place in ((bx, value[i][:, :width], 0), (by, gelu_w[i][...], 1)):
            part = jnp.dot(n1, weight, preferred_element_type=F32)
            if i == 0:
                out[...] = part if first else before[place][...] + part
            else:
                out[...] += part


def project(offsets, x, r1, value, gelu_w, before, width):
    total, block = x.shape[1:]
    count = len(offsets)
    first = before is None
    full = shaped((total, width), F32)
    extra = () if first else before
    at = 2 + 2 * count
    return pl.pallas_call(
        lambda *refs: project_kernel(offsets, first, width, *refs),
        in_specs=vmem(2 + 2 * count + len(extra)),
        out_shape=(full, full, shaped((count, total, block), BF16), shaped((count, 2, block), F32)),
        input_output_aliases={} if first else {at: 0, at + 1: 1},
        compiler_params=params(),
        cost_estimate=cost(4 * count * total * block * width, count * block * (4 * width + 4 * total)),
        name="project",
    )(x, r1, *value, *gelu_w, *extra)


NT = (((1,), (1,)), ((), ()))


def emit_kernel(ring_size, factors, *refs):
    half = refs[-1].shape[1]
    left = refs[:factors]
    own_o, other_o = refs[-2:]
    for o in range(ring_size):
        part = None
        for f in range(factors):
            weight = refs[factors + f * ring_size + o]
            width = left[f].shape[1]
            term = lax.dot_general(left[f][...], weight[:, :width], NT, preferred_element_type=F32)
            part = term if part is None else part + term
        own_o[o] = part[:half]
        other_o[o] = part[half:].astype(BF16)


def emit(lefts, weights, name):
    total, width = lefts[0].shape
    ring_size = len(weights[0])
    block = weights[0][0].shape[0]
    half = total // 2
    flat = [item for group in weights for item in group]
    return pl.pallas_call(
        lambda *refs: emit_kernel(ring_size, len(lefts), *refs),
        in_specs=vmem(len(lefts) + len(flat)),
        out_shape=(shaped((ring_size, half, block), F32), shaped((ring_size, half, block), BF16)),
        compiler_params=params(),
        cost_estimate=cost(
            2 * len(lefts) * total * width * ring_size * block, ring_size * block * (2 * width + 3 * total)
        ),
        name=name,
    )(*lefts, *flat)


def norm_kernel(x, pair, other, gains, h_o, n_o, r_o):
    ring_size, half, block = h_o.shape
    squares = jnp.zeros((half, block), F32)
    for o in range(ring_size):
        h = x[o, 0:half, :].astype(F32) + (pair[o].astype(F32) + other[o].astype(F32))
        h_o[o] = h
        squares = squares + h * h
    mean = jnp.sum(squares, 1, keepdims=True) * (1.0 / (ring_size * block))
    scale = lax.rsqrt(mean + EPSILON)
    r_o[...] = scale
    for o in range(ring_size):
        n_o[o] = (h_o[o] * scale * gains[o, 1:2, :]).astype(BF16)


def norm(x, pair, other, gains):
    ring_size, half, block = pair.shape
    return pl.pallas_call(
        norm_kernel,
        in_specs=vmem(4),
        out_shape=(shaped(pair.shape, F32), shaped(pair.shape, BF16), shaped((half, 1), F32)),
        compiler_params=params(),
        cost_estimate=cost(8 * pair.size, 12 * pair.size),
        name="norm",
    )(x, pair, other, gains)


def norm_back_kernel(pair, other, h1, r2, gains, g, dh_o, dhr_o, grad_o):
    ring_size, half, block = h1.shape
    dots = jnp.zeros((half, block), F32)
    scale = r2[...]
    for o in range(ring_size):
        grad = pair[o].astype(F32) + other[o].astype(F32)
        h = h1[o]
        product = grad * h
        dots = dots + product * gains[o, 1:2, :]
        grad_o[o] = jnp.sum(product * scale, 0, keepdims=True)
    mean = jnp.sum(dots, 1, keepdims=True) * (1.0 / (ring_size * block))
    bend = scale * scale * scale * mean
    for o in range(ring_size):
        grad = pair[o].astype(F32) + other[o].astype(F32)
        dh = g[o, 0:half, :].astype(F32) + scale * (grad * gains[o, 1:2, :]) - h1[o] * bend
        dh_o[o] = dh
        dhr_o[o] = dh.astype(BF16)


def norm_back(pair, other, h1, r2, gains, g):
    ring_size, half, block = pair.shape
    return pl.pallas_call(
        norm_back_kernel,
        in_specs=vmem(6),
        out_shape=(shaped(pair.shape, F32), shaped(pair.shape, BF16), shaped((ring_size, 1, block), F32)),
        compiler_params=params(),
        cost_estimate=cost(12 * pair.size, 16 * pair.size),
        name="norm_back",
    )(pair, other, h1, r2, gains, g)


def input_back_kernel(slots, pair, other, x, r1, gains, dh1, out_o, grad_o):
    ring_size, half, block = dh1.shape
    dots = jnp.zeros((half, block), F32)
    scale = r1[0:half, :]
    for o in range(ring_size):
        product = (pair[o].astype(F32) + other[o].astype(F32)) * x[o, 0:half, :].astype(F32)
        dots = dots + product * gains[o, 0:1, :]
        grad_o[o] = jnp.sum(product * scale, 0, keepdims=True)
    mean = jnp.sum(dots, 1, keepdims=True) * (1.0 / (ring_size * block))
    bend = scale * scale * scale * mean
    for k in range(ring_size):
        o = slots[k]
        grad = pair[o].astype(F32) + other[o].astype(F32)
        out_o[:, k * block : (k + 1) * block] = (
            dh1[o] + scale * (grad * gains[o, 0:1, :]) - x[o, 0:half, :].astype(F32) * bend
        )


def input_back(slots, pair, other, x, r1, gains, dh1):
    ring_size, half, block = pair.shape
    return pl.pallas_call(
        input_back_kernel,
        in_specs=[smem(), *vmem(6)],
        out_shape=(shaped((half, ring_size * block), F32), shaped((ring_size, 1, block), F32)),
        compiler_params=params(),
        cost_estimate=cost(12 * pair.size, 16 * pair.size),
        name="input_back",
    )(slots, pair, other, x, r1, gains, dh1)


def finish_kernel(slots, h1, pair, other, out_o):
    ring_size, half, block = h1.shape
    for k in range(ring_size):
        columns = slice(k * block, (k + 1) * block)
        out_o[:, columns] = h1[slots[k]] + (pair[:, columns].astype(F32) + other[:, columns].astype(F32))


def finish(slots, h1, pair, other):
    return pl.pallas_call(
        finish_kernel,
        in_specs=[smem(), *vmem(3)],
        out_shape=shaped(pair.shape, F32),
        compiler_params=params(),
        cost_estimate=cost(2 * pair.size, 12 * pair.size),
        name="finish",
    )(slots, h1, pair, other)


def unit_kernel(owners, n2, gate, up, dq, q_o, dga_o, dup_o):
    ring_size, total, block = n2.shape
    ga = upward = None
    for o in range(ring_size):
        at = pl.ds(pl.multiple_of(owners[o] * block, block), block)
        left = n2[o]
        term_g = jnp.dot(left, gate[at, :], preferred_element_type=F32)
        term_u = jnp.dot(left, up[at, :], preferred_element_type=F32)
        ga = term_g if ga is None else ga + term_g
        upward = term_u if upward is None else upward + term_u
    value, slope = gelu_both(ga)
    grad = dq[...]
    q_o[...] = (value * upward).astype(BF16)
    dga_o[...] = (grad * upward * slope).astype(BF16)
    dup_o[...] = (grad * value).astype(BF16)


def unit_pass(owners, n2, gate, up, dq):
    ring_size, total, block = n2.shape
    model, units = gate.shape
    tile = 256
    wide = pl.BlockSpec((total, tile), lambda i: (0, i))
    tall = pl.BlockSpec((model, tile), lambda i: (0, i))
    out = shaped((total, units), BF16)
    return pl.pallas_call(
        unit_kernel,
        grid=(units // tile,),
        in_specs=[smem(), pl.BlockSpec(n2.shape, lambda i: (0, 0, 0)), tall, tall, wide],
        out_specs=[wide, wide, wide],
        out_shape=(out, out, out),
        compiler_params=params(),
        cost_estimate=cost(4 * total * model * units, 4 * model * units + 10 * total * units, total * units),
        name="unit_pass",
    )(owners, n2, gate, up, dq)


def unit_back_kernel(owners, dga, dup, gate, up, own_o, other_o):
    half = other_o.shape[1]
    part = lax.dot_general(dga[...], gate[...], NT, preferred_element_type=F32)
    part = part + lax.dot_general(dup[...], up[...], NT, preferred_element_type=F32)
    own_o[0] = part[:half]
    other_o[0] = part[half:].astype(BF16)


def unit_back(owners, dga, dup, gate, up):
    ring_size = owners.shape[0]
    total, units = dga.shape
    half = total // 2
    block = gate.shape[0] // ring_size
    left = pl.BlockSpec((total, units), lambda o, owners: (0, 0))
    weight = pl.BlockSpec((block, units), lambda o, owners: (owners[o], 0))
    out = pl.BlockSpec((1, half, block), lambda o, owners: (o, 0, 0))
    return pl.pallas_call(
        unit_back_kernel,
        grid_spec=pltpu.PrefetchScalarGridSpec(
            num_scalar_prefetch=1,
            grid=(ring_size,),
            in_specs=[left, left, weight, weight],
            out_specs=[out, out],
        ),
        out_shape=(shaped((ring_size, half, block), F32), shaped((ring_size, half, block), BF16)),
        compiler_params=params(),
        cost_estimate=cost(4 * total * units * gate.shape[0], 4 * units * gate.shape[0] + 6 * total * gate.shape[0]),
        name="unit_back",
    )(owners, dga, dup, gate, up)


def local(
    tokens,
    cotangent,
    row_length,
    first_gain,
    value_weight,
    gelu_weight,
    conv_weight,
    conv_bias,
    input_gate,
    input_bias,
    recur_gate,
    recur_bias,
    decay_param,
    output_weight,
    second_gain,
    mlp_gate,
    mlp_up,
    mlp_down,
):
    ring_size = lax.axis_size("dp")
    middle = ring_size // 2
    ring = [2 * i if i < middle else 2 * (ring_size - 1 - i) + 1 for i in range(ring_size)]
    onward = [(ring[i], ring[(i + 1) % ring_size]) for i in range(ring_size)]
    backward = [(b, a) for a, b in onward]
    me = lax.axis_index("dp")
    core = lax.axis_index("mp") % 2
    core_pair = [(i, i ^ 1) for i in range(4)]
    chip_pair = [(i, i ^ 2) for i in range(4)]
    count = jnp.arange(ring_size, dtype=jnp.int32)

    def spot_of(index):
        return jnp.where(index % 2 == 0, index // 2, ring_size - 1 - index // 2)

    spots = (spot_of(me) + count) % ring_size
    owners = jnp.where(spots < middle, 2 * spots, 2 * (ring_size - 1 - spots) + 1).astype(jnp.int32)
    slots = ((spot_of(count) - spot_of(me) + ring_size) % ring_size).astype(jnp.int32)

    def hops(long_way_on):
        return (middle, ring_size - 1 - middle) if long_way_on else (ring_size - 1 - middle, middle)

    def ring_gather(shard, long_way_on):
        on, back = hops(long_way_on)
        got = [shard] + [None] * (ring_size - 1)
        moving = shard
        for s in range(1, on + 1):
            moving = lax.ppermute(moving, "dp", onward)
            got[ring_size - s] = moving
        moving = shard
        for s in range(1, back + 1):
            moving = lax.ppermute(moving, "dp", backward)
            got[s] = moving
        return got

    def ring_scatter(term, long_way_on, sent=BF16):
        on, back = hops(long_way_on)
        arrived = []
        for far, sign, way in ((on, 1, onward), (back, -1, backward)):
            moving = None
            for j in range(far, 0, -1):
                part = term(j if sign > 0 else ring_size - j)
                if moving is not None:
                    part = part + moving.astype(F32)
                moving = lax.ppermute(part.astype(sent), "dp", way)
            if moving is not None:
                arrived.append(moving)
        out = term(0)
        for item in arrived:
            out = out + item.astype(F32)
        return out

    def outer(left, right):
        return jnp.einsum("tb,tf->bf", left, right, preferred_element_type=F32)

    subs, row_count, length, model = tokens.shape
    half = row_count * length
    total = subs * half
    seqs = subs * row_count
    width, head = input_gate.shape
    block = model // ring_size
    lanes = (width + 128) // 128 * 128
    spare = lanes - width

    def mp_sum(own, other):
        got = lax.ppermute(other, "mp", core_pair)
        pair = (own + got.astype(F32)).astype(BF16)
        return pair, lax.ppermute(pair, "mp", chip_pair)

    def both_halves(own):
        return jnp.concatenate([own, lax.ppermute(own, "mp", core_pair)], 1)

    def in_order(own):
        got = lax.ppermute(own, "mp", core_pair)
        lower = jnp.where(core == 0, own, got)
        upper = jnp.where(core == 0, got, own)
        return jnp.stack([lower, upper]).reshape(subs, row_count, length, model)

    gain_lines = jnp.concatenate([first_gain.reshape(-1, spare), second_gain.reshape(-1, spare)])
    gain_lines = jnp.pad(gain_lines, ((0, block - gain_lines.shape[0]), (0, 0)))
    value_all = ring_gather(jnp.concatenate([value_weight, gain_lines], 1), True)
    gelu_all = ring_gather(gelu_weight, False)
    output_all = ring_gather(output_weight.T, True)

    scalars = jnp.concatenate([core[None], row_length.reshape(-1)]).astype(jnp.int32)
    x, g, g_flat, r1 = prepare(
        scalars, slots, tokens.reshape(subs, half, model), cotangent.reshape(subs, half, model), ring_size
    )
    dq = jnp.einsum("td,fd->tf", g_flat, mlp_down, preferred_element_type=F32)

    heads = width // head
    row_head = lax.broadcasted_iota(jnp.int32, (width, width), 0) // head
    column_head = lax.broadcasted_iota(jnp.int32, (width, width), 1) // head

    def block_matrix(gate):
        return jnp.where(row_head == column_head, jnp.tile(gate, (1, heads)), 0).astype(BF16)

    blocks_i, blocks_r = block_matrix(input_gate), block_matrix(recur_gate)
    decay_wide = decay_param.astype(F32)
    soft = jax.nn.softplus(-decay_wide)[None]
    gate_soft = jax.nn.sigmoid(-decay_wide)[None]
    taps = conv_weight.astype(F32)
    tap_bias = conv_bias.astype(F32)[None]
    bias_i, bias_r = input_bias.astype(F32)[None], recur_bias.astype(F32)[None]

    near = [o for o in range(ring_size) if min(o, ring_size - o) <= ring_size // 4]
    far = [o for o in range(ring_size) if o not in near]
    bx, by, n1_near, gains_near = project(
        near, x, r1, [value_all[o] for o in near], [gelu_all[o] for o in near], None, width
    )
    bx, by, n1_far, gains_far = project(
        far, x, r1, [value_all[o] for o in far], [gelu_all[o] for o in far], (bx, by), width
    )
    n1 = {o: n1_near[i] for i, o in enumerate(near)} | {o: n1_far[i] for i, o in enumerate(far)}
    gains = {o: gains_near[i] for i, o in enumerate(near)} | {o: gains_far[i] for i, o in enumerate(far)}
    gains = jnp.stack([gains[o] for o in range(ring_size)])

    p, cx, lx, lr, h = mixer_forward(
        seqs, bx, by, taps, tap_bias, blocks_i, blocks_r, bias_i, bias_r, soft
    )
    h1, n2_own, r2 = norm(x, *mp_sum(*emit([p], [output_all], "mixer_out")), gains)
    n2 = both_halves(n2_own)
    q, dga, dup = unit_pass(owners, n2, mlp_gate, mlp_up, dq)

    gate_grad = ring_scatter(lambda o: outer(n2[o], dga), True)
    up_grad = ring_scatter(lambda o: outer(n2[o], dup), False)
    down_grad = ring_scatter(lambda o: outer(g[o], q), True).T

    dh1, dhr_own, second_grad = norm_back(
        *mp_sum(*unit_back(owners, dga, dup, mlp_gate, mlp_up)), h1, r2, gains, g
    )
    dhr = both_halves(dhr_own)
    dbx, dby, gate_i, gate_r = mixer_backward(
        seqs, dhr, output_all, bx, by, cx, lx, lr, h, taps, blocks_i, blocks_r, soft, gate_soft, head
    )
    output_grad = ring_scatter(lambda o: outer(dhr[o], p), True).T
    value_grad = ring_scatter(lambda o: outer(n1[o], dbx), False)
    gelu_grad = ring_scatter(lambda o: outer(n1[o], dby), True)
    gate_i, gate_r = lax.psum((gate_i, gate_r), "dp")
    sums = jnp.concatenate(
        [gate_i[width + i * SUMS : width + (i + 1) * SUMS] for i in range(heads)], 1
    )

    input_own, first_grad = input_back(
        slots, *mp_sum(*emit([dbx, dby], [value_all, gelu_all], "input_out")), x, r1, gains, dh1
    )
    input_grad = in_order(input_own)
    gain_grads = jnp.concatenate([first_grad, second_grad], 1)
    gain_grads = gain_grads + lax.ppermute(gain_grads, "mp", core_pair)
    gain_grads = ring_scatter(lambda o: gain_grads[o], True, F32)

    out_own = jnp.dot(q[:half], mlp_down, preferred_element_type=F32)
    out_other = jnp.dot(q[half:], mlp_down, preferred_element_type=F32).astype(BF16)
    layer_out = in_order(finish(slots, h1, *mp_sum(out_own, out_other)))

    count = conv_weight.shape[0]
    return (
        layer_out,
        input_grad,
        gain_grads[0],
        value_grad,
        gelu_grad,
        sums[:count],
        sums[count],
        gate_i[:width],
        sums[count + 1],
        gate_r,
        sums[count + 2],
        sums[count + 3],
        output_grad,
        gain_grads[1],
        gate_grad,
        up_grad,
        down_grad,
    )


def solution(mesh):
    placed = (
        P(None, "dp", None, None),
        P(None, "dp", None, None),
        P(None, "dp"),
        P("dp"),
        P("dp", "mp"),
        P("dp", "mp"),
        P(None, "mp"),
        P("mp"),
        P("mp", None),
        P("mp"),
        P("mp", None),
        P("mp"),
        P("mp"),
        P("mp", "dp"),
        P("dp"),
        P(None, "mp"),
        P(None, "mp"),
        P("mp", None),
    )
    return jax.shard_map(
        local,
        mesh=mesh,
        in_specs=placed,
        out_specs=(
            P(None, "dp", None, None),
            P(None, "dp", None, None),
            P("dp"),
            P("dp", "mp"),
            P("dp", "mp"),
            P(None, "mp"),
            P("mp"),
            P("mp", None),
            P("mp"),
            P("mp", None),
            P("mp"),
            P("mp"),
            P("mp", "dp"),
            P("dp"),
            P("dp", "mp"),
            P("dp", "mp"),
            P("mp", "dp"),
        ),
        check_vma=False,
    )
```

```python
import jax
import jax.numpy as jnp
from jax import lax
from jax.experimental import pallas as pl
from jax.experimental.pallas import tpu as pltpu
from jax.sharding import PartitionSpec as P

EPSILON = 1e-06
DECAY_SCALE = 8.0
GELU_A = 0.7978845608028654
GELU_B = 0.044715
BF16 = jnp.bfloat16
F32 = jnp.float32
STEP = 16
HALF = 8
SUMS = 8
TN = (((0,), (0,)), ((), ()))
NT = (((1,), (1,)), ((), ()))


def gelu(v):
    return 0.5 * v * (1.0 + jnp.tanh(GELU_A * (v + GELU_B * v * v * v)))


def gelu_both(v):
    squared = v * v
    bent = jnp.tanh(GELU_A * v * (1.0 + GELU_B * squared))
    value = 0.5 * v * (1.0 + bent)
    slope = 0.5 * (1.0 + bent) + 0.5 * v * (1.0 - bent * bent) * GELU_A * (
        1.0 + 3.0 * GELU_B * squared
    )
    return value, slope


def negative_expm1(z, exp_z):
    series = 1.0 + z * (1.0 / 7.0)
    for k in (6.0, 5.0, 4.0, 3.0, 2.0):
        series = 1.0 + z * (1.0 / k) * series
    return jnp.where(z > -0.25, -z * series, 1.0 - exp_z)


def rows_of(shape):
    return lax.broadcasted_iota(jnp.int32, shape, 0)


def earlier(now, before, k, rows):
    return jnp.where(rows < k, pltpu.roll(before, k, 0), pltpu.roll(now, k, 0))


def later(now, after, k, rows):
    size = now.shape[0]
    return jnp.where(
        rows >= size - k, pltpu.roll(after, size - k, 0), pltpu.roll(now, size - k, 0)
    )


def shaped(shape, dtype):
    return jax.ShapeDtypeStruct(shape, dtype)


def launch(
    kernel, inputs, out_shape, name, scalars=0, after=(), mib=20, scratch=(), aliases=None, grid=None, flops=1
):
    count, extra = len(inputs), len(after)
    waits = [pl.BlockSpec(memory_space=pl.ANY)] * extra
    in_specs = [pl.BlockSpec(memory_space=pltpu.SMEM)] * scalars
    more = {}
    if grid is None:
        in_specs += [pl.BlockSpec(memory_space=pltpu.VMEM)] * (count - scalars)
    else:
        in_specs += grid[1]
        more = {"grid": grid[0], "out_specs": grid[2]}
    return pl.pallas_call(
        lambda *refs: kernel(*refs[:count], *refs[count + extra :]),
        in_specs=in_specs + waits,
        out_shape=out_shape,
        scratch_shapes=list(scratch),
        input_output_aliases=aliases or {},
        compiler_params=pltpu.CompilerParams(vmem_limit_bytes=mib << 20),
        cost_estimate=pl.CostEstimate(flops=flops, bytes_accessed=1, transcendentals=0),
        name=name,
        **more,
    )(*inputs, *after)


def in_hbm(array):
    return pltpu.with_memory_space_constraint(array, pltpu.HBM)


def mixer_forward_kernel(
    seqs, count, bx, by, lines, blocks_i, blocks_r, p_o, cx_o, lx_o, lr_o, h_o
):
    total, width = bx.shape
    length = total // seqs
    steps = length // STEP
    rows16 = rows_of((STEP, width))
    w = [jnp.broadcast_to(lines[k : k + 1, :], (STEP, width)) for k in range(count)]
    shift = jnp.broadcast_to(lines[count : count + 1, :], (STEP, width))
    bias_i, bias_r = lines[count + 1 : count + 2, :], lines[count + 2 : count + 3, :]
    soft = lines[count + 3 : count + 4, :]
    for seq in range(seqs):

        def conv(i, before):
            at = pl.ds(pl.multiple_of(seq * length + i * STEP, STEP), STEP)
            now = bx[at, :]
            mixed = shift + w[0] * now
            for k in range(1, count):
                mixed = mixed + w[k] * earlier(now, before, k, rows16)
            cx_o[at, :] = mixed.astype(BF16)
            return now

        lax.fori_loop(0, steps, conv, jnp.zeros((STEP, width), F32))
    lx_o[...] = lax.dot_general(cx_o[...], blocks_i[...], NT, preferred_element_type=F32) + bias_i
    lr_o[...] = lax.dot_general(cx_o[...], blocks_r[...], NT, preferred_element_type=F32) + bias_r
    rows8 = rows_of((HALF, width))
    soft8 = jnp.broadcast_to(-DECAY_SCALE * soft, (HALF, width))

    def scan(i, carries):
        out = []
        for seq in range(seqs):
            carry = carries[seq]
            base = seq * length + i * STEP
            at = pl.ds(pl.multiple_of(base, STEP), STEP)
            cx16 = cx_o[at, :].astype(F32)
            products = []
            for part in range(STEP // HALF):
                here = pl.ds(pl.multiple_of(base + part * HALF, HALF), HALF)
                cx = cx16[part * HALF : (part + 1) * HALF, :]
                ix = jax.nn.sigmoid(lx_o[here, :])
                la = soft8 * jax.nn.sigmoid(lr_o[here, :])
                a = jnp.exp(la)
                rest = negative_expm1(2.0 * la, a * a)
                m = jnp.where(rest > 0.0, rest * lax.rsqrt(rest), 0.0)
                u = m * ix * cx
                for s in (1, 2, 4):
                    keep = rows8 >= s
                    u = u + jnp.where(keep, a * pltpu.roll(u, s, 0), 0.0)
                    a = jnp.where(keep, a * pltpu.roll(a, s, 0), a)
                h = u + a * carry
                carry = jnp.broadcast_to(h[HALF - 1 : HALF, :], (HALF, width))
                h_o[here, :] = h
                products.append(h * gelu(by[here, :]))
            p_o[at, :] = jnp.concatenate(products, 0).astype(BF16)
            out.append(carry)
        return tuple(out)

    lax.fori_loop(0, steps, scan, tuple(jnp.zeros((HALF, width), F32) for _ in range(seqs)))


def mixer_forward(seqs, count, bx, by, lines, blocks_i, blocks_r):
    low, full = shaped(bx.shape, BF16), shaped(bx.shape, F32)
    return launch(
        lambda *refs: mixer_forward_kernel(seqs, count, *refs),
        (bx, by, lines, blocks_i, blocks_r),
        (low, low, full, full, full),
        "mixer_forward",
    )


def mixer_backward_kernel(seqs, head, count, split, dhr, *refs):
    ring_size = dhr.shape[0]
    second = refs[:ring_size]
    bx, by, cx_i, lx_i, lr_i, h_i, lines, blocks_i, blocks_r = refs[ring_size : ring_size + 9]
    dbx_o, dby_o, small_o, dlx_o, dlr_o, dcx_s, dp = refs[ring_size + 9 :]
    skip = bx.shape[1] - split
    soft, gate_soft = lines[count + 3 : count + 4, :], lines[count + 4 : count + 5, :]
    for o in range(ring_size):
        part = lax.dot_general(dhr[o], second[o][skip:, :], NT, preferred_element_type=F32)
        dp[...] = part if o == 0 else dp[...] + part
    total, width = bx.shape
    length = total // seqs
    steps = length // STEP
    rows8 = rows_of((HALF, width))
    soft8 = jnp.broadcast_to(-DECAY_SCALE * soft, (HALF, width))
    zero = jnp.zeros((HALF, width), F32)

    def scan(j, state):
        i = steps - 1 - j
        sums_i, sums_r, sums_d = state[0]
        out = []
        for seq in range(seqs):
            a_after, e_after = state[1][seq]
            base = seq * length + i * STEP
            at = pl.ds(pl.multiple_of(base, STEP), STEP)
            cx16 = cx_i[at, :].astype(F32)
            dby_parts, dlx_parts, dlr_parts = [None, None], [None, None], [None, None]
            for part in (1, 0):
                start = base + part * HALF
                here = pl.ds(pl.multiple_of(start, HALF), HALF)
                cx = cx16[part * HALF : (part + 1) * HALF, :]
                ix = jax.nn.sigmoid(lx_i[here, :])
                ra = jax.nn.sigmoid(lr_i[here, :])
                la = soft8 * ra
                a = jnp.exp(la)
                rest = negative_expm1(2.0 * la, a * a)
                inverse = lax.rsqrt(rest)
                m = rest * inverse
                h = h_i[here, :]
                first = (i == 0) if part == 0 else False
                back = jnp.maximum(start - HALF, 0)
                before = h_i[pl.ds(pl.multiple_of(back, HALF), HALF), :]
                if part == 0:
                    before = jnp.where(i == 0, 0.0, before)
                h_prev = earlier(h, before, 1, rows8)
                gy, slope = gelu_both(by[here, :])
                grad = dp[here, :]
                dby_parts[part] = grad * h * slope
                e = grad * gy
                f = later(a, a_after, 1, rows8)
                for s in (1, 2, 4):
                    keep = rows8 < HALF - s
                    e = e + jnp.where(keep, f * pltpu.roll(e, HALF - s, 0), 0.0)
                    f = jnp.where(keep, f * pltpu.roll(f, HALF - s, 0), f)
                e = e + f * e_after
                e_after = jnp.broadcast_to(e[0:1, :], (HALF, width))
                a_after = a
                eix = e * ix
                dla = (e * h_prev - eix * cx * a * inverse) * a
                dlx = eix * m * cx * (1.0 - ix)
                dlr = dla * la * (1.0 - ra)
                sums_i = sums_i + dlx
                sums_r = sums_r + dlr
                sums_d = sums_d + dla * ra
                dlx_parts[part], dlr_parts[part] = dlx, dlr
                dcx_s[here, :] = eix * m
            dby_o[at, :] = jnp.concatenate(dby_parts, 0).astype(BF16)
            dlx_o[at, :] = jnp.concatenate(dlx_parts, 0).astype(BF16)
            dlr_o[at, :] = jnp.concatenate(dlr_parts, 0).astype(BF16)
            out.append((a_after, e_after))
        return (sums_i, sums_r, sums_d), tuple(out)

    (sums_i, sums_r, sums_d), _ = lax.fori_loop(
        0, steps, scan, ((zero, zero, zero), tuple((zero, zero) for _ in range(seqs)))
    )
    dcx_s[...] += jnp.dot(dlx_o[...], blocks_i[...], preferred_element_type=F32) + jnp.dot(
        dlr_o[...], blocks_r[...], preferred_element_type=F32
    )
    rows16 = rows_of((STEP, width))
    w = [jnp.broadcast_to(lines[k : k + 1, :], (STEP, width)) for k in range(count)]
    zero16 = jnp.zeros((STEP, width), F32)
    sums_t = tuple(zero16 for _ in range(count))
    sums_b = zero16
    for seq in range(seqs):

        def conv(j, state):
            after, tap_sums, shift_sum = state
            at = pl.ds(pl.multiple_of(seq * length + (steps - 1 - j) * STEP, STEP), STEP)
            now = dcx_s[at, :]
            source = bx[at, :]
            grad = w[0] * now
            new_sums = [tap_sums[0] + now * source]
            for k in range(1, count):
                moved = later(now, after, k, rows16)
                grad = grad + w[k] * moved
                new_sums.append(tap_sums[k] + moved * source)
            dbx_o[at, :] = grad.astype(BF16)
            return now, tuple(new_sums), shift_sum + now

        _, sums_t, sums_b = lax.fori_loop(0, steps, conv, (zero16, sums_t, sums_b))
    rows = [jnp.sum(item, 0, keepdims=True) for item in (*sums_t, sums_b, sums_i, sums_r)]
    rows.append(DECAY_SCALE * gate_soft * jnp.sum(sums_d, 0, keepdims=True))
    spare = small_o.shape[0] - 2 * head - SUMS
    if spare:
        rows.append(jnp.zeros((spare, width), F32))
    small_o[2 * head :, :] = jnp.concatenate(rows, 0).astype(BF16)
    lanes = lax.broadcasted_iota(jnp.int32, (head, width), 1)
    for gate, grads in enumerate((dlx_o, dlr_o)):
        whole = lax.dot_general(grads[...], cx_i[...], TN, preferred_element_type=F32)
        picked = whole[:head]
        for i in range(1, width // head):
            picked = jnp.where(lanes < i * head, picked, whole[i * head : (i + 1) * head])
        small_o[gate * head : (gate + 1) * head, :] = picked.astype(BF16)


def mixer_backward(seqs, head, count, split, small_rows, dhr, second, saved, after):
    total, width = saved[0].shape
    low = shaped((total, width), BF16)
    return launch(
        lambda *refs: mixer_backward_kernel(seqs, head, count, split, *refs),
        (dhr, *second, *saved),
        (low, low, shaped((small_rows, width), BF16)),
        "mixer_backward",
        after=after,
        mib=32,
        scratch=[
            pltpu.VMEM((total, width), BF16),
            pltpu.VMEM((total, width), BF16),
            pltpu.VMEM((total, width), F32),
            pltpu.VMEM((total, width), F32),
        ],
    )


def prepare_kernel(scalars, slots, tokens, cotangent, gate_i, gate_r, x_o, g_o, flat_o, r_o, blocks_i, blocks_r):
    ring_size, total, block = x_o.shape
    half = total // 2
    row_count = (scalars.shape[0] - 1) // 2
    length = half // row_count
    rows = lax.broadcasted_iota(jnp.int32, (length, block), 0)
    for place in range(2):
        sub = scalars[0] if place == 0 else 1 - scalars[0]
        for row in range(row_count):
            at = slice(place * half + row * length, place * half + (row + 1) * length)
            source = pl.ds(row * length, length)
            valid = jnp.where(rows < scalars[1 + sub * row_count + row], 1.0, 0.0)
            squares = jnp.zeros((length, block), F32)
            for k in range(ring_size):
                columns = slice(k * block, (k + 1) * block)
                piece = tokens[sub, source, columns]
                wide = piece.astype(F32)
                squares = squares + wide * wide
                x_o[slots[k], at, :] = piece
                masked = (cotangent[sub, source, columns].astype(F32) * valid).astype(BF16)
                g_o[slots[k], at, :] = masked
                flat_o[at, columns] = masked
            mean = jnp.sum(squares, 1, keepdims=True) * (1.0 / (ring_size * block))
            r_o[at, :] = lax.rsqrt(mean + EPSILON)
    head, width = gate_i.shape
    lanes = lax.broadcasted_iota(jnp.int32, (head, width), 1)
    for source, out in ((gate_i, blocks_i), (gate_r, blocks_r)):
        wide = source[...].astype(F32)
        for i in range(width // head):
            inside = (lanes >= i * head) & (lanes < (i + 1) * head)
            out[i * head : (i + 1) * head, :] = jnp.where(inside, wide, 0.0).astype(BF16)


def prepare(scalars, slots, tokens, cotangent, gate_i, gate_r, after):
    subs, half, model = tokens.shape
    total, ring_size, width = subs * half, slots.shape[0], gate_i.shape[1]
    rel = shaped((ring_size, total, model // ring_size), BF16)
    blocks = shaped((width, width), BF16)
    return launch(
        prepare_kernel,
        (scalars, slots, tokens, cotangent, gate_i, gate_r),
        (rel, rel, shaped((total, model), BF16), shaped((total, 1), F32), blocks, blocks),
        "prepare",
        scalars=2,
        after=after,
    )


def project_kernel(offsets, first, width, split, x, r1, *refs):
    count = len(offsets)
    one, two = refs[:count], refs[count : 2 * count]
    rest = refs[2 * count :]
    if not first:
        before = rest[:2]
        rest = rest[2:]
    bx, by, n1_o = rest
    scale = r1[...]
    for i, o in enumerate(offsets):
        gain = one[i][width : width + 16, :].astype(F32)[0:1, :]
        n1 = (x[o].astype(F32) * scale * gain).astype(BF16)
        n1_o[i] = n1
        for out, place, columns, weight in (
            (bx, 0, slice(0, width), one[i][:width, :]),
            (by, 1, slice(0, split), one[i][width + 16 :, :]),
            (by, 1, slice(split, width), two[i][: width - split, :]),
        ):
            part = lax.dot_general(n1, weight, NT, preferred_element_type=F32)
            if i > 0:
                out[:, columns] += part
            elif first:
                out[:, columns] = part
            else:
                out[:, columns] = before[place][:, columns] + part


def project(offsets, x, r1, one, two, before, width, split):
    total, block = x.shape[1:]
    count = len(offsets)
    full = shaped((total, width), F32)
    at = 2 + 2 * count
    return launch(
        lambda *refs: project_kernel(offsets, before is None, width, split, *refs),
        (x, r1, *one, *two, *(before or ())),
        (full, full, shaped((count, total, block), BF16)),
        "project",
        aliases={} if before is None else {at: 0, at + 1: 1},
    )


def mixer_out_kernel(skip, p, *refs):
    own_o, other_o, gains_o = refs[-3:]
    count, half = own_o.shape[:2]
    width = p.shape[1]
    for o in range(count):
        part = jnp.dot(p[...], refs[count + o][skip:, :], preferred_element_type=F32)
        own_o[o] = part[:half]
        other_o[o] = part[half:].astype(BF16)
        gains_o[o] = refs[o][width : width + 16, :].astype(F32)[0:2, :]


def mixer_out(p, one, two, split):
    total, width = p.shape
    count, block = len(one), one[0].shape[1]
    shape = (count, total // 2, block)
    return launch(
        lambda *refs: mixer_out_kernel(width - split, *refs),
        (p, *one, *two),
        (shaped(shape, F32), shaped(shape, BF16), shaped((count, 2, block), F32)),
        "mixer_out",
        mib=24,
    )


def input_out_kernel(split, dbx, dby, *refs):
    own_o, other_o = refs[-2:]
    count, half = own_o.shape[:2]
    width = dbx.shape[1]
    for o in range(count):
        one, two = refs[o], refs[count + o]
        part = (
            jnp.dot(dbx[...], one[:width, :], preferred_element_type=F32)
            + jnp.dot(dby[:, :split], one[width + 16 :, :], preferred_element_type=F32)
            + jnp.dot(dby[:, split:], two[: width - split, :], preferred_element_type=F32)
        )
        own_o[o] = part[:half]
        other_o[o] = part[half:].astype(BF16)


def input_out(dbx, dby, one, two, split, after):
    shape = (len(one), dbx.shape[0] // 2, one[0].shape[1])
    return launch(
        lambda *refs: input_out_kernel(split, *refs),
        (dbx, dby, *one, *two),
        (shaped(shape, F32), shaped(shape, BF16)),
        "input_out",
        after=after,
        mib=24,
    )


def pair_kernel(own, got, out):
    out[...] = (own[...] + got[...].astype(F32)).astype(BF16)


def pair_sum(own, got, after):
    return launch(pair_kernel, (own, got), shaped(own.shape, BF16), "pair_sum", after=after)


def norm_kernel(slots, x, gains, pair, other, h_o, n_o, r_o):
    ring_size, half, block = h_o.shape
    squares = jnp.zeros((half, block), F32)
    for o in range(ring_size):
        h = x[o, 0:half, :].astype(F32) + (pair[o].astype(F32) + other[o].astype(F32))
        h_o[o] = h
        squares = squares + h * h
    mean = jnp.sum(squares, 1, keepdims=True) * (1.0 / (ring_size * block))
    scale = lax.rsqrt(mean + EPSILON)
    r_o[...] = scale
    for k in range(ring_size):
        o = slots[k]
        n_o[:, k * block : (k + 1) * block] = (h_o[o] * scale * gains[o, 1:2, :]).astype(BF16)


def norm(slots, x, gains, pair, other, after):
    ring_size, half, block = pair.shape
    return launch(
        norm_kernel,
        (slots, x, gains, pair, other),
        (shaped(pair.shape, F32), shaped((half, ring_size * block), BF16), shaped((half, 1), F32)),
        "norm",
        scalars=1,
        after=after,
    )


def norm_back_kernel(pair, other, h1, r2, gains, g, dh_o, dhr_o, grad_o):
    ring_size, half, block = h1.shape
    dots = jnp.zeros((half, block), F32)
    scale = r2[...]
    for o in range(ring_size):
        product = (pair[o].astype(F32) + other[o].astype(F32)) * h1[o]
        dots = dots + product * gains[o, 1:2, :]
        grad_o[o] = jnp.sum(product * scale, 0, keepdims=True)
    mean = jnp.sum(dots, 1, keepdims=True) * (1.0 / (ring_size * block))
    bend = scale * scale * scale * mean
    for o in range(ring_size):
        grad = pair[o].astype(F32) + other[o].astype(F32)
        dh = g[o, 0:half, :].astype(F32) + scale * (grad * gains[o, 1:2, :]) - h1[o] * bend
        dh_o[o] = dh
        dhr_o[o] = dh.astype(BF16)


def norm_back(pair, other, h1, r2, gains, g, after):
    ring_size, half, block = pair.shape
    return launch(
        norm_back_kernel,
        (pair, other, h1, r2, gains, g),
        (shaped(pair.shape, F32), shaped(pair.shape, BF16), shaped((ring_size, 1, block), F32)),
        "norm_back",
        after=after,
    )


def input_back_kernel(slots, pair, other, x, r1, gains, dh1, second, out_o, grad_o):
    ring_size, half, block = dh1.shape
    dots = jnp.zeros((half, block), F32)
    scale = r1[0:half, :]
    for o in range(ring_size):
        product = (pair[o].astype(F32) + other[o].astype(F32)) * x[o, 0:half, :].astype(F32)
        dots = dots + product * gains[o, 0:1, :]
        grad_o[o, 0:1, :] = jnp.sum(product * scale, 0, keepdims=True)
        grad_o[o, 1:2, :] = second[o]
    mean = jnp.sum(dots, 1, keepdims=True) * (1.0 / (ring_size * block))
    bend = scale * scale * scale * mean
    for k in range(ring_size):
        o = slots[k]
        grad = pair[o].astype(F32) + other[o].astype(F32)
        out_o[:, k * block : (k + 1) * block] = (
            dh1[o] + scale * (grad * gains[o, 0:1, :]) - x[o, 0:half, :].astype(F32) * bend
        )


def input_back(slots, pair, other, x, r1, gains, dh1, second, after):
    ring_size, half, block = pair.shape
    return launch(
        input_back_kernel,
        (slots, pair, other, x, r1, gains, dh1, second),
        (shaped((half, ring_size * block), F32), shaped((ring_size, 2, block), F32)),
        "input_back",
        scalars=1,
        after=after,
    )


def finish_kernel(slots, h1, pair, other, out_o):
    ring_size, half, block = h1.shape
    for k in range(ring_size):
        columns = slice(k * block, (k + 1) * block)
        out_o[:, columns] = h1[slots[k]] + (pair[:, columns].astype(F32) + other[:, columns].astype(F32))


def finish(slots, h1, pair, other, after):
    return launch(
        finish_kernel, (slots, h1, pair, other), shaped(pair.shape, F32), "finish", scalars=1, after=after
    )


def arrange_kernel(scalars, own, got, out):
    core = scalars[0]
    out[core] = own[...]
    out[1 - core] = got[...]


def arrange(scalars, own, got, after):
    return launch(
        arrange_kernel, (scalars, own, got), shaped((2, *own.shape), own.dtype), "arrange", scalars=1, after=after
    )


def unit_grad_kernel(g, down, dq_o):
    dq_o[...] = lax.dot_general(g[...], down[...], NT, preferred_element_type=F32)


def unit_grad(g, down, after):
    total, model = g.shape
    units = down.shape[0]
    tile = 256
    grid = (
        (units // tile,),
        [pl.BlockSpec((total, model), lambda i: (0, 0)), pl.BlockSpec((tile, model), lambda i: (i, 0))],
        pl.BlockSpec((total, tile), lambda i: (0, i)),
    )
    return launch(unit_grad_kernel, (g, in_hbm(down)), shaped((total, units), F32), "unit_grad", after=after, grid=grid)


def unit_kernel(slots, n2, gate, up, dq, q_o, dga_o, dup_o, rel_o):
    ring_size, total, block = rel_o.shape

    @pl.when(pl.program_id(0) == 0)
    def _():
        for k in range(ring_size):
            rel_o[slots[k]] = n2[:, k * block : (k + 1) * block]

    ga = jnp.dot(n2[...], gate[...], preferred_element_type=F32)
    upward = jnp.dot(n2[...], up[...], preferred_element_type=F32)
    value, slope = gelu_both(ga)
    grad = dq[...]
    q_o[...] = (value * upward).astype(BF16)
    dga_o[...] = (grad * upward * slope).astype(BF16)
    dup_o[...] = (grad * value).astype(BF16)


def unit_pass(slots, n2, gate, up, dq):
    total, model = n2.shape
    ring_size = slots.shape[0]
    units = gate.shape[1]
    tile = 256
    rel = (ring_size, total, model // ring_size)
    wide = pl.BlockSpec((total, tile), lambda i: (0, i))
    tall = pl.BlockSpec((model, tile), lambda i: (0, i))
    out = shaped((total, units), BF16)
    grid = (
        (units // tile,),
        [pl.BlockSpec((total, model), lambda i: (0, 0)), tall, tall, wide],
        [wide, wide, wide, pl.BlockSpec(rel, lambda i: (0, 0, 0))],
    )
    return launch(
        unit_kernel,
        (slots, n2, in_hbm(gate), in_hbm(up), dq),
        (out, out, out, shaped(rel, BF16)),
        "unit_pass",
        scalars=1,
        mib=28,
        grid=grid,
    )


def unit_out_kernel(q, down, own_o, other_o):
    half = own_o.shape[0]
    part = jnp.dot(q[...], down[...], preferred_element_type=F32)
    own_o[...] = part[:half]
    other_o[...] = part[half:].astype(BF16)


def unit_out(q, down, after):
    total, units = q.shape
    model = down.shape[1]
    half = total // 2
    tile = 256
    out = pl.BlockSpec((half, tile), lambda i: (0, i))
    grid = (
        (model // tile,),
        [pl.BlockSpec((total, units), lambda i: (0, 0)), pl.BlockSpec((units, tile), lambda i: (0, i))],
        [out, out],
    )
    return launch(
        unit_out_kernel,
        (q, in_hbm(down)),
        (shaped((half, model), F32), shaped((half, model), BF16)),
        "unit_out",
        after=after,
        grid=grid,
    )


def unit_back_kernel(owners, dga, dup, gate, up, *refs):
    own_o, other_o = refs[-2:]
    half = other_o.shape[1]
    part = lax.dot_general(dga[...], gate[...], NT, preferred_element_type=F32)
    part = part + lax.dot_general(dup[...], up[...], NT, preferred_element_type=F32)
    own_o[0] = part[:half]
    other_o[0] = part[half:].astype(BF16)


def unit_back(owners, dga, dup, gate, up, after):
    ring_size = owners.shape[0]
    total, units = dga.shape
    half = total // 2
    block = gate.shape[0] // ring_size
    left = pl.BlockSpec((total, units), lambda o, owners: (0, 0))
    weight = pl.BlockSpec((block, units), lambda o, owners: (owners[o], 0))
    out = pl.BlockSpec((1, half, block), lambda o, owners: (o, 0, 0))
    return pl.pallas_call(
        unit_back_kernel,
        grid_spec=pltpu.PrefetchScalarGridSpec(
            num_scalar_prefetch=1,
            grid=(ring_size,),
            in_specs=[left, left, weight, weight, *[pl.BlockSpec(memory_space=pl.ANY)] * len(after)],
            out_specs=[out, out],
        ),
        out_shape=(shaped((ring_size, half, block), F32), shaped((ring_size, half, block), BF16)),
        compiler_params=pltpu.CompilerParams(vmem_limit_bytes=24 << 20),
        cost_estimate=pl.CostEstimate(flops=1, bytes_accessed=1, transcendentals=0),
        name="unit_back",
    )(owners, dga, dup, in_hbm(gate), in_hbm(up), *after)


def unit_term_kernel(part, turns, fold, n2, g, right, q, *refs):
    units = right.shape[1]
    share = units // 2
    columns = slice(part * share, (part + 1) * share)
    rest = list(refs)
    outs = rest[len(rest) - len(turns) - (2 if fold else 0) :]
    for (o, has), out in zip(turns, outs):
        recv = rest.pop(0) if has else None
        grad = lax.dot_general(n2[o], right[...], TN, preferred_element_type=F32)
        down = lax.dot_general(g[o], q[:, columns], TN, preferred_element_type=F32)
        if recv is not None:
            grad = grad + recv[:, :units].astype(F32)
            down = down + recv[:, units:].astype(F32)
        out[:, :units] = grad.astype(BF16)
        out[:, units:] = down.astype(BF16)
    if fold:
        recv = rest.pop(0)
        grad_o, down_o = outs[len(turns) :]
        grad = lax.dot_general(n2[0], right[...], TN, preferred_element_type=F32)
        grad_o[...] = grad + recv[:, :units].astype(F32)
        down = lax.dot_general(q[:, columns], g[0], TN, preferred_element_type=F32)
        down_o[...] = down + recv[:, units:].astype(F32).T


def unit_term(part, n2, g, right, q, turns, fold, after):
    block, units = n2.shape[2], right.shape[1]
    arrived = [item for _, item in turns if item is not None] + ([] if fold is None else [fold])
    plan = [(o, item is not None) for o, item in turns]
    out = [shaped((block, units + units // 2), BF16) for _ in turns]
    if fold is not None:
        out += [shaped((block, units), F32), shaped((units // 2, block), F32)]
    return launch(
        lambda *refs: unit_term_kernel(part, plan, fold is not None, *refs),
        (n2, g, right, q, *arrived),
        tuple(out),
        "unit_term",
        after=after,
        mib=24,
        flops=10**9,
    )


def unit_end_kernel(grad, down, item, grad_o, down_o):
    units = grad.shape[1]
    grad_o[...] = grad[...] + item[:, :units].astype(F32)
    down_o[...] = down[...] + item[:, units:].astype(F32).T


def unit_end(own, item, after):
    grad, down = own
    return launch(
        unit_end_kernel,
        (grad, down, item),
        (shaped(grad.shape, F32), shaped(down.shape, F32)),
        "unit_end",
        after=after,
        flops=10**9,
    )


def small_pieces(width, block):
    return [slice(i, min(i + block, width)) for i in range(0, width, block)]


def mixer_term_kernel(part, places, groups, split, chunk, turns, fold, owners, *refs):
    n1_all = refs[:groups]
    dhr, grads, p = refs[groups : groups + 3]
    rest = list(refs[groups + 3 :])
    extra = rest.pop(0) if part == 0 else None
    outs = rest[len(rest) - len(turns) - (3 - part if fold else 0) :]
    width, block = grads.shape[1], dhr.shape[2]
    columns = slice(0, split) if part == 0 else slice(split, width)
    size = columns.stop - columns.start
    at = width + size
    pieces = small_pieces(width, block)

    def terms(o, recv):
        group, i = places[o]
        grad = lax.dot_general(grads[...], n1_all[group][i], TN, preferred_element_type=F32)
        out = lax.dot_general(p[:, columns], dhr[o], TN, preferred_element_type=F32)
        if recv is not None:
            grad = grad + recv[:width, :].astype(F32)
            out = out + recv[width:at, :].astype(F32)
        return grad, out

    def small(o, recv):
        own = extra[pl.ds(pl.multiple_of(owners[o] * chunk, 16), chunk), :].astype(F32)
        out = []
        for i, piece in enumerate(pieces):
            total = own[:, piece]
            if recv is not None:
                total = total + recv[at + i * chunk : at + (i + 1) * chunk, : piece.stop - piece.start].astype(F32)
            out.append(total)
        return out

    for (o, has), out_ref in zip(turns, outs):
        recv = rest.pop(0) if has else None
        grad, out = terms(o, recv)
        out_ref[:width, :] = grad.astype(BF16)
        out_ref[width:at, :] = out.astype(BF16)
        if part == 0:
            for i, total in enumerate(small(o, recv)):
                rows = slice(at + i * chunk, at + (i + 1) * chunk)
                wide = total.shape[1]
                out_ref[rows, :wide] = total.astype(BF16)
                if wide < block:
                    out_ref[rows, wide:] = jnp.zeros((chunk, block - wide), BF16)
    if fold:
        recv = rest.pop(0)
        outs[len(turns)][...], outs[len(turns) + 1][...] = terms(0, recv)
        if part == 0:
            for piece, total in zip(pieces, small(0, recv)):
                outs[len(turns) + 2][:, piece] = total


def mixer_term(part, places, split, chunk, owners, n1, dhr, grads, p, extra, turns, fold, after):
    block, width = dhr.shape[2], grads.shape[1]
    size = split if part == 0 else width - split
    arrived = [item for _, item in turns if item is not None] + ([] if fold is None else [fold])
    more = 0 if part == 1 else chunk * len(small_pieces(width, block))
    out = [shaped((width + size + more, block), BF16) for _ in turns]
    if fold is not None:
        out += [shaped((width, block), F32), shaped((size, block), F32)]
        out += [shaped((chunk, width), F32)] if part == 0 else []
    plan = [(o, item is not None) for o, item in turns]
    return launch(
        lambda *refs: mixer_term_kernel(part, places, len(n1), split, chunk, plan, fold is not None, *refs),
        (owners, *n1, dhr, grads, p, *([extra] if part == 0 else []), *arrived),
        tuple(out),
        "mixer_term",
        scalars=1,
        after=after,
        mib=24,
        flops=10**9,
    )


def mixer_end_kernel(part, *refs):
    own, item, outs = refs[: 3 - part], refs[3 - part], refs[4 - part :]
    width, block = own[0].shape
    at = width + own[1].shape[0]
    outs[0][...] = own[0][...] + item[:width, :].astype(F32)
    outs[1][...] = own[1][...] + item[width:at, :].astype(F32)
    if part == 0:
        chunk = own[2].shape[0]
        for i, piece in enumerate(small_pieces(width, block)):
            rows = slice(at + i * chunk, at + (i + 1) * chunk)
            total = own[2][:, piece] + item[rows, : piece.stop - piece.start].astype(F32)
            outs[2][:, piece] = total.astype(BF16)


def mixer_end(part, own, item, after):
    shapes = [shaped(own[0].shape, F32), shaped(own[1].shape, F32)]
    if part == 0:
        shapes.append(shaped(own[2].shape, BF16))
    return launch(
        lambda *refs: mixer_end_kernel(part, *refs), (*own, item), tuple(shapes), "mixer_end", after=after, flops=10**9
    )


def spread_kernel(head, owners, *refs):
    ring_size = owners.shape[0]
    gate_i, gate_r, sums, gain_o, whole = refs[ring_size:]
    block = gain_o.shape[1]
    chunk = refs[0].shape[0] - 2 * ring_size
    gain = jnp.zeros((2, block), F32)
    for o in range(ring_size):
        at = pl.ds(pl.multiple_of(owners[o] * chunk, 16), chunk)
        whole[at, :] = refs[o][:chunk, :].astype(F32)
        mine = 2 * ((ring_size - o) % ring_size)
        gain = gain + refs[o][chunk:, :block].astype(F32)[mine : mine + 2, :]
    gate_i[...] = whole[:head, :]
    gate_r[...] = whole[head : 2 * head, :]
    sums[...] = whole[2 * head : 2 * head + SUMS, :]
    gain_o[...] = gain


def spread(head, block, owners, chunks, after):
    ring_size = len(chunks)
    rows, width = chunks[0].shape
    gate = shaped((head, width), F32)
    return launch(
        lambda *refs: spread_kernel(head, *refs),
        (owners, *chunks),
        (gate, gate, shaped((SUMS, width), F32), shaped((2, block), F32)),
        "spread",
        scalars=1,
        after=after,
        scratch=[pltpu.VMEM(((rows - 2 * ring_size) * ring_size, width), F32)],
    )


def local(
    tokens,
    cotangent,
    row_length,
    first_gain,
    value_weight,
    gelu_weight,
    conv_weight,
    conv_bias,
    input_gate,
    input_bias,
    recur_gate,
    recur_bias,
    decay_param,
    output_weight,
    second_gain,
    mlp_gate,
    mlp_up,
    mlp_down,
):
    ring_size = lax.axis_size("dp")
    middle = ring_size // 2
    ring = [2 * i if i < middle else 2 * (ring_size - 1 - i) + 1 for i in range(ring_size)]
    onward = [(ring[i], ring[(i + 1) % ring_size]) for i in range(ring_size)]
    backward = [(b, a) for a, b in onward]
    me = lax.axis_index("dp")
    core = lax.axis_index("mp") % 2
    core_pair = [(i, i ^ 1) for i in range(4)]
    chip_pair = [(i, i ^ 2) for i in range(4)]
    index = jnp.arange(ring_size, dtype=jnp.int32)

    def spot_of(place):
        return jnp.where(place % 2 == 0, place // 2, ring_size - 1 - place // 2)

    spots = (spot_of(me) + index) % ring_size
    owners = jnp.where(spots < middle, 2 * spots, 2 * (ring_size - 1 - spots) + 1).astype(jnp.int32)
    slots = ((spot_of(index) - spot_of(me) + ring_size) % ring_size).astype(jnp.int32)

    subs, row_count, length, model = tokens.shape
    half = row_count * length
    seqs = subs * row_count
    block = model // ring_size
    width, head = input_gate.shape
    count = conv_weight.shape[0]
    split = (width // 2 + 127) // 128 * 128
    chunk = -(-(2 * head + SUMS) // (16 * ring_size)) * 16
    small_rows = chunk * ring_size

    def hops(long_way_on):
        return (middle, ring_size - 1 - middle) if long_way_on else (ring_size - 1 - middle, middle)

    token = []

    def mark(*values):
        token[:] = values

    class Gather:
        def __init__(self, shard, long_way_on):
            self.hops = hops(long_way_on)
            self.moving = [shard, shard]
            self.got = [shard] + [None] * (ring_size - 1)

        def step(self, s):
            for d, way in enumerate((onward, backward)):
                if s <= self.hops[d]:
                    self.moving[d] = lax.ppermute(self.moving[d], "dp", way)
                    self.got[ring_size - s if d == 0 else s] = self.moving[d]

    class Scatter:
        def __init__(self, term, end, long_way_on):
            self.term, self.ending = term, end
            self.hops = hops(long_way_on)
            self.moving = [None, None]
            self.own = None

        def step(self, s):
            turns, ways, fold = [], [], None
            for d in range(2):
                far = self.hops[d] - s
                if far > 0:
                    turns.append((far if d == 0 else ring_size - far, self.moving[d]))
                    ways.append(d)
                elif far == 0:
                    fold = self.moving[d]
            parts = self.term(turns, fold, tuple(token))
            if fold is not None:
                self.own = parts[len(turns) :]
            mark(parts[0])
            for d, part in zip(ways, parts):
                self.moving[d] = lax.ppermute(part, "dp", (onward, backward)[d])

        def end(self):
            last = 0 if self.hops[0] > self.hops[1] else 1
            out = self.ending(self.own, self.moving[last], tuple(token))
            mark(out[0])
            return out

    def core_swap(other):
        return lax.ppermute(other, "mp", core_pair)

    def chip_swap(own, got, after):
        pair = pair_sum(own, got, after)
        mark(pair)
        return pair, lax.ppermute(pair, "mp", chip_pair)

    def both_halves(own, dim):
        return jnp.concatenate([own, lax.ppermute(own, "mp", core_pair)], dim)

    scalars = jnp.concatenate([core[None], row_length.reshape(-1)]).astype(jnp.int32)
    gain_lines = jnp.pad(jnp.stack([first_gain, second_gain]), ((0, 14), (0, 0)))
    gelu_t = gelu_weight.T
    ring_one = Gather(jnp.concatenate([value_weight.T, gain_lines, gelu_t[:split]]), True)
    ring_two = Gather(jnp.concatenate([gelu_t[split:], output_weight]), False)
    ring_one.step(1)
    ring_two.step(1)

    decay_wide = decay_param.astype(F32)
    lines = jnp.concatenate(
        [
            conv_weight.astype(F32),
            jnp.stack(
                [
                    conv_bias.astype(F32),
                    input_bias.astype(F32),
                    recur_bias.astype(F32),
                    jax.nn.softplus(-decay_wide),
                    jax.nn.sigmoid(-decay_wide),
                ]
            ),
        ]
    )
    x, g, g_flat, r1, blocks_i, blocks_r = prepare(
        scalars,
        slots,
        tokens.reshape(subs, half, model),
        cotangent.reshape(subs, half, model),
        input_gate.T,
        recur_gate.T,
        (lines,),
    )
    x, *moved = lax.optimization_barrier((x, *ring_one.moving, *ring_two.moving))
    ring_one.moving, ring_two.moving = moved[:2], moved[2:]
    for s in range(2, middle + 1):
        ring_one.step(s)
        ring_two.step(s)
    one, two = ring_one.got, ring_two.got

    hop_groups = [[0, 1, ring_size - 1]] + [[s, ring_size - s] for s in range(2, middle)] + [[middle]]
    places, n1, sums_so_far = {}, [], None
    for place, offsets in enumerate(hop_groups):
        bx, by, n1_part = project(
            offsets, x, r1, [one[o] for o in offsets], [two[o] for o in offsets], sums_so_far, width, split
        )
        sums_so_far = (bx, by)
        n1.append(n1_part)
        places |= {o: (place, i) for i, o in enumerate(offsets)}

    p, cx, lx, lr, h = mixer_forward(seqs, count, bx, by, lines, blocks_i, blocks_r)
    own, other, gains = mixer_out(p, one, two, split)
    pair, other = chip_swap(own, core_swap(other), ())
    dq = unit_grad(g_flat, mlp_down, (pair,))
    h1, n2_own, r2 = norm(slots, x, gains, pair, other, (dq,))
    q, dga, dup, n2 = unit_pass(slots, both_halves(n2_own, 0), mlp_gate, mlp_up, dq)

    unit_a = Scatter(lambda *a: unit_term(0, n2, g, dga, q, *a), unit_end, True)
    unit_b = Scatter(lambda *a: unit_term(1, n2, g, dup, q, *a), unit_end, False)
    last = middle - 1

    def now():
        return tuple(token)

    unit_a.step(0)
    unit_b.step(0)
    own, other = unit_back(owners, dga, dup, mlp_gate, mlp_up, now())
    mark(own)
    got = core_swap(other)
    for s in range(1, max(last - 1, 1)):
        unit_a.step(s)
        if s == 1:
            pair, other = chip_swap(own, got, now())
        unit_b.step(s)
    unit_a.step(last - 1)
    dh1, dhr_own, second_grad = norm_back(pair, other, h1, r2, gains, g, now())
    mark(dhr_own)
    dhr = both_halves(dhr_own, 1)
    unit_b.step(last - 1)
    dbx, dby, small = mixer_backward(
        seqs, head, count, split, small_rows, dhr, two, (bx, by, cx, lx, lr, h, lines, blocks_i, blocks_r), now()
    )
    mark(dbx)
    out_own, out_other = unit_out(q, mlp_down, now())
    mark(out_own)
    out_got = core_swap(out_other)
    unit_a.step(last)
    layer_pair = pair_sum(out_own, out_got, now())
    mark(layer_pair)
    layer_other = lax.ppermute(layer_pair, "mp", chip_pair)
    own, other = input_out(dbx, dby, one, two, split, now())
    mark(own)
    got = core_swap(other)
    unit_b.step(last)
    pair, other = chip_swap(own, got, now())

    half_split = width // 2 // 128 * 128
    mixer_a = Scatter(
        lambda *a: mixer_term(0, places, half_split, chunk, owners, n1, dhr, dbx, p, small, *a),
        lambda *a: mixer_end(0, *a),
        True,
    )
    mixer_b = Scatter(
        lambda *a: mixer_term(1, places, half_split, chunk, owners, n1, dhr, dby, p, None, *a),
        lambda *a: mixer_end(1, *a),
        False,
    )
    mixer_a.step(0)
    gate_grad, down_low = unit_a.end()
    up_grad, down_high = unit_b.end()
    mixer_b.step(0)
    input_own, gain_grads = input_back(slots, pair, other, x, r1, gains, dh1, second_grad, now())
    mark(input_own)
    input_got = core_swap(input_own)
    for s in range(1, middle):
        mixer_a.step(s)
        mixer_b.step(s)
        if s == 1:
            input_grad = arrange(scalars, input_own, input_got, now())
            mark(input_grad)
        elif s == 2:
            layer_own = finish(slots, h1, layer_pair, layer_other, now())
            mark(layer_own)
            layer_got = core_swap(layer_own)
        elif s == 3:
            layer_out = arrange(scalars, layer_own, layer_got, now())
            mark(layer_out)
    value_grad, output_low, small = mixer_a.end()
    gain_grads = gain_grads + core_swap(gain_grads)
    gain_rows = jnp.pad(gain_grads.reshape(2 * ring_size, block), ((0, 0), (0, width - block)))
    small_ring = Gather(jnp.concatenate([small, gain_rows.astype(BF16)]), True)
    for s in range(1, middle + 1):
        small_ring.step(s)
    gelu_grad, output_high = mixer_b.end()
    output_grad = jnp.concatenate([output_low, output_high], 0)
    down_grad = jnp.concatenate([down_low, down_high], 0)
    down_grad = jnp.concatenate([down_low, down_high], 0)
    gate_i, gate_r, sums, gain_grads = spread(head, block, owners, small_ring.got, now())

    return (
        layer_out.reshape(tokens.shape),
        input_grad.reshape(tokens.shape),
        gain_grads[0],
        value_grad.T,
        gelu_grad.T,
        sums[:count],
        sums[count],
        gate_i.T,
        sums[count + 1],
        gate_r.T,
        sums[count + 2],
        sums[count + 3],
        output_grad,
        gain_grads[1],
        gate_grad,
        up_grad,
        down_grad,
    )


def solution(mesh):
    placed = (
        P(None, "dp", None, None),
        P(None, "dp", None, None),
        P(None, "dp"),
        P("dp"),
        P("dp", "mp"),
        P("dp", "mp"),
        P(None, "mp"),
        P("mp"),
        P("mp", None),
        P("mp"),
        P("mp", None),
        P("mp"),
        P("mp"),
        P("mp", "dp"),
        P("dp"),
        P(None, "mp"),
        P(None, "mp"),
        P("mp", None),
    )
    return jax.shard_map(
        local,
        mesh=mesh,
        in_specs=placed,
        out_specs=(
            P(None, "dp", None, None),
            P(None, "dp", None, None),
            P("dp"),
            P("dp", "mp"),
            P("dp", "mp"),
            P(None, "mp"),
            P("mp"),
            P("mp", None),
            P("mp"),
            P("mp", None),
            P("mp"),
            P("mp"),
            P("mp", "dp"),
            P("dp"),
            P("dp", "mp"),
            P("dp", "mp"),
            P("mp", "dp"),
        ),
        check_vma=False,
    )
```

```python
import jax
import jax.numpy as jnp
from jax import lax
from jax.experimental import pallas as pl
from jax.experimental.pallas import tpu as pltpu
from jax.sharding import PartitionSpec as P

EPSILON = 1e-06
DECAY_SCALE = 8.0
GELU_A = 0.7978845608028654
GELU_B = 0.044715
BF16 = jnp.bfloat16
F32 = jnp.float32
STEP = 16
HALF = 8
SUMS = 8
TN = (((0,), (0,)), ((), ()))
NT = (((1,), (1,)), ((), ()))


def gelu(v):
    return 0.5 * v * (1.0 + jnp.tanh(GELU_A * (v + GELU_B * v * v * v)))


def gelu_both(v):
    squared = v * v
    bent = jnp.tanh(GELU_A * v * (1.0 + GELU_B * squared))
    value = 0.5 * v * (1.0 + bent)
    slope = 0.5 * (1.0 + bent) + 0.5 * v * (1.0 - bent * bent) * GELU_A * (
        1.0 + 3.0 * GELU_B * squared
    )
    return value, slope


def negative_expm1(z, exp_z):
    series = 1.0 + z * (1.0 / 7.0)
    for k in (6.0, 5.0, 4.0, 3.0, 2.0):
        series = 1.0 + z * (1.0 / k) * series
    return jnp.where(z > -0.25, -z * series, 1.0 - exp_z)


def rows_of(shape):
    return lax.broadcasted_iota(jnp.int32, shape, 0)


def earlier(now, before, k, rows):
    return jnp.where(rows < k, pltpu.roll(before, k, 0), pltpu.roll(now, k, 0))


def later(now, after, k, rows):
    size = now.shape[0]
    return jnp.where(
        rows >= size - k, pltpu.roll(after, size - k, 0), pltpu.roll(now, size - k, 0)
    )


def shaped(shape, dtype):
    return jax.ShapeDtypeStruct(shape, dtype)


def launch(
    kernel, inputs, out_shape, name, scalars=0, after=(), mib=20, scratch=(), aliases=None, grid=None, flops=1
):
    count, extra = len(inputs), len(after)
    waits = [pl.BlockSpec(memory_space=pl.ANY)] * extra
    in_specs = [pl.BlockSpec(memory_space=pltpu.SMEM)] * scalars
    more = {}
    if grid is None:
        in_specs += [pl.BlockSpec(memory_space=pltpu.VMEM)] * (count - scalars)
    else:
        in_specs += grid[1]
        more = {"grid": grid[0], "out_specs": grid[2]}
    return pl.pallas_call(
        lambda *refs: kernel(*refs[:count], *refs[count + extra :]),
        in_specs=in_specs + waits,
        out_shape=out_shape,
        scratch_shapes=list(scratch),
        input_output_aliases=aliases or {},
        compiler_params=pltpu.CompilerParams(vmem_limit_bytes=mib << 20),
        cost_estimate=pl.CostEstimate(flops=flops, bytes_accessed=1, transcendentals=0),
        name=name,
        **more,
    )(*inputs, *after)


def in_hbm(array):
    return pltpu.with_memory_space_constraint(array, pltpu.HBM)


def mixer_forward_kernel(
    seqs, count, bx, by, lines, blocks_i, blocks_r, p_o, cx_o, lx_o, lr_o, h_o
):
    total, width = bx.shape
    length = total // seqs
    steps = length // STEP
    rows16 = rows_of((STEP, width))
    w = [jnp.broadcast_to(lines[k : k + 1, :], (STEP, width)) for k in range(count)]
    shift = jnp.broadcast_to(lines[count : count + 1, :], (STEP, width))
    bias_i, bias_r = lines[count + 1 : count + 2, :], lines[count + 2 : count + 3, :]
    soft = lines[count + 3 : count + 4, :]
    for seq in range(seqs):

        def conv(i, before):
            at = pl.ds(pl.multiple_of(seq * length + i * STEP, STEP), STEP)
            now = bx[at, :]
            mixed = shift + w[0] * now
            for k in range(1, count):
                mixed = mixed + w[k] * earlier(now, before, k, rows16)
            cx_o[at, :] = mixed.astype(BF16)
            return now

        lax.fori_loop(0, steps, conv, jnp.zeros((STEP, width), F32))
    lx_o[...] = lax.dot_general(cx_o[...], blocks_i[...], NT, preferred_element_type=F32) + bias_i
    lr_o[...] = lax.dot_general(cx_o[...], blocks_r[...], NT, preferred_element_type=F32) + bias_r
    rows8 = rows_of((HALF, width))
    soft8 = jnp.broadcast_to(-DECAY_SCALE * soft, (HALF, width))

    def scan(i, carries):
        out = []
        for seq in range(seqs):
            carry = carries[seq]
            base = seq * length + i * STEP
            at = pl.ds(pl.multiple_of(base, STEP), STEP)
            cx16 = cx_o[at, :].astype(F32)
            products = []
            for part in range(STEP // HALF):
                here = pl.ds(pl.multiple_of(base + part * HALF, HALF), HALF)
                cx = cx16[part * HALF : (part + 1) * HALF, :]
                ix = jax.nn.sigmoid(lx_o[here, :])
                la = soft8 * jax.nn.sigmoid(lr_o[here, :])
                a = jnp.exp(la)
                rest = negative_expm1(2.0 * la, a * a)
                m = jnp.where(rest > 0.0, rest * lax.rsqrt(rest), 0.0)
                u = m * ix * cx
                for s in (1, 2, 4):
                    keep = rows8 >= s
                    u = u + jnp.where(keep, a * pltpu.roll(u, s, 0), 0.0)
                    a = jnp.where(keep, a * pltpu.roll(a, s, 0), a)
                h = u + a * carry
                carry = jnp.broadcast_to(h[HALF - 1 : HALF, :], (HALF, width))
                h_o[here, :] = h
                products.append(h * gelu(by[here, :]))
            p_o[at, :] = jnp.concatenate(products, 0).astype(BF16)
            out.append(carry)
        return tuple(out)

    lax.fori_loop(0, steps, scan, tuple(jnp.zeros((HALF, width), F32) for _ in range(seqs)))


def mixer_forward(seqs, count, bx, by, lines, blocks_i, blocks_r):
    low, full = shaped(bx.shape, BF16), shaped(bx.shape, F32)
    return launch(
        lambda *refs: mixer_forward_kernel(seqs, count, *refs),
        (bx, by, lines, blocks_i, blocks_r),
        (low, low, full, full, full),
        "mixer_forward",
    )


def mixer_backward_kernel(seqs, head, count, split, dhr, *refs):
    ring_size = dhr.shape[0]
    second = refs[:ring_size]
    bx, by, cx_i, lx_i, lr_i, h_i, lines, blocks_i, blocks_r = refs[ring_size : ring_size + 9]
    dbx_o, dby_o, small_o, dlx_o, dlr_o, dcx_s, dp = refs[ring_size + 9 :]
    skip = bx.shape[1] - split
    soft, gate_soft = lines[count + 3 : count + 4, :], lines[count + 4 : count + 5, :]
    for o in range(ring_size):
        part = lax.dot_general(dhr[o], second[o][skip:, :], NT, preferred_element_type=F32)
        dp[...] = part if o == 0 else dp[...] + part
    total, width = bx.shape
    length = total // seqs
    steps = length // STEP
    rows8 = rows_of((HALF, width))
    soft8 = jnp.broadcast_to(-DECAY_SCALE * soft, (HALF, width))
    zero = jnp.zeros((HALF, width), F32)

    def scan(j, state):
        i = steps - 1 - j
        sums_i, sums_r, sums_d = state[0]
        out = []
        for seq in range(seqs):
            a_after, e_after = state[1][seq]
            base = seq * length + i * STEP
            at = pl.ds(pl.multiple_of(base, STEP), STEP)
            cx16 = cx_i[at, :].astype(F32)
            dby_parts, dlx_parts, dlr_parts = [None, None], [None, None], [None, None]
            for part in (1, 0):
                start = base + part * HALF
                here = pl.ds(pl.multiple_of(start, HALF), HALF)
                cx = cx16[part * HALF : (part + 1) * HALF, :]
                ix = jax.nn.sigmoid(lx_i[here, :])
                ra = jax.nn.sigmoid(lr_i[here, :])
                la = soft8 * ra
                a = jnp.exp(la)
                rest = negative_expm1(2.0 * la, a * a)
                inverse = lax.rsqrt(rest)
                m = rest * inverse
                h = h_i[here, :]
                first = (i == 0) if part == 0 else False
                back = jnp.maximum(start - HALF, 0)
                before = h_i[pl.ds(pl.multiple_of(back, HALF), HALF), :]
                if part == 0:
                    before = jnp.where(i == 0, 0.0, before)
                h_prev = earlier(h, before, 1, rows8)
                gy, slope = gelu_both(by[here, :])
                grad = dp[here, :]
                dby_parts[part] = grad * h * slope
                e = grad * gy
                f = later(a, a_after, 1, rows8)
                for s in (1, 2, 4):
                    keep = rows8 < HALF - s
                    e = e + jnp.where(keep, f * pltpu.roll(e, HALF - s, 0), 0.0)
                    f = jnp.where(keep, f * pltpu.roll(f, HALF - s, 0), f)
                e = e + f * e_after
                e_after = jnp.broadcast_to(e[0:1, :], (HALF, width))
                a_after = a
                eix = e * ix
                dla = (e * h_prev - eix * cx * a * inverse) * a
                dlx = eix * m * cx * (1.0 - ix)
                dlr = dla * la * (1.0 - ra)
                sums_i = sums_i + dlx
                sums_r = sums_r + dlr
                sums_d = sums_d + dla * ra
                dlx_parts[part], dlr_parts[part] = dlx, dlr
                dcx_s[here, :] = eix * m
            dby_o[at, :] = jnp.concatenate(dby_parts, 0).astype(BF16)
            dlx_o[at, :] = jnp.concatenate(dlx_parts, 0).astype(BF16)
            dlr_o[at, :] = jnp.concatenate(dlr_parts, 0).astype(BF16)
            out.append((a_after, e_after))
        return (sums_i, sums_r, sums_d), tuple(out)

    (sums_i, sums_r, sums_d), _ = lax.fori_loop(
        0, steps, scan, ((zero, zero, zero), tuple((zero, zero) for _ in range(seqs)))
    )
    dcx_s[...] += jnp.dot(dlx_o[...], blocks_i[...], preferred_element_type=F32) + jnp.dot(
        dlr_o[...], blocks_r[...], preferred_element_type=F32
    )
    rows16 = rows_of((STEP, width))
    w = [jnp.broadcast_to(lines[k : k + 1, :], (STEP, width)) for k in range(count)]
    zero16 = jnp.zeros((STEP, width), F32)
    sums_t = tuple(zero16 for _ in range(count))
    sums_b = zero16
    for seq in range(seqs):

        def conv(j, state):
            after, tap_sums, shift_sum = state
            at = pl.ds(pl.multiple_of(seq * length + (steps - 1 - j) * STEP, STEP), STEP)
            now = dcx_s[at, :]
            source = bx[at, :]
            grad = w[0] * now
            new_sums = [tap_sums[0] + now * source]
            for k in range(1, count):
                moved = later(now, after, k, rows16)
                grad = grad + w[k] * moved
                new_sums.append(tap_sums[k] + moved * source)
            dbx_o[at, :] = grad.astype(BF16)
            return now, tuple(new_sums), shift_sum + now

        _, sums_t, sums_b = lax.fori_loop(0, steps, conv, (zero16, sums_t, sums_b))
    rows = [jnp.sum(item, 0, keepdims=True) for item in (*sums_t, sums_b, sums_i, sums_r)]
    rows.append(DECAY_SCALE * gate_soft * jnp.sum(sums_d, 0, keepdims=True))
    spare = small_o.shape[0] - 2 * head - SUMS
    if spare:
        rows.append(jnp.zeros((spare, width), F32))
    small_o[2 * head :, :] = jnp.concatenate(rows, 0).astype(BF16)
    lanes = lax.broadcasted_iota(jnp.int32, (head, width), 1)
    for gate, grads in enumerate((dlx_o, dlr_o)):
        whole = lax.dot_general(grads[...], cx_i[...], TN, preferred_element_type=F32)
        picked = whole[:head]
        for i in range(1, width // head):
            picked = jnp.where(lanes < i * head, picked, whole[i * head : (i + 1) * head])
        small_o[gate * head : (gate + 1) * head, :] = picked.astype(BF16)


def mixer_backward(seqs, head, count, split, small_rows, dhr, second, saved, after):
    total, width = saved[0].shape
    low = shaped((total, width), BF16)
    return launch(
        lambda *refs: mixer_backward_kernel(seqs, head, count, split, *refs),
        (dhr, *second, *saved),
        (low, low, shaped((small_rows, width), BF16)),
        "mixer_backward",
        after=after,
        mib=32,
        scratch=[
            pltpu.VMEM((total, width), BF16),
            pltpu.VMEM((total, width), BF16),
            pltpu.VMEM((total, width), F32),
            pltpu.VMEM((total, width), F32),
        ],
    )


def pack_kernel(split, value, gelu_w, output, gain_one, gain_two, one_o, two_o):
    width = value.shape[0]
    one_o[:width, :] = value[...]
    spare = jnp.zeros((14, value.shape[1]), F32)
    lines = jnp.concatenate([gain_one[...].astype(F32), gain_two[...].astype(F32), spare], 0)
    one_o[width : width + 16, :] = lines.astype(BF16)
    one_o[width + 16 :, :] = gelu_w[:split, :]
    two_o[: width - split, :] = gelu_w[split:, :]
    two_o[width - split :, :] = output[...]


def pack(split, value, gelu_w, output, gain_one, gain_two):
    width, block = value.shape
    return launch(
        lambda *refs: pack_kernel(split, *refs),
        (value, gelu_w, output, gain_one, gain_two),
        (shaped((width + 16 + split, block), BF16), shaped((2 * width - split, block), BF16)),
        "pack",
    )


def prepare_kernel(scalars, slots, tokens, cotangent, gate_i, gate_r, x_o, g_o, flat_o, r_o, blocks_i, blocks_r):
    ring_size, total, block = x_o.shape
    half = total // 2
    row_count = (scalars.shape[0] - 1) // 2
    length = half // row_count
    rows = lax.broadcasted_iota(jnp.int32, (length, block), 0)
    for place in range(2):
        sub = scalars[0] if place == 0 else 1 - scalars[0]
        for row in range(row_count):
            at = slice(place * half + row * length, place * half + (row + 1) * length)
            source = pl.ds(row * length, length)
            valid = jnp.where(rows < scalars[1 + sub * row_count + row], 1.0, 0.0)
            squares = jnp.zeros((length, block), F32)
            for k in range(ring_size):
                columns = slice(k * block, (k + 1) * block)
                piece = tokens[sub, source, columns]
                wide = piece.astype(F32)
                squares = squares + wide * wide
                x_o[slots[k], at, :] = piece
                masked = (cotangent[sub, source, columns].astype(F32) * valid).astype(BF16)
                g_o[slots[k], at, :] = masked
                flat_o[at, columns] = masked
            mean = jnp.sum(squares, 1, keepdims=True) * (1.0 / (ring_size * block))
            r_o[at, :] = lax.rsqrt(mean + EPSILON)
    head, width = gate_i.shape
    lanes = lax.broadcasted_iota(jnp.int32, (head, width), 1)
    for source, out in ((gate_i, blocks_i), (gate_r, blocks_r)):
        wide = source[...].astype(F32)
        for i in range(width // head):
            inside = (lanes >= i * head) & (lanes < (i + 1) * head)
            out[i * head : (i + 1) * head, :] = jnp.where(inside, wide, 0.0).astype(BF16)


def prepare(scalars, slots, tokens, cotangent, gate_i, gate_r, after):
    subs, half, model = tokens.shape
    total, ring_size, width = subs * half, slots.shape[0], gate_i.shape[1]
    rel = shaped((ring_size, total, model // ring_size), BF16)
    blocks = shaped((width, width), BF16)
    return launch(
        prepare_kernel,
        (scalars, slots, tokens, cotangent, gate_i, gate_r),
        (rel, rel, shaped((total, model), BF16), shaped((total, 1), F32), blocks, blocks),
        "prepare",
        scalars=2,
        after=after,
    )


def project_kernel(offsets, first, width, split, x, r1, *refs):
    count = len(offsets)
    one, two = refs[:count], refs[count : 2 * count]
    rest = refs[2 * count :]
    if not first:
        before = rest[:2]
        rest = rest[2:]
    bx, by, n1_o = rest
    scale = r1[...]
    for i, o in enumerate(offsets):
        gain = one[i][width : width + 16, :].astype(F32)[0:1, :]
        n1 = (x[o].astype(F32) * scale * gain).astype(BF16)
        n1_o[i] = n1
        for out, place, columns, weight in (
            (bx, 0, slice(0, width), one[i][:width, :]),
            (by, 1, slice(0, split), one[i][width + 16 :, :]),
            (by, 1, slice(split, width), two[i][: width - split, :]),
        ):
            part = lax.dot_general(n1, weight, NT, preferred_element_type=F32)
            if i > 0:
                out[:, columns] += part
            elif first:
                out[:, columns] = part
            else:
                out[:, columns] = before[place][:, columns] + part


def project(offsets, x, r1, one, two, before, width, split):
    total, block = x.shape[1:]
    count = len(offsets)
    full = shaped((total, width), F32)
    at = 2 + 2 * count
    return launch(
        lambda *refs: project_kernel(offsets, before is None, width, split, *refs),
        (x, r1, *one, *two, *(before or ())),
        (full, full, shaped((count, total, block), BF16)),
        "project",
        aliases={} if before is None else {at: 0, at + 1: 1},
    )


def mixer_out_kernel(skip, p, *refs):
    own_o, other_o, gains_o = refs[-3:]
    count, half = own_o.shape[:2]
    width = p.shape[1]
    for o in range(count):
        part = jnp.dot(p[...], refs[count + o][skip:, :], preferred_element_type=F32)
        own_o[o] = part[:half]
        other_o[o] = part[half:].astype(BF16)
        gains_o[o] = refs[o][width : width + 16, :].astype(F32)[0:2, :]


def mixer_out(p, one, two, split):
    total, width = p.shape
    count, block = len(one), one[0].shape[1]
    shape = (count, total // 2, block)
    return launch(
        lambda *refs: mixer_out_kernel(width - split, *refs),
        (p, *one, *two),
        (shaped(shape, F32), shaped(shape, BF16), shaped((count, 2, block), F32)),
        "mixer_out",
        mib=24,
    )


def input_out_kernel(split, dbx, dby, *refs):
    own_o, other_o = refs[-2:]
    count, half = own_o.shape[:2]
    width = dbx.shape[1]
    for o in range(count):
        one, two = refs[o], refs[count + o]
        part = (
            jnp.dot(dbx[...], one[:width, :], preferred_element_type=F32)
            + jnp.dot(dby[:, :split], one[width + 16 :, :], preferred_element_type=F32)
            + jnp.dot(dby[:, split:], two[: width - split, :], preferred_element_type=F32)
        )
        own_o[o] = part[:half]
        other_o[o] = part[half:].astype(BF16)


def input_out(dbx, dby, one, two, split, after):
    shape = (len(one), dbx.shape[0] // 2, one[0].shape[1])
    return launch(
        lambda *refs: input_out_kernel(split, *refs),
        (dbx, dby, *one, *two),
        (shaped(shape, F32), shaped(shape, BF16)),
        "input_out",
        after=after,
        mib=24,
    )


def pair_kernel(own, got, out):
    out[...] = (own[...] + got[...].astype(F32)).astype(BF16)


def pair_sum(own, got, after):
    return launch(pair_kernel, (own, got), shaped(own.shape, BF16), "pair_sum", after=after)


def relay_kernel(source, out):
    out[...] = source[...]


def relay(source, after):
    return launch(relay_kernel, (source,), shaped(source.shape, source.dtype), "relay", after=after)


def norm_kernel(slots, x, gains, pair, other, h_o, n_o, r_o):
    ring_size, half, block = h_o.shape
    squares = jnp.zeros((half, block), F32)
    for o in range(ring_size):
        h = x[o, 0:half, :].astype(F32) + (pair[o].astype(F32) + other[o].astype(F32))
        h_o[o] = h
        squares = squares + h * h
    mean = jnp.sum(squares, 1, keepdims=True) * (1.0 / (ring_size * block))
    scale = lax.rsqrt(mean + EPSILON)
    r_o[...] = scale
    for k in range(ring_size):
        o = slots[k]
        n_o[:, k * block : (k + 1) * block] = (h_o[o] * scale * gains[o, 1:2, :]).astype(BF16)


def norm(slots, x, gains, pair, other, after):
    ring_size, half, block = pair.shape
    return launch(
        norm_kernel,
        (slots, x, gains, pair, other),
        (shaped(pair.shape, F32), shaped((half, ring_size * block), BF16), shaped((half, 1), F32)),
        "norm",
        scalars=1,
        after=after,
    )


def norm_back_kernel(pair, other, h1, r2, gains, g, dh_o, dhr_o, grad_o):
    ring_size, half, block = h1.shape
    dots = jnp.zeros((half, block), F32)
    scale = r2[...]
    for o in range(ring_size):
        product = (pair[o].astype(F32) + other[o].astype(F32)) * h1[o]
        dots = dots + product * gains[o, 1:2, :]
        grad_o[o] = jnp.sum(product * scale, 0, keepdims=True)
    mean = jnp.sum(dots, 1, keepdims=True) * (1.0 / (ring_size * block))
    bend = scale * scale * scale * mean
    for o in range(ring_size):
        grad = pair[o].astype(F32) + other[o].astype(F32)
        dh = g[o, 0:half, :].astype(F32) + scale * (grad * gains[o, 1:2, :]) - h1[o] * bend
        dh_o[o] = dh
        dhr_o[o] = dh.astype(BF16)


def norm_back(pair, other, h1, r2, gains, g, after):
    ring_size, half, block = pair.shape
    return launch(
        norm_back_kernel,
        (pair, other, h1, r2, gains, g),
        (shaped(pair.shape, F32), shaped(pair.shape, BF16), shaped((ring_size, 1, block), F32)),
        "norm_back",
        after=after,
    )


def input_back_kernel(slots, pair, other, x, r1, gains, dh1, second, out_o, grad_o):
    ring_size, half, block = dh1.shape
    dots = jnp.zeros((half, block), F32)
    scale = r1[0:half, :]
    for o in range(ring_size):
        product = (pair[o].astype(F32) + other[o].astype(F32)) * x[o, 0:half, :].astype(F32)
        dots = dots + product * gains[o, 0:1, :]
        grad_o[o, 0:1, :] = jnp.sum(product * scale, 0, keepdims=True)
        grad_o[o, 1:2, :] = second[o]
    mean = jnp.sum(dots, 1, keepdims=True) * (1.0 / (ring_size * block))
    bend = scale * scale * scale * mean
    for k in range(ring_size):
        o = slots[k]
        grad = pair[o].astype(F32) + other[o].astype(F32)
        out_o[:, k * block : (k + 1) * block] = (
            dh1[o] + scale * (grad * gains[o, 0:1, :]) - x[o, 0:half, :].astype(F32) * bend
        )


def input_back(slots, pair, other, x, r1, gains, dh1, second, after):
    ring_size, half, block = pair.shape
    return launch(
        input_back_kernel,
        (slots, pair, other, x, r1, gains, dh1, second),
        (shaped((half, ring_size * block), F32), shaped((ring_size, 2, block), F32)),
        "input_back",
        scalars=1,
        after=after,
    )


def finish_kernel(slots, h1, pair, other, beside, out_o):
    ring_size, half, block = h1.shape
    out_o[0] = beside[...]
    for k in range(ring_size):
        columns = slice(k * block, (k + 1) * block)
        summed = pair[:, columns].astype(F32) + other[:, columns].astype(F32)
        out_o[1, :, columns] = h1[slots[k]] + summed


def finish(slots, h1, pair, other, beside, after):
    return launch(
        finish_kernel,
        (slots, h1, pair, other, beside),
        shaped((2, *beside.shape), F32),
        "finish",
        scalars=1,
        after=after,
        mib=24,
    )


def arrange_kernel(scalars, own, got, *outs):
    core = scalars[0]
    for i, out in enumerate(outs):
        out[core] = own[i]
        out[1 - core] = got[i]


def arrange(scalars, own, got, after):
    out = shaped((2, *own.shape[1:]), own.dtype)
    return launch(
        arrange_kernel, (scalars, own, got), (out,) * own.shape[0], "arrange", scalars=1, after=after, mib=24
    )


def unit_grad_kernel(g, down, dq_o):
    dq_o[...] = lax.dot_general(g[...], down[...], NT, preferred_element_type=F32)


def unit_grad(g, down, after):
    total, model = g.shape
    units = down.shape[0]
    tile = 256
    grid = (
        (units // tile,),
        [pl.BlockSpec((total, model), lambda i: (0, 0)), pl.BlockSpec((tile, model), lambda i: (i, 0))],
        pl.BlockSpec((total, tile), lambda i: (0, i)),
    )
    return launch(unit_grad_kernel, (g, in_hbm(down)), shaped((total, units), F32), "unit_grad", after=after, grid=grid)


def unit_kernel(with_rel, slots, n2, gate, up, dq, q_o, dga_o, dup_o, *rel):
    if with_rel:
        rel_o = rel[0]
        ring_size, total, block = rel_o.shape

        @pl.when(pl.program_id(0) == 0)
        def _():
            for k in range(ring_size):
                rel_o[slots[k]] = n2[:, k * block : (k + 1) * block]

    ga = jnp.dot(n2[...], gate[...], preferred_element_type=F32)
    upward = jnp.dot(n2[...], up[...], preferred_element_type=F32)
    value, slope = gelu_both(ga)
    grad = dq[...]
    q_o[...] = (value * upward).astype(BF16)
    dga_o[...] = (grad * upward * slope).astype(BF16)
    dup_o[...] = (grad * value).astype(BF16)


def unit_pass(part, slots, n2, gate, up, dq, after):
    total, model = n2.shape
    ring_size = slots.shape[0]
    share = gate.shape[1] // 2
    tile = 256
    first = part * (share // tile)
    rel = (ring_size, total, model // ring_size)
    wide = pl.BlockSpec((total, tile), lambda i: (0, i))
    out = shaped((total, share), BF16)
    grid = (
        (share // tile,),
        [
            pl.BlockSpec((total, model), lambda i: (0, 0)),
            pl.BlockSpec((model, tile), lambda i: (0, i + first)),
            pl.BlockSpec((model, tile), lambda i: (0, i + first)),
            pl.BlockSpec((total, tile), lambda i: (0, i + first)),
        ],
        [wide, wide, wide] + [pl.BlockSpec(rel, lambda i: (0, 0, 0))] * (1 - part),
    )
    return launch(
        lambda *refs: unit_kernel(part == 0, *refs),
        (slots, n2, in_hbm(gate), in_hbm(up), dq),
        (out, out, out) + (shaped(rel, BF16),) * (1 - part),
        "unit_pass",
        scalars=1,
        after=after,
        mib=28,
        grid=grid,
    )


def unit_out_kernel(q_a, q_b, down, own_o, other_o):
    half = own_o.shape[0]
    share = q_a.shape[1]
    part = jnp.dot(q_a[...], down[:share, :], preferred_element_type=F32)
    part = part + jnp.dot(q_b[...], down[share:, :], preferred_element_type=F32)
    own_o[...] = part[:half]
    other_o[...] = part[half:].astype(BF16)


def unit_out(q_a, q_b, down, after):
    total, share = q_a.shape
    units, model = down.shape
    half = total // 2
    tile = 256
    out = pl.BlockSpec((half, tile), lambda i: (0, i))
    left = pl.BlockSpec((total, share), lambda i: (0, 0))
    grid = ((model // tile,), [left, left, pl.BlockSpec((units, tile), lambda i: (0, i))], [out, out])
    return launch(
        unit_out_kernel,
        (q_a, q_b, in_hbm(down)),
        (shaped((half, model), F32), shaped((half, model), BF16)),
        "unit_out",
        after=after,
        grid=grid,
    )


def unit_back_kernel(owners, dga_a, dga_b, dup_a, dup_b, gate, up, *refs):
    own_o, other_o = refs[-2:]
    half = other_o.shape[1]
    share = dga_a.shape[1]
    part = None
    for left, right in (
        (dga_a, gate[:, :share]),
        (dga_b, gate[:, share:]),
        (dup_a, up[:, :share]),
        (dup_b, up[:, share:]),
    ):
        term = lax.dot_general(left[...], right, NT, preferred_element_type=F32)
        part = term if part is None else part + term
    own_o[0] = part[:half]
    other_o[0] = part[half:].astype(BF16)


def unit_back(owners, grads, gate, up, after):
    ring_size = owners.shape[0]
    total, share = grads[0].shape
    model, units = gate.shape
    half = total // 2
    block = model // ring_size
    left = pl.BlockSpec((total, share), lambda o, owners: (0, 0))
    weight = pl.BlockSpec((block, units), lambda o, owners: (owners[o], 0))
    out = pl.BlockSpec((1, half, block), lambda o, owners: (o, 0, 0))
    return pl.pallas_call(
        unit_back_kernel,
        grid_spec=pltpu.PrefetchScalarGridSpec(
            num_scalar_prefetch=1,
            grid=(ring_size,),
            in_specs=[left] * 4 + [weight, weight, *[pl.BlockSpec(memory_space=pl.ANY)] * len(after)],
            out_specs=[out, out],
        ),
        out_shape=(shaped((ring_size, half, block), F32), shaped((ring_size, half, block), BF16)),
        compiler_params=pltpu.CompilerParams(vmem_limit_bytes=24 << 20),
        cost_estimate=pl.CostEstimate(flops=1, bytes_accessed=1, transcendentals=0),
        name="unit_back",
    )(owners, *grads, in_hbm(gate), in_hbm(up), *after)


def unit_term_kernel(turns, fold, n2, g, dga, dup, q, *refs):
    share = q.shape[1]
    rest = list(refs)
    outs = rest[len(rest) - len(turns) - (3 if fold else 0) :]
    parts = [slice(i * share, (i + 1) * share) for i in range(3)]

    def terms(o):
        return (
            lax.dot_general(n2[o], dga[...], TN, preferred_element_type=F32),
            lax.dot_general(n2[o], dup[...], TN, preferred_element_type=F32),
        )

    for (o, has), out in zip(turns, outs):
        recv = rest.pop(0) if has else None
        down = lax.dot_general(g[o], q[...], TN, preferred_element_type=F32)
        for grad, columns in zip((*terms(o), down), parts):
            if recv is not None:
                grad = grad + recv[:, columns].astype(F32)
            out[:, columns] = grad.astype(BF16)
    if fold:
        recv = rest.pop(0)
        gate_o, up_o, down_o = outs[len(turns) :]
        for grad, columns, out in zip(terms(0), parts, (gate_o, up_o)):
            out[...] = grad + recv[:, columns].astype(F32)
        down = lax.dot_general(q[...], g[0], TN, preferred_element_type=F32)
        down_o[...] = down + recv[:, parts[2]].astype(F32).T


def unit_term(n2, g, dga, dup, q, turns, fold, after, weight=100 * 10**9):
    block, share = n2.shape[2], q.shape[1]
    arrived = [item for _, item in turns if item is not None] + ([] if fold is None else [fold])
    plan = [(o, item is not None) for o, item in turns]
    out = [shaped((block, 3 * share), BF16) for _ in turns]
    if fold is not None:
        out += [shaped((block, share), F32), shaped((block, share), F32), shaped((share, block), F32)]
    return launch(
        lambda *refs: unit_term_kernel(plan, fold is not None, *refs),
        (n2, g, dga, dup, q, *arrived),
        tuple(out),
        "unit_term",
        after=after,
        mib=24,
        flops=weight if arrived else 1,
    )


def unit_end_kernel(count, *refs):
    own, item, low, outs = refs[:3], refs[3], refs[4 : 4 + count], refs[4 + count :]
    share = own[0].shape[1]
    for i in range(2):
        total = own[i][...] + item[:, i * share : (i + 1) * share].astype(F32)
        if count:
            outs[i][:, :share] = low[i][...]
            outs[i][:, share:] = total
        else:
            outs[i][...] = total
    total = own[2][...] + item[:, 2 * share :].astype(F32).T
    if count:
        outs[2][:share, :] = low[2][...]
        outs[2][share:, :] = total
    else:
        outs[2][...] = total


def unit_end(low, own, item, after):
    block, share = own[0].shape
    wide = 2 if low else 1
    grad = shaped((block, wide * share), F32)
    return launch(
        lambda *refs: unit_end_kernel(len(low), *refs),
        (*own, item, *low),
        (grad, grad, shaped((wide * share, block), F32)),
        "unit_end",
        after=after,
        flops=100 * 10**9,
    )


def small_pieces(width, block):
    return [slice(i, min(i + block, width)) for i in range(0, width, block)]


def mixer_term_kernel(part, places, groups, split, chunk, turns, fold, owners, *refs):
    n1_all = refs[:groups]
    dhr, grads, p = refs[groups : groups + 3]
    rest = list(refs[groups + 3 :])
    extra = rest.pop(0) if part == 0 else None
    outs = rest[len(rest) - len(turns) - (3 - part if fold else 0) :]
    width, block = grads.shape[1], dhr.shape[2]
    columns = slice(0, split) if part == 0 else slice(split, width)
    size = columns.stop - columns.start
    at = width + size
    pieces = small_pieces(width, block)

    def terms(o, recv):
        group, i = places[o]
        grad = lax.dot_general(grads[...], n1_all[group][i], TN, preferred_element_type=F32)
        out = lax.dot_general(p[:, columns], dhr[o], TN, preferred_element_type=F32)
        if recv is not None:
            grad = grad + recv[:width, :].astype(F32)
            out = out + recv[width:at, :].astype(F32)
        return grad, out

    def small(o, recv):
        own = extra[pl.ds(pl.multiple_of(owners[o] * chunk, 16), chunk), :].astype(F32)
        out = []
        for i, piece in enumerate(pieces):
            total = own[:, piece]
            if recv is not None:
                total = total + recv[at + i * chunk : at + (i + 1) * chunk, : piece.stop - piece.start].astype(F32)
            out.append(total)
        return out

    for (o, has), out_ref in zip(turns, outs):
        recv = rest.pop(0) if has else None
        grad, out = terms(o, recv)
        out_ref[:width, :] = grad.astype(BF16)
        out_ref[width:at, :] = out.astype(BF16)
        if part == 0:
            for i, total in enumerate(small(o, recv)):
                rows = slice(at + i * chunk, at + (i + 1) * chunk)
                wide = total.shape[1]
                out_ref[rows, :wide] = total.astype(BF16)
                if wide < block:
                    out_ref[rows, wide:] = jnp.zeros((chunk, block - wide), BF16)
    if fold:
        recv = rest.pop(0)
        outs[len(turns)][...], outs[len(turns) + 1][...] = terms(0, recv)
        if part == 0:
            for piece, total in zip(pieces, small(0, recv)):
                outs[len(turns) + 2][:, piece] = total


def mixer_term(part, places, split, chunk, owners, n1, dhr, grads, p, extra, turns, fold, after):
    block, width = dhr.shape[2], grads.shape[1]
    size = split if part == 0 else width - split
    arrived = [item for _, item in turns if item is not None] + ([] if fold is None else [fold])
    more = 0 if part == 1 else chunk * len(small_pieces(width, block))
    out = [shaped((width + size + more, block), BF16) for _ in turns]
    if fold is not None:
        out += [shaped((width, block), F32), shaped((size, block), F32)]
        out += [shaped((chunk, width), F32)] if part == 0 else []
    plan = [(o, item is not None) for o, item in turns]
    return launch(
        lambda *refs: mixer_term_kernel(part, places, len(n1), split, chunk, plan, fold is not None, *refs),
        (owners, *n1, dhr, grads, p, *([extra] if part == 0 else []), *arrived),
        tuple(out),
        "mixer_term",
        scalars=1,
        after=after,
        mib=24,
        flops=100 * 10**9,
    )


def mixer_end_kernel(part, *refs):
    own, item = refs[: 3 - part], refs[3 - part]
    extra, outs = refs[4 - part : 6 - 2 * part], refs[6 - 2 * part :]
    width, block = own[0].shape
    at = width + own[1].shape[0]
    outs[0][...] = own[0][...] + item[:width, :].astype(F32)
    total = own[1][...] + item[width:at, :].astype(F32)
    if part == 1:
        low = extra[0]
        split = low.shape[0]
        outs[1][:split, :] = low[...]
        outs[1][split:, :] = total
        return
    outs[1][...] = total
    chunk = own[2].shape[0]
    for i, piece in enumerate(small_pieces(width, block)):
        rows = slice(at + i * chunk, at + (i + 1) * chunk)
        total = own[2][:, piece] + item[rows, : piece.stop - piece.start].astype(F32)
        outs[2][:chunk, piece] = total.astype(BF16)
    ring_size = extra[0].shape[0]
    lines = jnp.concatenate([extra[0][o] + extra[1][o] for o in range(ring_size)], 0)
    outs[2][chunk:, :block] = lines.astype(BF16)
    outs[2][chunk:, block:] = jnp.zeros((2 * ring_size, width - block), BF16)


def mixer_end(part, extra, own, item, after):
    width, block = own[0].shape
    if part == 0:
        rows = own[2].shape[0] + 2 * extra[0].shape[0]
        shapes = [own[0].shape, own[1].shape, (rows, width)]
    else:
        shapes = [own[0].shape, own[0].shape]
    return launch(
        lambda *refs: mixer_end_kernel(part, *refs),
        (*own, item, *extra),
        tuple(shaped(shape, BF16 if i == 2 else F32) for i, shape in enumerate(shapes)),
        "mixer_end",
        after=after,
        flops=100 * 10**9,
    )


def spread_kernel(head, owners, *refs):
    ring_size = owners.shape[0]
    gate_i, gate_r, sums, gain_o, whole = refs[ring_size:]
    block = gain_o.shape[1]
    chunk = refs[0].shape[0] - 2 * ring_size
    gain = jnp.zeros((2, block), F32)
    for o in range(ring_size):
        at = pl.ds(pl.multiple_of(owners[o] * chunk, 16), chunk)
        whole[at, :] = refs[o][:chunk, :].astype(F32)
        mine = 2 * ((ring_size - o) % ring_size)
        gain = gain + refs[o][chunk:, :block].astype(F32)[mine : mine + 2, :]
    gate_i[...] = whole[:head, :]
    gate_r[...] = whole[head : 2 * head, :]
    sums[...] = whole[2 * head : 2 * head + SUMS, :]
    gain_o[...] = gain


def spread(head, block, owners, chunks, after):
    ring_size = len(chunks)
    rows, width = chunks[0].shape
    gate = shaped((head, width), F32)
    return launch(
        lambda *refs: spread_kernel(head, *refs),
        (owners, *chunks),
        (gate, gate, shaped((SUMS, width), F32), shaped((2, block), F32)),
        "spread",
        scalars=1,
        after=after,
        scratch=[pltpu.VMEM(((rows - 2 * ring_size) * ring_size, width), F32)],
    )


def local(
    tokens,
    cotangent,
    row_length,
    first_gain,
    value_weight,
    gelu_weight,
    conv_weight,
    conv_bias,
    input_gate,
    input_bias,
    recur_gate,
    recur_bias,
    decay_param,
    output_weight,
    second_gain,
    mlp_gate,
    mlp_up,
    mlp_down,
):
    ring_size = lax.axis_size("dp")
    middle = ring_size // 2
    ring = [2 * i if i < middle else 2 * (ring_size - 1 - i) + 1 for i in range(ring_size)]
    onward = [(ring[i], ring[(i + 1) % ring_size]) for i in range(ring_size)]
    backward = [(b, a) for a, b in onward]
    me = lax.axis_index("dp")
    core = lax.axis_index("mp") % 2
    core_pair = [(i, i ^ 1) for i in range(4)]
    chip_pair = [(i, i ^ 2) for i in range(4)]
    index = jnp.arange(ring_size, dtype=jnp.int32)

    def spot_of(place):
        return jnp.where(place % 2 == 0, place // 2, ring_size - 1 - place // 2)

    spots = (spot_of(me) + index) % ring_size
    owners = jnp.where(spots < middle, 2 * spots, 2 * (ring_size - 1 - spots) + 1).astype(jnp.int32)
    slots = ((spot_of(index) - spot_of(me) + ring_size) % ring_size).astype(jnp.int32)

    subs, row_count, length, model = tokens.shape
    half = row_count * length
    seqs = subs * row_count
    block = model // ring_size
    width, head = input_gate.shape
    count = conv_weight.shape[0]
    split = (width // 2 + 127) // 128 * 128
    chunk = -(-(2 * head + SUMS) // (16 * ring_size)) * 16
    small_rows = chunk * ring_size

    def hops(long_way_on):
        return (middle, ring_size - 1 - middle) if long_way_on else (ring_size - 1 - middle, middle)

    token = []

    def mark(*values):
        token[:] = values

    class Gather:
        def __init__(self, shard, long_way_on):
            self.hops = hops(long_way_on)
            self.moving = [shard, shard]
            self.got = [shard] + [None] * (ring_size - 1)

        def step(self, s):
            for d, way in enumerate((onward, backward)):
                if s <= self.hops[d]:
                    self.moving[d] = lax.ppermute(self.moving[d], "dp", way)
                    self.got[ring_size - s if d == 0 else s] = self.moving[d]

    class Scatter:
        def __init__(self, term, end, long_way_on):
            self.term, self.ending = term, end
            self.hops = hops(long_way_on)
            self.moving = [None, None]
            self.own = None

        def step(self, s):
            turns, ways, fold = [], [], None
            for d in range(2):
                far = self.hops[d] - s
                if far > 0:
                    turns.append((far if d == 0 else ring_size - far, self.moving[d]))
                    ways.append(d)
                elif far == 0:
                    fold = self.moving[d]
            parts = self.term(turns, fold, tuple(token))
            if fold is not None:
                self.own = parts[len(turns) :]
            mark(parts[0])
            for d, part in zip(ways, parts):
                self.moving[d] = lax.ppermute(part, "dp", (onward, backward)[d])

        def end(self, *low):
            last = 0 if self.hops[0] > self.hops[1] else 1
            out = self.ending(low, self.own, self.moving[last], tuple(token))
            mark(out[0])
            return out

    def core_swap(other):
        return lax.ppermute(other, "mp", core_pair)

    def chip_swap(own, got, after):
        pair = pair_sum(own, got, after)
        mark(pair)
        return pair, lax.ppermute(pair, "mp", chip_pair)

    def both_halves(own, dim):
        return jnp.concatenate([own, lax.ppermute(own, "mp", core_pair)], dim)

    scalars = jnp.concatenate([core[None], row_length.reshape(-1)]).astype(jnp.int32)
    shard_one, shard_two = pack(
        split, value_weight.T, gelu_weight.T, output_weight, first_gain[None], second_gain[None]
    )
    ring_one, ring_two = Gather(shard_one, True), Gather(shard_two, False)
    ring_one.step(1)
    ring_two.step(1)

    decay_wide = decay_param.astype(F32)
    lines = jnp.concatenate(
        [
            conv_weight.astype(F32),
            jnp.stack(
                [
                    conv_bias.astype(F32),
                    input_bias.astype(F32),
                    recur_bias.astype(F32),
                    jax.nn.softplus(-decay_wide),
                    jax.nn.sigmoid(-decay_wide),
                ]
            ),
        ]
    )
    x, g, g_flat, r1, blocks_i, blocks_r = prepare(
        scalars,
        slots,
        tokens.reshape(subs, half, model),
        cotangent.reshape(subs, half, model),
        input_gate.T,
        recur_gate.T,
        (lines,),
    )
    x, *moved = lax.optimization_barrier((x, *ring_one.moving, *ring_two.moving))
    ring_one.moving, ring_two.moving = moved[:2], moved[2:]
    for s in range(2, middle + 1):
        ring_one.step(s)
        ring_two.step(s)
    one, two = ring_one.got, ring_two.got

    hop_groups = [[0, 1, ring_size - 1]] + [[s, ring_size - s] for s in range(2, middle)] + [[middle]]
    places, n1, sums_so_far = {}, [], None
    for place, offsets in enumerate(hop_groups):
        bx, by, n1_part = project(
            offsets, x, r1, [one[o] for o in offsets], [two[o] for o in offsets], sums_so_far, width, split
        )
        sums_so_far = (bx, by)
        n1.append(n1_part)
        places |= {o: (place, i) for i, o in enumerate(offsets)}

    p, cx, lx, lr, h = mixer_forward(seqs, count, bx, by, lines, blocks_i, blocks_r)
    own, other, gains = mixer_out(p, one, two, split)
    pair, other = chip_swap(own, core_swap(other), ())
    dq = unit_grad(g_flat, mlp_down, (pair,))
    h1, n2_own, r2 = norm(slots, x, gains, pair, other, (dq,))
    n2 = both_halves(n2_own, 0)
    q_a, dga_a, dup_a, n2_rel = unit_pass(0, slots, n2, mlp_gate, mlp_up, dq, ())
    unit_a = Scatter(lambda *a: unit_term(n2_rel, g, dga_a, dup_a, q_a, *a), unit_end, True)
    unit_a.step(0)
    q_b, dga_b, dup_b = unit_pass(1, slots, n2, mlp_gate, mlp_up, dq, tuple(token))
    unit_b = Scatter(lambda *a: unit_term(n2_rel, g, dga_b, dup_b, q_b, *a), unit_end, False)
    unit_b.step(0)
    last = middle - 1

    def now():
        return tuple(token)

    own, other = unit_back(owners, (dga_a, dga_b, dup_a, dup_b), mlp_gate, mlp_up, now())
    mark(own)
    got = core_swap(other)
    for s in range(1, max(last - 1, 1)):
        unit_a.step(s)
        if s == 1:
            pair, other = chip_swap(own, got, now())
        unit_b.step(s)
    unit_a.step(last - 1)
    dh1, dhr_own, second_grad = norm_back(pair, other, h1, r2, gains, g, now())
    mark(dhr_own)
    dhr = both_halves(dhr_own, 1)
    unit_b.step(last - 1)
    dbx, dby, small = mixer_backward(
        seqs, head, count, split, small_rows, dhr, two, (bx, by, cx, lx, lr, h, lines, blocks_i, blocks_r), now()
    )
    mark(dbx)
    half_split = width // 2 // 128 * 128
    mixer_a = Scatter(
        lambda *a: mixer_term(0, places, half_split, chunk, owners, n1, dhr, dbx, p, small, *a),
        lambda *a: mixer_end(0, *a),
        True,
    )
    mixer_b = Scatter(
        lambda *a: mixer_term(1, places, half_split, chunk, owners, n1, dhr, dby, p, None, *a),
        lambda *a: mixer_end(1, *a),
        False,
    )
    mixer_a.step(0)
    unit_a.step(last)
    out_own, out_other = unit_out(q_a, q_b, mlp_down, now())
    mark(out_own)
    layer_pair = pair_sum(out_own, core_swap(out_other), now())
    mark(layer_pair)
    own, other = input_out(dbx, dby, one, two, split, now())
    mark(own)
    got = core_swap(other)
    unit_b.step(last)
    pair, other = chip_swap(own, got, now())
    mixer_a.step(1)
    low = unit_a.end()
    mixer_b.step(0)
    gate_grad, up_grad, down_grad = unit_b.end(*low)
    input_own, gain_grads = input_back(slots, pair, other, x, r1, gains, dh1, second_grad, now())
    mark(input_own)
    layer_pair = relay(layer_pair, now())
    mark(layer_pair)
    layer_other = lax.ppermute(layer_pair, "mp", chip_pair)
    gain_got = core_swap(gain_grads)
    for s in range(2, middle):
        mixer_a.step(s)
        if s == middle - 1:
            both_own = finish(slots, h1, layer_pair, layer_other, input_own, now())
            mark(both_own)
        mixer_b.step(s - 1)
    input_grad, layer_out = arrange(scalars, both_own, core_swap(both_own), now())
    mark(layer_out)
    value_grad, output_low, small = mixer_a.end(gain_grads, gain_got)
    small_ring = Gather(small, True)
    small_ring.step(1)
    mark(*token, *small_ring.moving)
    mixer_b.step(last)
    for s in range(2, middle + 1):
        small_ring.step(s)
    gelu_grad, output_grad = mixer_b.end(output_low)
    gate_i, gate_r, sums, gain_grads = spread(head, block, owners, small_ring.got, now())

    return (
        layer_out.reshape(tokens.shape),
        input_grad.reshape(tokens.shape),
        gain_grads[0],
        value_grad.T,
        gelu_grad.T,
        sums[:count],
        sums[count],
        gate_i.T,
        sums[count + 1],
        gate_r.T,
        sums[count + 2],
        sums[count + 3],
        output_grad,
        gain_grads[1],
        gate_grad,
        up_grad,
        down_grad,
    )


def solution(mesh):
    placed = (
        P(None, "dp", None, None),
        P(None, "dp", None, None),
        P(None, "dp"),
        P("dp"),
        P("dp", "mp"),
        P("dp", "mp"),
        P(None, "mp"),
        P("mp"),
        P("mp", None),
        P("mp"),
        P("mp", None),
        P("mp"),
        P("mp"),
        P("mp", "dp"),
        P("dp"),
        P(None, "mp"),
        P(None, "mp"),
        P("mp", None),
    )
    return jax.shard_map(
        local,
        mesh=mesh,
        in_specs=placed,
        out_specs=(
            P(None, "dp", None, None),
            P(None, "dp", None, None),
            P("dp"),
            P("dp", "mp"),
            P("dp", "mp"),
            P(None, "mp"),
            P("mp"),
            P("mp", None),
            P("mp"),
            P("mp", None),
            P("mp"),
            P("mp"),
            P("mp", "dp"),
            P("dp"),
            P("dp", "mp"),
            P("dp", "mp"),
            P("mp", "dp"),
        ),
        check_vma=False,
    )
```

```python
import jax
import jax.numpy as jnp
from jax import lax
from jax.experimental import pallas as pl
from jax.experimental.pallas import tpu as pltpu
from jax.sharding import PartitionSpec as P

EPSILON = 1e-06
DECAY_SCALE = 8.0
GELU_A = 0.7978845608028654
GELU_B = 0.044715
BF16 = jnp.bfloat16
F32 = jnp.float32
STEP = 16
HALF = 8
SUMS = 8
HEAVY = 100 * 10**9
END_WEIGHT = 1
TN = (((0,), (0,)), ((), ()))
NT = (((1,), (1,)), ((), ()))


def gelu(v):
    return 0.5 * v * (1.0 + jnp.tanh(GELU_A * (v + GELU_B * v * v * v)))


def gelu_both(v):
    squared = v * v
    bent = jnp.tanh(GELU_A * v * (1.0 + GELU_B * squared))
    value = 0.5 * v * (1.0 + bent)
    slope = 0.5 * (1.0 + bent) + 0.5 * v * (1.0 - bent * bent) * GELU_A * (
        1.0 + 3.0 * GELU_B * squared
    )
    return value, slope


def negative_expm1(z, exp_z):
    series = 1.0 + z * (1.0 / 7.0)
    for k in (6.0, 5.0, 4.0, 3.0, 2.0):
        series = 1.0 + z * (1.0 / k) * series
    return jnp.where(z > -0.25, -z * series, 1.0 - exp_z)


def rows_of(shape):
    return lax.broadcasted_iota(jnp.int32, shape, 0)


def earlier(now, before, k, rows):
    return jnp.where(rows < k, pltpu.roll(before, k, 0), pltpu.roll(now, k, 0))


def later(now, after, k, rows):
    size = now.shape[0]
    return jnp.where(
        rows >= size - k, pltpu.roll(after, size - k, 0), pltpu.roll(now, size - k, 0)
    )


def shaped(shape, dtype):
    return jax.ShapeDtypeStruct(shape, dtype)


def launch(
    kernel, inputs, out_shape, name, scalars=0, after=(), mib=20, scratch=(), aliases=None, grid=None, flops=1
):
    count, extra = len(inputs), len(after)
    waits = [pl.BlockSpec(memory_space=pl.ANY)] * extra
    in_specs = [pl.BlockSpec(memory_space=pltpu.SMEM)] * scalars
    more = {}
    if grid is None:
        in_specs += [pl.BlockSpec(memory_space=pltpu.VMEM)] * (count - scalars)
    else:
        in_specs += grid[1]
        more = {"grid": grid[0], "out_specs": grid[2]}
    return pl.pallas_call(
        lambda *refs: kernel(*refs[:count], *refs[count + extra :]),
        in_specs=in_specs + waits,
        out_shape=out_shape,
        scratch_shapes=list(scratch),
        input_output_aliases=aliases or {},
        compiler_params=pltpu.CompilerParams(vmem_limit_bytes=mib << 20),
        cost_estimate=pl.CostEstimate(flops=flops, bytes_accessed=1, transcendentals=0),
        name=name,
        **more,
    )(*inputs, *after)


def in_hbm(array):
    return pltpu.with_memory_space_constraint(array, pltpu.HBM)


def mixer_forward_kernel(
    seqs, count, bx, by, lines, blocks_i, blocks_r, p_o, cx_o, lx_o, lr_o, h_o
):
    total, width = bx.shape
    length = total // seqs
    steps = length // STEP
    rows16 = rows_of((STEP, width))
    w = [jnp.broadcast_to(lines[k : k + 1, :], (STEP, width)) for k in range(count)]
    shift = jnp.broadcast_to(lines[count : count + 1, :], (STEP, width))
    bias_i, bias_r = lines[count + 1 : count + 2, :], lines[count + 2 : count + 3, :]
    soft = lines[count + 3 : count + 4, :]
    for seq in range(seqs):

        def conv(i, before):
            at = pl.ds(pl.multiple_of(seq * length + i * STEP, STEP), STEP)
            now = bx[at, :]
            mixed = shift + w[0] * now
            for k in range(1, count):
                mixed = mixed + w[k] * earlier(now, before, k, rows16)
            cx_o[at, :] = mixed.astype(BF16)
            return now

        lax.fori_loop(0, steps, conv, jnp.zeros((STEP, width), F32))
    lx_o[...] = lax.dot_general(cx_o[...], blocks_i[...], NT, preferred_element_type=F32) + bias_i
    lr_o[...] = lax.dot_general(cx_o[...], blocks_r[...], NT, preferred_element_type=F32) + bias_r
    rows8 = rows_of((HALF, width))
    soft8 = jnp.broadcast_to(-DECAY_SCALE * soft, (HALF, width))

    def scan(i, carries):
        out = []
        for seq in range(seqs):
            carry = carries[seq]
            base = seq * length + i * STEP
            at = pl.ds(pl.multiple_of(base, STEP), STEP)
            cx16 = cx_o[at, :].astype(F32)
            products = []
            for part in range(STEP // HALF):
                here = pl.ds(pl.multiple_of(base + part * HALF, HALF), HALF)
                cx = cx16[part * HALF : (part + 1) * HALF, :]
                ix = jax.nn.sigmoid(lx_o[here, :])
                la = soft8 * jax.nn.sigmoid(lr_o[here, :])
                a = jnp.exp(la)
                rest = negative_expm1(2.0 * la, a * a)
                m = jnp.where(rest > 0.0, rest * lax.rsqrt(rest), 0.0)
                u = m * ix * cx
                for s in (1, 2, 4):
                    keep = rows8 >= s
                    u = u + jnp.where(keep, a * pltpu.roll(u, s, 0), 0.0)
                    a = jnp.where(keep, a * pltpu.roll(a, s, 0), a)
                h = u + a * carry
                carry = jnp.broadcast_to(h[HALF - 1 : HALF, :], (HALF, width))
                h_o[here, :] = h
                products.append(h * gelu(by[here, :]))
            p_o[at, :] = jnp.concatenate(products, 0).astype(BF16)
            out.append(carry)
        return tuple(out)

    lax.fori_loop(0, steps, scan, tuple(jnp.zeros((HALF, width), F32) for _ in range(seqs)))


def mixer_forward(seqs, count, bx, by, lines, blocks_i, blocks_r):
    low, full = shaped(bx.shape, BF16), shaped(bx.shape, F32)
    return launch(
        lambda *refs: mixer_forward_kernel(seqs, count, *refs),
        (bx, by, lines, blocks_i, blocks_r),
        (low, low, full, full, full),
        "mixer_forward",
    )


def mixer_backward_kernel(seqs, head, count, split, dhr, *refs):
    ring_size = dhr.shape[0]
    second = refs[:ring_size]
    bx, by, cx_i, lx_i, lr_i, h_i, lines, blocks_i, blocks_r = refs[ring_size : ring_size + 9]
    dbx_o, dby_o, small_o, dlx_o, dlr_o, dcx_s, dp = refs[ring_size + 9 :]
    skip = bx.shape[1] - split
    soft, gate_soft = lines[count + 3 : count + 4, :], lines[count + 4 : count + 5, :]
    for o in range(ring_size):
        part = lax.dot_general(dhr[o], second[o][skip:, :], NT, preferred_element_type=F32)
        dp[...] = part if o == 0 else dp[...] + part
    total, width = bx.shape
    length = total // seqs
    steps = length // STEP
    rows8 = rows_of((HALF, width))
    soft8 = jnp.broadcast_to(-DECAY_SCALE * soft, (HALF, width))
    zero = jnp.zeros((HALF, width), F32)

    def scan(j, state):
        i = steps - 1 - j
        sums_i, sums_r, sums_d = state[0]
        out = []
        for seq in range(seqs):
            a_after, e_after = state[1][seq]
            base = seq * length + i * STEP
            at = pl.ds(pl.multiple_of(base, STEP), STEP)
            cx16 = cx_i[at, :].astype(F32)
            dby_parts, dlx_parts, dlr_parts = [None, None], [None, None], [None, None]
            for part in (1, 0):
                start = base + part * HALF
                here = pl.ds(pl.multiple_of(start, HALF), HALF)
                cx = cx16[part * HALF : (part + 1) * HALF, :]
                ix = jax.nn.sigmoid(lx_i[here, :])
                ra = jax.nn.sigmoid(lr_i[here, :])
                la = soft8 * ra
                a = jnp.exp(la)
                rest = negative_expm1(2.0 * la, a * a)
                inverse = lax.rsqrt(rest)
                m = rest * inverse
                h = h_i[here, :]
                first = (i == 0) if part == 0 else False
                back = jnp.maximum(start - HALF, 0)
                before = h_i[pl.ds(pl.multiple_of(back, HALF), HALF), :]
                if part == 0:
                    before = jnp.where(i == 0, 0.0, before)
                h_prev = earlier(h, before, 1, rows8)
                gy, slope = gelu_both(by[here, :])
                grad = dp[here, :]
                dby_parts[part] = grad * h * slope
                e = grad * gy
                f = later(a, a_after, 1, rows8)
                for s in (1, 2, 4):
                    keep = rows8 < HALF - s
                    e = e + jnp.where(keep, f * pltpu.roll(e, HALF - s, 0), 0.0)
                    f = jnp.where(keep, f * pltpu.roll(f, HALF - s, 0), f)
                e = e + f * e_after
                e_after = jnp.broadcast_to(e[0:1, :], (HALF, width))
                a_after = a
                eix = e * ix
                dla = (e * h_prev - eix * cx * a * inverse) * a
                dlx = eix * m * cx * (1.0 - ix)
                dlr = dla * la * (1.0 - ra)
                sums_i = sums_i + dlx
                sums_r = sums_r + dlr
                sums_d = sums_d + dla * ra
                dlx_parts[part], dlr_parts[part] = dlx, dlr
                dcx_s[here, :] = eix * m
            dby_o[at, :] = jnp.concatenate(dby_parts, 0).astype(BF16)
            dlx_o[at, :] = jnp.concatenate(dlx_parts, 0).astype(BF16)
            dlr_o[at, :] = jnp.concatenate(dlr_parts, 0).astype(BF16)
            out.append((a_after, e_after))
        return (sums_i, sums_r, sums_d), tuple(out)

    (sums_i, sums_r, sums_d), _ = lax.fori_loop(
        0, steps, scan, ((zero, zero, zero), tuple((zero, zero) for _ in range(seqs)))
    )
    dcx_s[...] += jnp.dot(dlx_o[...], blocks_i[...], preferred_element_type=F32) + jnp.dot(
        dlr_o[...], blocks_r[...], preferred_element_type=F32
    )
    rows16 = rows_of((STEP, width))
    w = [jnp.broadcast_to(lines[k : k + 1, :], (STEP, width)) for k in range(count)]
    zero16 = jnp.zeros((STEP, width), F32)
    sums_t = tuple(zero16 for _ in range(count))
    sums_b = zero16
    for seq in range(seqs):

        def conv(j, state):
            after, tap_sums, shift_sum = state
            at = pl.ds(pl.multiple_of(seq * length + (steps - 1 - j) * STEP, STEP), STEP)
            now = dcx_s[at, :]
            source = bx[at, :]
            grad = w[0] * now
            new_sums = [tap_sums[0] + now * source]
            for k in range(1, count):
                moved = later(now, after, k, rows16)
                grad = grad + w[k] * moved
                new_sums.append(tap_sums[k] + moved * source)
            dbx_o[at, :] = grad.astype(BF16)
            return now, tuple(new_sums), shift_sum + now

        _, sums_t, sums_b = lax.fori_loop(0, steps, conv, (zero16, sums_t, sums_b))
    rows = [jnp.sum(item, 0, keepdims=True) for item in (*sums_t, sums_b, sums_i, sums_r)]
    rows.append(DECAY_SCALE * gate_soft * jnp.sum(sums_d, 0, keepdims=True))
    spare = small_o.shape[0] - 2 * head - SUMS
    if spare:
        rows.append(jnp.zeros((spare, width), F32))
    small_o[2 * head :, :] = jnp.concatenate(rows, 0).astype(BF16)
    lanes = lax.broadcasted_iota(jnp.int32, (head, width), 1)
    for gate, grads in enumerate((dlx_o, dlr_o)):
        whole = lax.dot_general(grads[...], cx_i[...], TN, preferred_element_type=F32)
        picked = whole[:head]
        for i in range(1, width // head):
            picked = jnp.where(lanes < i * head, picked, whole[i * head : (i + 1) * head])
        small_o[gate * head : (gate + 1) * head, :] = picked.astype(BF16)


def mixer_backward(seqs, head, count, split, small_rows, dhr, second, saved, after):
    total, width = saved[0].shape
    low = shaped((total, width), BF16)
    return launch(
        lambda *refs: mixer_backward_kernel(seqs, head, count, split, *refs),
        (dhr, *second, *saved),
        (low, low, shaped((small_rows, width), BF16)),
        "mixer_backward",
        after=after,
        mib=32,
        scratch=[
            pltpu.VMEM((total, width), BF16),
            pltpu.VMEM((total, width), BF16),
            pltpu.VMEM((total, width), F32),
            pltpu.VMEM((total, width), F32),
        ],
    )


def pack_kernel(split, gain_one, gain_two, value, gelu_w, output, one_o, two_o, sems):
    width = value.shape[0]
    copies = [
        pltpu.make_async_copy(source, target, sems.at[i])
        for i, (source, target) in enumerate(
            (
                (value, one_o.at[pl.ds(0, width)]),
                (gelu_w.at[pl.ds(0, split)], one_o.at[pl.ds(width + 16, split)]),
                (gelu_w.at[pl.ds(split, width - split)], two_o.at[pl.ds(0, width - split)]),
                (output, two_o.at[pl.ds(width - split, width)]),
            )
        )
    ]
    for copy in copies:
        copy.start()
    spare = jnp.zeros((14, value.shape[1]), F32)
    lines = jnp.concatenate([gain_one[...].astype(F32), gain_two[...].astype(F32), spare], 0)
    one_o[width : width + 16, :] = lines.astype(BF16)
    for copy in copies:
        copy.wait()


def pack(split, value, gelu_w, output, gain_one, gain_two):
    width, block = value.shape
    whole = pl.BlockSpec(memory_space=pltpu.VMEM)
    anywhere = pl.BlockSpec(memory_space=pl.ANY)
    return launch(
        lambda *refs: pack_kernel(split, *refs),
        (gain_one, gain_two, in_hbm(value), in_hbm(gelu_w), in_hbm(output)),
        (shaped((width + 16 + split, block), BF16), shaped((2 * width - split, block), BF16)),
        "pack",
        scratch=[pltpu.SemaphoreType.DMA((4,))],
        grid=((), [whole, whole, anywhere, anywhere, anywhere], [whole, whole]),
    )


def prepare_kernel(scalars, slots, tokens, cotangent, gate_i, gate_r, x_o, g_o, flat_o, r_o, blocks_i, blocks_r):
    ring_size, total, block = x_o.shape
    half = total // 2
    row_count = (scalars.shape[0] - 1) // 2
    length = half // row_count
    rows = lax.broadcasted_iota(jnp.int32, (length, block), 0)
    for place in range(2):
        sub = scalars[0] if place == 0 else 1 - scalars[0]
        for row in range(row_count):
            at = slice(place * half + row * length, place * half + (row + 1) * length)
            source = pl.ds(row * length, length)
            valid = jnp.where(rows < scalars[1 + sub * row_count + row], 1.0, 0.0)
            squares = jnp.zeros((length, block), F32)
            for k in range(ring_size):
                columns = slice(k * block, (k + 1) * block)
                piece = tokens[sub, source, columns]
                wide = piece.astype(F32)
                squares = squares + wide * wide
                x_o[slots[k], at, :] = piece
                masked = (cotangent[sub, source, columns].astype(F32) * valid).astype(BF16)
                g_o[slots[k], at, :] = masked
                flat_o[at, columns] = masked
            mean = jnp.sum(squares, 1, keepdims=True) * (1.0 / (ring_size * block))
            r_o[at, :] = lax.rsqrt(mean + EPSILON)
    head, width = gate_i.shape
    lanes = lax.broadcasted_iota(jnp.int32, (head, width), 1)
    for source, out in ((gate_i, blocks_i), (gate_r, blocks_r)):
        wide = source[...].astype(F32)
        for i in range(width // head):
            inside = (lanes >= i * head) & (lanes < (i + 1) * head)
            out[i * head : (i + 1) * head, :] = jnp.where(inside, wide, 0.0).astype(BF16)


def prepare(scalars, slots, tokens, cotangent, gate_i, gate_r, after):
    subs, half, model = tokens.shape
    total, ring_size, width = subs * half, slots.shape[0], gate_i.shape[1]
    rel = shaped((ring_size, total, model // ring_size), BF16)
    blocks = shaped((width, width), BF16)
    return launch(
        prepare_kernel,
        (scalars, slots, tokens, cotangent, gate_i, gate_r),
        (rel, rel, shaped((total, model), BF16), shaped((total, 1), F32), blocks, blocks),
        "prepare",
        scalars=2,
        after=after,
    )


def project_kernel(offsets, first, width, split, x, r1, *refs):
    count = len(offsets)
    one, two = refs[:count], refs[count : 2 * count]
    rest = refs[2 * count :]
    if not first:
        before = rest[:2]
        rest = rest[2:]
    bx, by, n1_o = rest
    scale = r1[...]
    for i, o in enumerate(offsets):
        gain = one[i][width : width + 16, :].astype(F32)[0:1, :]
        n1 = (x[o].astype(F32) * scale * gain).astype(BF16)
        n1_o[i] = n1
        for out, place, columns, weight in (
            (bx, 0, slice(0, width), one[i][:width, :]),
            (by, 1, slice(0, split), one[i][width + 16 :, :]),
            (by, 1, slice(split, width), two[i][: width - split, :]),
        ):
            part = lax.dot_general(n1, weight, NT, preferred_element_type=F32)
            if i > 0:
                out[:, columns] += part
            elif first:
                out[:, columns] = part
            else:
                out[:, columns] = before[place][:, columns] + part


def project(offsets, x, r1, one, two, before, width, split):
    total, block = x.shape[1:]
    count = len(offsets)
    full = shaped((total, width), F32)
    at = 2 + 2 * count
    return launch(
        lambda *refs: project_kernel(offsets, before is None, width, split, *refs),
        (x, r1, *one, *two, *(before or ())),
        (full, full, shaped((count, total, block), BF16)),
        "project",
        aliases={} if before is None else {at: 0, at + 1: 1},
    )


def mixer_out_kernel(skip, p, *refs):
    own_o, other_o, gains_o = refs[-3:]
    count, half = own_o.shape[:2]
    width = p.shape[1]
    for o in range(count):
        part = jnp.dot(p[...], refs[count + o][skip:, :], preferred_element_type=F32)
        own_o[o] = part[:half]
        other_o[o] = part[half:].astype(BF16)
        gains_o[o] = refs[o][width : width + 16, :].astype(F32)[0:2, :]


def mixer_out(p, one, two, split):
    total, width = p.shape
    count, block = len(one), one[0].shape[1]
    shape = (count, total // 2, block)
    return launch(
        lambda *refs: mixer_out_kernel(width - split, *refs),
        (p, *one, *two),
        (shaped(shape, F32), shaped(shape, BF16), shaped((count, 2, block), F32)),
        "mixer_out",
        mib=24,
    )


def input_out_kernel(split, dbx, dby, *refs):
    own_o, other_o = refs[-2:]
    count, half = own_o.shape[:2]
    width = dbx.shape[1]
    for o in range(count):
        one, two = refs[o], refs[count + o]
        part = (
            jnp.dot(dbx[...], one[:width, :], preferred_element_type=F32)
            + jnp.dot(dby[:, :split], one[width + 16 :, :], preferred_element_type=F32)
            + jnp.dot(dby[:, split:], two[: width - split, :], preferred_element_type=F32)
        )
        own_o[o] = part[:half]
        other_o[o] = part[half:].astype(BF16)


def input_out(dbx, dby, one, two, split, after):
    shape = (len(one), dbx.shape[0] // 2, one[0].shape[1])
    return launch(
        lambda *refs: input_out_kernel(split, *refs),
        (dbx, dby, *one, *two),
        (shaped(shape, F32), shaped(shape, BF16)),
        "input_out",
        after=after,
        mib=24,
    )


def pair_kernel(own, got, out):
    out[...] = (own[...] + got[...].astype(F32)).astype(BF16)


def pair_sum(own, got, after):
    return launch(pair_kernel, (own, got), shaped(own.shape, BF16), "pair_sum", after=after)


def relay_kernel(source, out):
    out[...] = source[...]


def relay(source, after):
    return launch(relay_kernel, (source,), shaped(source.shape, source.dtype), "relay", after=after)


def norm_kernel(slots, x, gains, pair, other, h_o, n_o, r_o):
    ring_size, half, block = h_o.shape
    squares = jnp.zeros((half, block), F32)
    for o in range(ring_size):
        h = x[o, 0:half, :].astype(F32) + (pair[o].astype(F32) + other[o].astype(F32))
        h_o[o] = h
        squares = squares + h * h
    mean = jnp.sum(squares, 1, keepdims=True) * (1.0 / (ring_size * block))
    scale = lax.rsqrt(mean + EPSILON)
    r_o[...] = scale
    for k in range(ring_size):
        o = slots[k]
        n_o[:, k * block : (k + 1) * block] = (h_o[o] * scale * gains[o, 1:2, :]).astype(BF16)


def norm(slots, x, gains, pair, other, after):
    ring_size, half, block = pair.shape
    return launch(
        norm_kernel,
        (slots, x, gains, pair, other),
        (shaped(pair.shape, F32), shaped((half, ring_size * block), BF16), shaped((half, 1), F32)),
        "norm",
        scalars=1,
        after=after,
    )


def norm_back_kernel(pair, other, h1, r2, gains, g, dh_o, dhr_o, grad_o):
    ring_size, half, block = h1.shape
    dots = jnp.zeros((half, block), F32)
    scale = r2[...]
    for o in range(ring_size):
        product = (pair[o].astype(F32) + other[o].astype(F32)) * h1[o]
        dots = dots + product * gains[o, 1:2, :]
        grad_o[o] = jnp.sum(product * scale, 0, keepdims=True)
    mean = jnp.sum(dots, 1, keepdims=True) * (1.0 / (ring_size * block))
    bend = scale * scale * scale * mean
    for o in range(ring_size):
        grad = pair[o].astype(F32) + other[o].astype(F32)
        dh = g[o, 0:half, :].astype(F32) + scale * (grad * gains[o, 1:2, :]) - h1[o] * bend
        dh_o[o] = dh
        dhr_o[o] = dh.astype(BF16)


def norm_back(pair, other, h1, r2, gains, g, after):
    ring_size, half, block = pair.shape
    return launch(
        norm_back_kernel,
        (pair, other, h1, r2, gains, g),
        (shaped(pair.shape, F32), shaped(pair.shape, BF16), shaped((ring_size, 1, block), F32)),
        "norm_back",
        after=after,
    )


def input_back_kernel(slots, pair, other, x, r1, gains, dh1, second, out_o, grad_o):
    ring_size, half, block = dh1.shape
    dots = jnp.zeros((half, block), F32)
    scale = r1[0:half, :]
    for o in range(ring_size):
        product = (pair[o].astype(F32) + other[o].astype(F32)) * x[o, 0:half, :].astype(F32)
        dots = dots + product * gains[o, 0:1, :]
        grad_o[o, 0:1, :] = jnp.sum(product * scale, 0, keepdims=True)
        grad_o[o, 1:2, :] = second[o]
    mean = jnp.sum(dots, 1, keepdims=True) * (1.0 / (ring_size * block))
    bend = scale * scale * scale * mean
    for k in range(ring_size):
        o = slots[k]
        grad = pair[o].astype(F32) + other[o].astype(F32)
        out_o[:, k * block : (k + 1) * block] = (
            dh1[o] + scale * (grad * gains[o, 0:1, :]) - x[o, 0:half, :].astype(F32) * bend
        )


def input_back(slots, pair, other, x, r1, gains, dh1, second, after):
    ring_size, half, block = pair.shape
    return launch(
        input_back_kernel,
        (slots, pair, other, x, r1, gains, dh1, second),
        (shaped((half, ring_size * block), F32), shaped((ring_size, 2, block), F32)),
        "input_back",
        scalars=1,
        after=after,
    )


def finish_kernel(slots, h1, pair, other, beside, out_o):
    ring_size, half, block = h1.shape
    out_o[0] = beside[...]
    for k in range(ring_size):
        columns = slice(k * block, (k + 1) * block)
        summed = pair[:, columns].astype(F32) + other[:, columns].astype(F32)
        out_o[1, :, columns] = h1[slots[k]] + summed


def finish(slots, h1, pair, other, beside, after):
    return launch(
        finish_kernel,
        (slots, h1, pair, other, beside),
        shaped((2, *beside.shape), F32),
        "finish",
        scalars=1,
        after=after,
        mib=24,
    )


def arrange_kernel(scalars, own, got, *outs):
    core = scalars[0]
    for i, out in enumerate(outs):
        out[core] = own[i]
        out[1 - core] = got[i]


def arrange(scalars, own, got, after):
    out = shaped((2, *own.shape[1:]), own.dtype)
    return launch(
        arrange_kernel, (scalars, own, got), (out,) * own.shape[0], "arrange", scalars=1, after=after, mib=24
    )


def unit_grad_kernel(g, down, dq_o):
    dq_o[...] = lax.dot_general(g[...], down[...], NT, preferred_element_type=F32)


def unit_grad(g, down, after):
    total, model = g.shape
    units = down.shape[0]
    tile = 256
    grid = (
        (units // tile,),
        [pl.BlockSpec((total, model), lambda i: (0, 0)), pl.BlockSpec((tile, model), lambda i: (i, 0))],
        pl.BlockSpec((total, tile), lambda i: (0, i)),
    )
    return launch(unit_grad_kernel, (g, in_hbm(down)), shaped((total, units), F32), "unit_grad", after=after, grid=grid)


def fetch_kernel(gate, up, gate_o, up_o, sems):
    columns = pl.ds(0, gate_o.shape[1])
    copies = [
        pltpu.make_async_copy(source.at[:, columns], target, sems.at[i])
        for i, (source, target) in enumerate(((gate, gate_o), (up, up_o)))
    ]
    for copy in copies:
        copy.start()
    for copy in copies:
        copy.wait()


def fetch(gate, up, after):
    model, units = gate.shape
    whole = pl.BlockSpec(memory_space=pltpu.VMEM)
    anywhere = pl.BlockSpec(memory_space=pl.ANY)
    half = shaped((model, units // 2), BF16)
    return launch(
        fetch_kernel,
        (in_hbm(gate), in_hbm(up)),
        (half, half),
        "fetch",
        after=after,
        scratch=[pltpu.SemaphoreType.DMA((2,))],
        grid=((), [anywhere, anywhere], [whole, whole]),
    )


def unit_products(ga, upward, grad):
    value, slope = gelu_both(ga)
    return value * upward, grad * upward * slope, grad * value


def unit_first_kernel(slots, n2, gate, up, dq, q_o, dga_o, dup_o, rel_o):
    ring_size, total, block = rel_o.shape
    tile = 256
    for i in range(0, gate.shape[1], tile):
        columns = slice(i, i + tile)
        ga = jnp.dot(n2[...], gate[:, columns], preferred_element_type=F32)
        upward = jnp.dot(n2[...], up[:, columns], preferred_element_type=F32)
        for out, item in zip((q_o, dga_o, dup_o), unit_products(ga, upward, dq[:, columns])):
            out[:, columns] = item.astype(BF16)
    for k in range(ring_size):
        rel_o[slots[k]] = n2[:, k * block : (k + 1) * block]


def unit_first(slots, n2, gate, up, dq):
    total, model = n2.shape
    ring_size = slots.shape[0]
    out = shaped((total, gate.shape[1]), BF16)
    return launch(
        unit_first_kernel,
        (slots, n2, gate, up, dq),
        (out, out, out, shaped((ring_size, total, model // ring_size), BF16)),
        "unit_first",
        scalars=1,
        mib=28,
    )


def unit_kernel(n2, gate, up, dq, q_o, dga_o, dup_o):
    ga = jnp.dot(n2[...], gate[...], preferred_element_type=F32)
    upward = jnp.dot(n2[...], up[...], preferred_element_type=F32)
    for out, item in zip((q_o, dga_o, dup_o), unit_products(ga, upward, dq[...])):
        out[...] = item.astype(BF16)


def unit_second(n2, gate, up, dq, after):
    total, model = n2.shape
    share = gate.shape[1] // 2
    tile = 256
    first = share // tile
    wide = pl.BlockSpec((total, tile), lambda i: (0, i))
    tall = pl.BlockSpec((model, tile), lambda i: (0, i + first))
    out = shaped((total, share), BF16)
    grid = (
        (share // tile,),
        [
            pl.BlockSpec((total, model), lambda i: (0, 0)),
            tall,
            tall,
            pl.BlockSpec((total, tile), lambda i: (0, i + first)),
        ],
        [wide, wide, wide],
    )
    return launch(
        unit_kernel,
        (n2, in_hbm(gate), in_hbm(up), dq),
        (out, out, out),
        "unit_second",
        after=after,
        mib=28,
        grid=grid,
    )


def unit_out_kernel(q_a, q_b, down, own_o, other_o):
    half = own_o.shape[0]
    share = q_a.shape[1]
    part = jnp.dot(q_a[...], down[:share, :], preferred_element_type=F32)
    part = part + jnp.dot(q_b[...], down[share:, :], preferred_element_type=F32)
    own_o[...] = part[:half]
    other_o[...] = part[half:].astype(BF16)


def unit_out(q_a, q_b, down, after):
    total, share = q_a.shape
    units, model = down.shape
    half = total // 2
    tile = 256
    out = pl.BlockSpec((half, tile), lambda i: (0, i))
    left = pl.BlockSpec((total, share), lambda i: (0, 0))
    grid = ((model // tile,), [left, left, pl.BlockSpec((units, tile), lambda i: (0, i))], [out, out])
    return launch(
        unit_out_kernel,
        (q_a, q_b, in_hbm(down)),
        (shaped((half, model), F32), shaped((half, model), BF16)),
        "unit_out",
        after=after,
        grid=grid,
    )


def unit_back_kernel(owners, dga_a, dga_b, dup_a, dup_b, gate, up, *refs):
    own_o, other_o = refs[-2:]
    half = other_o.shape[1]
    share = dga_a.shape[1]
    part = None
    for left, right in (
        (dga_a, gate[:, :share]),
        (dga_b, gate[:, share:]),
        (dup_a, up[:, :share]),
        (dup_b, up[:, share:]),
    ):
        term = lax.dot_general(left[...], right, NT, preferred_element_type=F32)
        part = term if part is None else part + term
    own_o[0] = part[:half]
    other_o[0] = part[half:].astype(BF16)


def unit_back(owners, grads, gate, up, after):
    ring_size = owners.shape[0]
    total, share = grads[0].shape
    model, units = gate.shape
    half = total // 2
    block = model // ring_size
    left = pl.BlockSpec((total, share), lambda o, owners: (0, 0))
    weight = pl.BlockSpec((block, units), lambda o, owners: (owners[o], 0))
    out = pl.BlockSpec((1, half, block), lambda o, owners: (o, 0, 0))
    return pl.pallas_call(
        unit_back_kernel,
        grid_spec=pltpu.PrefetchScalarGridSpec(
            num_scalar_prefetch=1,
            grid=(ring_size,),
            in_specs=[left] * 4 + [weight, weight, *[pl.BlockSpec(memory_space=pl.ANY)] * len(after)],
            out_specs=[out, out],
        ),
        out_shape=(shaped((ring_size, half, block), F32), shaped((ring_size, half, block), BF16)),
        compiler_params=pltpu.CompilerParams(vmem_limit_bytes=24 << 20),
        cost_estimate=pl.CostEstimate(flops=1, bytes_accessed=1, transcendentals=0),
        name="unit_back",
    )(owners, *grads, in_hbm(gate), in_hbm(up), *after)


def unit_term_kernel(turns, fold, n2, g, dga, dup, q, *refs):
    share = q.shape[1]
    rest = list(refs)
    outs = rest[len(rest) - len(turns) - (3 if fold else 0) :]
    parts = [slice(i * share, (i + 1) * share) for i in range(3)]

    def terms(o):
        return (
            lax.dot_general(n2[o], dga[...], TN, preferred_element_type=F32),
            lax.dot_general(n2[o], dup[...], TN, preferred_element_type=F32),
        )

    for (o, has), out in zip(turns, outs):
        recv = rest.pop(0) if has else None
        down = lax.dot_general(g[o], q[...], TN, preferred_element_type=F32)
        for grad, columns in zip((*terms(o), down), parts):
            if recv is not None:
                grad = grad + recv[:, columns].astype(F32)
            out[:, columns] = grad.astype(BF16)
    if fold:
        recv = rest.pop(0)
        gate_o, up_o, down_o = outs[len(turns) :]
        for grad, columns, out in zip(terms(0), parts, (gate_o, up_o)):
            out[...] = grad + recv[:, columns].astype(F32)
        down = lax.dot_general(q[...], g[0], TN, preferred_element_type=F32)
        down_o[...] = down + recv[:, parts[2]].astype(F32).T


def unit_term(n2, g, dga, dup, q, turns, fold, after, weight):
    block, share = n2.shape[2], q.shape[1]
    arrived = [item for _, item in turns if item is not None] + ([] if fold is None else [fold])
    plan = [(o, item is not None) for o, item in turns]
    out = [shaped((block, 3 * share), BF16) for _ in turns]
    if fold is not None:
        out += [shaped((block, share), F32), shaped((block, share), F32), shaped((share, block), F32)]
    return launch(
        lambda *refs: unit_term_kernel(plan, fold is not None, *refs),
        (n2, g, dga, dup, q, *arrived),
        tuple(out),
        "unit_term",
        after=after,
        mib=24,
        flops=weight,
    )


def unit_end_kernel(count, *refs):
    own, item, low, outs = refs[:3], refs[3], refs[4 : 4 + count], refs[4 + count :]
    share = own[0].shape[1]
    for i in range(2):
        total = own[i][...] + item[:, i * share : (i + 1) * share].astype(F32)
        if count:
            outs[i][:, :share] = low[i][...]
            outs[i][:, share:] = total
        else:
            outs[i][...] = total
    total = own[2][...] + item[:, 2 * share :].astype(F32).T
    if count:
        outs[2][:share, :] = low[2][...]
        outs[2][share:, :] = total
    else:
        outs[2][...] = total


def unit_end(low, own, item, after):
    block, share = own[0].shape
    wide = 2 if low else 1
    grad = shaped((block, wide * share), F32)
    return launch(
        lambda *refs: unit_end_kernel(len(low), *refs),
        (*own, item, *low),
        (grad, grad, shaped((wide * share, block), F32)),
        "unit_end",
        after=after,
        flops=END_WEIGHT,
    )


def small_pieces(width, block):
    return [slice(i, min(i + block, width)) for i in range(0, width, block)]


def mixer_term_kernel(part, places, groups, split, chunk, turns, fold, owners, *refs):
    n1_all = refs[:groups]
    dhr, grads, p = refs[groups : groups + 3]
    rest = list(refs[groups + 3 :])
    extra = rest.pop(0) if part == 0 else None
    outs = rest[len(rest) - len(turns) - (3 - part if fold else 0) :]
    width, block = grads.shape[1], dhr.shape[2]
    columns = slice(0, split) if part == 0 else slice(split, width)
    size = columns.stop - columns.start
    at = width + size
    pieces = small_pieces(width, block)

    def terms(o, recv):
        group, i = places[o]
        grad = lax.dot_general(grads[...], n1_all[group][i], TN, preferred_element_type=F32)
        out = lax.dot_general(p[:, columns], dhr[o], TN, preferred_element_type=F32)
        if recv is not None:
            grad = grad + recv[:width, :].astype(F32)
            out = out + recv[width:at, :].astype(F32)
        return grad, out

    def small(o, recv):
        own = extra[pl.ds(pl.multiple_of(owners[o] * chunk, 16), chunk), :].astype(F32)
        out = []
        for i, piece in enumerate(pieces):
            total = own[:, piece]
            if recv is not None:
                total = total + recv[at + i * chunk : at + (i + 1) * chunk, : piece.stop - piece.start].astype(F32)
            out.append(total)
        return out

    for (o, has), out_ref in zip(turns, outs):
        recv = rest.pop(0) if has else None
        grad, out = terms(o, recv)
        out_ref[:width, :] = grad.astype(BF16)
        out_ref[width:at, :] = out.astype(BF16)
        if part == 0:
            for i, total in enumerate(small(o, recv)):
                rows = slice(at + i * chunk, at + (i + 1) * chunk)
                wide = total.shape[1]
                out_ref[rows, :wide] = total.astype(BF16)
                if wide < block:
                    out_ref[rows, wide:] = jnp.zeros((chunk, block - wide), BF16)
    if fold:
        recv = rest.pop(0)
        outs[len(turns)][...], outs[len(turns) + 1][...] = terms(0, recv)
        if part == 0:
            for piece, total in zip(pieces, small(0, recv)):
                outs[len(turns) + 2][:, piece] = total


def mixer_term(part, places, split, chunk, owners, n1, dhr, grads, p, extra, turns, fold, after, weight):
    block, width = dhr.shape[2], grads.shape[1]
    size = split if part == 0 else width - split
    arrived = [item for _, item in turns if item is not None] + ([] if fold is None else [fold])
    more = 0 if part == 1 else chunk * len(small_pieces(width, block))
    out = [shaped((width + size + more, block), BF16) for _ in turns]
    if fold is not None:
        out += [shaped((width, block), F32), shaped((size, block), F32)]
        out += [shaped((chunk, width), F32)] if part == 0 else []
    plan = [(o, item is not None) for o, item in turns]
    return launch(
        lambda *refs: mixer_term_kernel(part, places, len(n1), split, chunk, plan, fold is not None, *refs),
        (owners, *n1, dhr, grads, p, *([extra] if part == 0 else []), *arrived),
        tuple(out),
        "mixer_term",
        scalars=1,
        after=after,
        mib=24,
        flops=weight,
    )


def mixer_end_kernel(part, *refs):
    own, item = refs[: 3 - part], refs[3 - part]
    extra, outs = refs[4 - part : 6 - 2 * part], refs[6 - 2 * part :]
    width, block = own[0].shape
    at = width + own[1].shape[0]
    outs[0][...] = own[0][...] + item[:width, :].astype(F32)
    total = own[1][...] + item[width:at, :].astype(F32)
    if part == 1:
        low = extra[0]
        split = low.shape[0]
        outs[1][:split, :] = low[...]
        outs[1][split:, :] = total
        return
    outs[1][...] = total
    chunk = own[2].shape[0]
    for i, piece in enumerate(small_pieces(width, block)):
        rows = slice(at + i * chunk, at + (i + 1) * chunk)
        total = own[2][:, piece] + item[rows, : piece.stop - piece.start].astype(F32)
        outs[2][:chunk, piece] = total.astype(BF16)
    ring_size = extra[0].shape[0]
    lines = jnp.concatenate([extra[0][o] + extra[1][o] for o in range(ring_size)], 0)
    outs[2][chunk:, :block] = lines.astype(BF16)
    outs[2][chunk:, block:] = jnp.zeros((2 * ring_size, width - block), BF16)


def mixer_end(part, extra, own, item, after):
    width, block = own[0].shape
    if part == 0:
        rows = own[2].shape[0] + 2 * extra[0].shape[0]
        shapes = [own[0].shape, own[1].shape, (rows, width)]
    else:
        shapes = [own[0].shape, own[0].shape]
    return launch(
        lambda *refs: mixer_end_kernel(part, *refs),
        (*own, item, *extra),
        tuple(shaped(shape, BF16 if i == 2 else F32) for i, shape in enumerate(shapes)),
        "mixer_end",
        after=after,
        flops=HEAVY,
    )


def spread_kernel(head, owners, *refs):
    ring_size = owners.shape[0]
    gate_i, gate_r, taps, sums, gain_o, whole = refs[ring_size:]
    block = gain_o.shape[1]
    chunk = refs[0].shape[0] - 2 * ring_size
    gain = jnp.zeros((2, block), F32)
    for o in range(ring_size):
        at = pl.ds(pl.multiple_of(owners[o] * chunk, 16), chunk)
        whole[at, :] = refs[o][:chunk, :].astype(F32)
        mine = 2 * ((ring_size - o) % ring_size)
        gain = gain + refs[o][chunk:, :block].astype(F32)[mine : mine + 2, :]
    gate_i[...] = whole[:head, :]
    gate_r[...] = whole[head : 2 * head, :]
    count = taps.shape[0]
    taps[...] = whole[2 * head : 2 * head + count, :]
    sums[...] = whole[2 * head + count : 2 * head + SUMS, :]
    gain_o[...] = gain


def spread(head, count, block, owners, chunks, after):
    ring_size = len(chunks)
    rows, width = chunks[0].shape
    gate = shaped((head, width), F32)
    return launch(
        lambda *refs: spread_kernel(head, *refs),
        (owners, *chunks),
        (gate, gate, shaped((count, width), F32), shaped((SUMS - count, width), F32), shaped((2, block), F32)),
        "spread",
        scalars=1,
        after=after,
        scratch=[pltpu.VMEM(((rows - 2 * ring_size) * ring_size, width), F32)],
    )


def local(
    tokens,
    cotangent,
    row_length,
    first_gain,
    value_weight,
    gelu_weight,
    conv_weight,
    conv_bias,
    input_gate,
    input_bias,
    recur_gate,
    recur_bias,
    decay_param,
    output_weight,
    second_gain,
    mlp_gate,
    mlp_up,
    mlp_down,
):
    ring_size = lax.axis_size("dp")
    middle = ring_size // 2
    ring = [2 * i if i < middle else 2 * (ring_size - 1 - i) + 1 for i in range(ring_size)]
    onward = [(ring[i], ring[(i + 1) % ring_size]) for i in range(ring_size)]
    backward = [(b, a) for a, b in onward]
    me = lax.axis_index("dp")
    core = lax.axis_index("mp") % 2
    core_pair = [(i, i ^ 1) for i in range(4)]
    chip_pair = [(i, i ^ 2) for i in range(4)]
    index = jnp.arange(ring_size, dtype=jnp.int32)

    def spot_of(place):
        return jnp.where(place % 2 == 0, place // 2, ring_size - 1 - place // 2)

    spots = (spot_of(me) + index) % ring_size
    owners = jnp.where(spots < middle, 2 * spots, 2 * (ring_size - 1 - spots) + 1).astype(jnp.int32)
    slots = ((spot_of(index) - spot_of(me) + ring_size) % ring_size).astype(jnp.int32)

    subs, row_count, length, model = tokens.shape
    half = row_count * length
    seqs = subs * row_count
    block = model // ring_size
    width, head = input_gate.shape
    count = conv_weight.shape[0]
    split = (width // 2 + 127) // 128 * 128
    chunk = -(-(2 * head + SUMS) // (16 * ring_size)) * 16
    small_rows = chunk * ring_size

    def hops(long_way_on):
        return (middle, ring_size - 1 - middle) if long_way_on else (ring_size - 1 - middle, middle)

    token = []

    def mark(*values):
        token[:] = values

    class Gather:
        def __init__(self, shard, long_way_on):
            self.hops = hops(long_way_on)
            self.moving = [shard, shard]
            self.got = [shard] + [None] * (ring_size - 1)

        def step(self, s):
            for d, way in enumerate((onward, backward)):
                if s <= self.hops[d]:
                    self.moving[d] = lax.ppermute(self.moving[d], "dp", way)
                    self.got[ring_size - s if d == 0 else s] = self.moving[d]

    class Scatter:
        def __init__(self, term, end, long_way_on):
            self.term, self.ending = term, end
            self.hops = hops(long_way_on)
            self.moving = [None, None]
            self.own = None

        def step(self, s, weight=HEAVY, apart=False):
            turns, ways, fold = [], [], None
            for d in range(2):
                far = self.hops[d] - s
                if far > 0:
                    turns.append((far if d == 0 else ring_size - far, self.moving[d]))
                    ways.append(d)
                elif far == 0:
                    fold = self.moving[d]
            parts = self.term(turns, None if apart else fold, tuple(token), weight)
            mark(parts[0])
            for d, part in zip(ways, parts):
                self.moving[d] = lax.ppermute(part, "dp", (onward, backward)[d])
            if fold is not None:
                self.own = parts[len(turns) :]
                if apart:
                    self.own = self.term([], fold, tuple(token), weight)
                    mark(self.own[0])

        def end(self, *low):
            last = 0 if self.hops[0] > self.hops[1] else 1
            out = self.ending(low, self.own, self.moving[last], tuple(token))
            mark(out[0])
            return out

    def core_swap(other):
        return lax.ppermute(other, "mp", core_pair)

    def chip_swap(own, got, after):
        pair = pair_sum(own, got, after)
        mark(pair)
        return pair, lax.ppermute(pair, "mp", chip_pair)

    def both_halves(own, dim):
        return jnp.concatenate([own, lax.ppermute(own, "mp", core_pair)], dim)

    scalars = jnp.concatenate([core[None], row_length.reshape(-1)]).astype(jnp.int32)
    shard_one, shard_two = pack(
        split, value_weight.T, gelu_weight.T, output_weight, first_gain[None], second_gain[None]
    )
    ring_one, ring_two = Gather(shard_one, True), Gather(shard_two, False)
    ring_one.step(1)
    ring_two.step(1)

    decay_wide = decay_param.astype(F32)
    lines = jnp.concatenate(
        [
            conv_weight.astype(F32),
            jnp.stack(
                [
                    conv_bias.astype(F32),
                    input_bias.astype(F32),
                    recur_bias.astype(F32),
                    jax.nn.softplus(-decay_wide),
                    jax.nn.sigmoid(-decay_wide),
                ]
            ),
        ]
    )
    x, g, g_flat, r1, blocks_i, blocks_r = prepare(
        scalars,
        slots,
        tokens.reshape(subs, half, model),
        cotangent.reshape(subs, half, model),
        input_gate.T,
        recur_gate.T,
        (lines,),
    )
    x, *moved = lax.optimization_barrier((x, *ring_one.moving, *ring_two.moving))
    ring_one.moving, ring_two.moving = moved[:2], moved[2:]
    for s in range(2, middle + 1):
        ring_one.step(s)
        ring_two.step(s)
    one, two = ring_one.got, ring_two.got

    hop_groups = [[0, 1, ring_size - 1]] + [[s, ring_size - s] for s in range(2, middle)] + [[middle]]
    places, n1, sums_so_far = {}, [], None
    for place, offsets in enumerate(hop_groups):
        bx, by, n1_part = project(
            offsets, x, r1, [one[o] for o in offsets], [two[o] for o in offsets], sums_so_far, width, split
        )
        sums_so_far = (bx, by)
        n1.append(n1_part)
        places |= {o: (place, i) for i, o in enumerate(offsets)}

    p, cx, lx, lr, h = mixer_forward(seqs, count, bx, by, lines, blocks_i, blocks_r)
    own, other, gains = mixer_out(p, one, two, split)
    pair, other = chip_swap(own, core_swap(other), ())
    dq = unit_grad(g_flat, mlp_down, (pair,))
    fetched = fetch(mlp_gate, mlp_up, (dq,))
    h1, n2_own, r2 = norm(slots, x, gains, pair, other, (fetched[0],))
    n2 = both_halves(n2_own, 0)
    q_a, dga_a, dup_a, n2_rel = unit_first(slots, n2, *fetched, dq)
    unit_a = Scatter(lambda *a: unit_term(n2_rel, g, dga_a, dup_a, q_a, *a), unit_end, True)
    unit_a.step(0)
    q_b, dga_b, dup_b = unit_second(n2, mlp_gate, mlp_up, dq, tuple(token))
    unit_b = Scatter(lambda *a: unit_term(n2_rel, g, dga_b, dup_b, q_b, *a), unit_end, False)
    unit_b.step(0, 1)
    last = middle - 1

    def now():
        return tuple(token)

    own, other = unit_back(owners, (dga_a, dga_b, dup_a, dup_b), mlp_gate, mlp_up, now())
    mark(own)
    got = core_swap(other)
    for s in range(1, max(last - 1, 1)):
        unit_a.step(s)
        if s == 1:
            pair, other = chip_swap(own, got, now())
        unit_b.step(s)
    unit_a.step(last - 1)
    dh1, dhr_own, second_grad = norm_back(pair, other, h1, r2, gains, g, now())
    mark(dhr_own)
    dhr = both_halves(dhr_own, 1)
    unit_b.step(last - 1)
    dbx, dby, small = mixer_backward(
        seqs, head, count, split, small_rows, dhr, two, (bx, by, cx, lx, lr, h, lines, blocks_i, blocks_r), now()
    )
    mark(dbx)
    half_split = width // 2 // 128 * 128
    mixer_a = Scatter(
        lambda *a: mixer_term(0, places, half_split, chunk, owners, n1, dhr, dbx, p, small, *a),
        lambda *a: mixer_end(0, *a),
        True,
    )
    mixer_b = Scatter(
        lambda *a: mixer_term(1, places, half_split, chunk, owners, n1, dhr, dby, p, None, *a),
        lambda *a: mixer_end(1, *a),
        False,
    )
    mixer_a.step(0)
    unit_a.step(last)
    out_own, out_other = unit_out(q_a, q_b, mlp_down, now())
    mark(out_own)
    layer_pair = pair_sum(out_own, core_swap(out_other), now())
    mark(layer_pair)
    own, other = input_out(dbx, dby, one, two, split, now())
    mark(own)
    got = core_swap(other)
    unit_b.step(last)
    pair, other = chip_swap(own, got, now())
    mixer_a.step(1)
    low = unit_a.end()
    mixer_b.step(0, 1)
    gate_grad, up_grad, down_grad = unit_b.end(*low)
    input_own, gain_grads = input_back(slots, pair, other, x, r1, gains, dh1, second_grad, now())
    mark(input_own)
    layer_pair = relay(layer_pair, now())
    mark(layer_pair)
    layer_other = lax.ppermute(layer_pair, "mp", chip_pair)
    gain_got = core_swap(gain_grads)
    for s in range(2, middle):
        mixer_a.step(s)
        if s == middle - 1:
            both_own = finish(slots, h1, layer_pair, layer_other, input_own, now())
            mark(both_own)
        mixer_b.step(s - 1)
    input_grad, layer_out = arrange(scalars, both_own, core_swap(both_own), now())
    mark(layer_out)
    value_grad, output_low, small = mixer_a.end(gain_grads, gain_got)
    small_ring = Gather(small, True)
    mixer_b.step(last, 1, True)
    for s in range(1, middle + 1):
        small_ring.step(s)
    gelu_grad, output_grad = mixer_b.end(output_low)
    gate_i, gate_r, taps_grad, sums, gain_grads = spread(head, count, block, owners, small_ring.got, now())

    return (
        layer_out.reshape(tokens.shape),
        input_grad.reshape(tokens.shape),
        gain_grads[0],
        value_grad.T,
        gelu_grad.T,
        taps_grad,
        sums[0],
        gate_i.T,
        sums[1],
        gate_r.T,
        sums[2],
        sums[3],
        output_grad,
        gain_grads[1],
        gate_grad,
        up_grad,
        down_grad,
    )


def solution(mesh):
    placed = (
        P(None, "dp", None, None),
        P(None, "dp", None, None),
        P(None, "dp"),
        P("dp"),
        P("dp", "mp"),
        P("dp", "mp"),
        P(None, "mp"),
        P("mp"),
        P("mp", None),
        P("mp"),
        P("mp", None),
        P("mp"),
        P("mp"),
        P("mp", "dp"),
        P("dp"),
        P(None, "mp"),
        P(None, "mp"),
        P("mp", None),
    )
    return jax.shard_map(
        local,
        mesh=mesh,
        in_specs=placed,
        out_specs=(
            P(None, "dp", None, None),
            P(None, "dp", None, None),
            P("dp"),
            P("dp", "mp"),
            P("dp", "mp"),
            P(None, "mp"),
            P("mp"),
            P("mp", None),
            P("mp"),
            P("mp", None),
            P("mp"),
            P("mp"),
            P("mp", "dp"),
            P("dp"),
            P("dp", "mp"),
            P("dp", "mp"),
            P("mp", "dp"),
        ),
        check_vma=False,
    )
```

```python
import jax
import jax.numpy as jnp
from jax import lax
from jax.experimental import pallas as pl
from jax.experimental.pallas import tpu as pltpu
from jax.sharding import PartitionSpec as P

EPSILON = 1e-06
DECAY_SCALE = 8.0
GELU_A = 0.7978845608028654
GELU_B = 0.044715
BF16 = jnp.bfloat16
F32 = jnp.float32
STEP = 16
HALF = 8
SUMS = 8
HEAVY = 100 * 10**9
END_WEIGHT = 1
TN = (((0,), (0,)), ((), ()))
NT = (((1,), (1,)), ((), ()))


def gelu(v):
    return 0.5 * v * (1.0 + jnp.tanh(GELU_A * (v + GELU_B * v * v * v)))


def gelu_both(v):
    squared = v * v
    bent = jnp.tanh(GELU_A * v * (1.0 + GELU_B * squared))
    value = 0.5 * v * (1.0 + bent)
    slope = 0.5 * (1.0 + bent) + 0.5 * v * (1.0 - bent * bent) * GELU_A * (
        1.0 + 3.0 * GELU_B * squared
    )
    return value, slope


def negative_expm1(z, exp_z):
    series = 1.0 + z * (1.0 / 7.0)
    for k in (6.0, 5.0, 4.0, 3.0, 2.0):
        series = 1.0 + z * (1.0 / k) * series
    return jnp.where(z > -0.25, -z * series, 1.0 - exp_z)


def rows_of(shape):
    return lax.broadcasted_iota(jnp.int32, shape, 0)


def earlier(now, before, k, rows):
    return jnp.where(rows < k, pltpu.roll(before, k, 0), pltpu.roll(now, k, 0))


def later(now, after, k, rows):
    size = now.shape[0]
    return jnp.where(
        rows >= size - k, pltpu.roll(after, size - k, 0), pltpu.roll(now, size - k, 0)
    )


def shaped(shape, dtype):
    return jax.ShapeDtypeStruct(shape, dtype)


def launch(
    kernel, inputs, out_shape, name, scalars=0, after=(), mib=10, scratch=(), aliases=None, grid=None, flops=1
):
    count, extra = len(inputs), len(after)
    waits = [pl.BlockSpec(memory_space=pl.ANY)] * extra
    in_specs = [pl.BlockSpec(memory_space=pltpu.SMEM)] * scalars
    more = {}
    if grid is None:
        in_specs += [pl.BlockSpec(memory_space=pltpu.VMEM)] * (count - scalars)
    else:
        in_specs += grid[1]
        more = {"grid": grid[0], "out_specs": grid[2]}
    return pl.pallas_call(
        lambda *refs: kernel(*refs[:count], *refs[count + extra :]),
        in_specs=in_specs + waits,
        out_shape=out_shape,
        scratch_shapes=list(scratch),
        input_output_aliases=aliases or {},
        compiler_params=pltpu.CompilerParams(vmem_limit_bytes=mib << 20),
        cost_estimate=pl.CostEstimate(flops=flops, bytes_accessed=1, transcendentals=0),
        name=name,
        **more,
    )(*inputs, *after)


def in_hbm(array):
    return pltpu.with_memory_space_constraint(array, pltpu.HBM)


def mixer_forward_kernel(
    seqs, count, bx, by, lines, blocks_i, blocks_r, p_o, cx_o, lx_o, lr_o, h_o
):
    total, width = bx.shape
    length = total // seqs
    steps = length // STEP
    rows16 = rows_of((STEP, width))
    w = [jnp.broadcast_to(lines[k : k + 1, :], (STEP, width)) for k in range(count)]
    shift = jnp.broadcast_to(lines[count : count + 1, :], (STEP, width))
    bias_i, bias_r = lines[count + 1 : count + 2, :], lines[count + 2 : count + 3, :]
    soft = lines[count + 3 : count + 4, :]
    for seq in range(seqs):

        def conv(i, before):
            at = pl.ds(pl.multiple_of(seq * length + i * STEP, STEP), STEP)
            now = bx[at, :]
            mixed = shift + w[0] * now
            for k in range(1, count):
                mixed = mixed + w[k] * earlier(now, before, k, rows16)
            cx_o[at, :] = mixed.astype(BF16)
            return now

        lax.fori_loop(0, steps, conv, jnp.zeros((STEP, width), F32), unroll=2)
    lx_o[...] = lax.dot_general(cx_o[...], blocks_i[...], NT, preferred_element_type=F32) + bias_i
    lr_o[...] = lax.dot_general(cx_o[...], blocks_r[...], NT, preferred_element_type=F32) + bias_r
    rows8 = rows_of((HALF, width))
    soft8 = jnp.broadcast_to(-DECAY_SCALE * soft, (HALF, width))

    def scan(i, carries):
        out = []
        for seq in range(seqs):
            carry = carries[seq]
            base = seq * length + i * STEP
            at = pl.ds(pl.multiple_of(base, STEP), STEP)
            cx16 = cx_o[at, :].astype(F32)
            products = []
            for part in range(STEP // HALF):
                here = pl.ds(pl.multiple_of(base + part * HALF, HALF), HALF)
                cx = cx16[part * HALF : (part + 1) * HALF, :]
                ix = jax.nn.sigmoid(lx_o[here, :])
                la = soft8 * jax.nn.sigmoid(lr_o[here, :])
                a = jnp.exp(la)
                rest = negative_expm1(2.0 * la, a * a)
                m = jnp.where(rest > 0.0, rest * lax.rsqrt(rest), 0.0)
                u = m * ix * cx
                for s in (1, 2, 4):
                    keep = rows8 >= s
                    u = u + jnp.where(keep, a * pltpu.roll(u, s, 0), 0.0)
                    a = jnp.where(keep, a * pltpu.roll(a, s, 0), a)
                h = u + a * carry
                carry = jnp.broadcast_to(h[HALF - 1 : HALF, :], (HALF, width))
                h_o[here, :] = h
                products.append(h * gelu(by[here, :]))
            p_o[at, :] = jnp.concatenate(products, 0).astype(BF16)
            out.append(carry)
        return tuple(out)

    lax.fori_loop(0, steps, scan, tuple(jnp.zeros((HALF, width), F32) for _ in range(seqs)), unroll=4)


def mixer_forward(seqs, count, bx, by, lines, blocks_i, blocks_r):
    low, full = shaped(bx.shape, BF16), shaped(bx.shape, F32)
    return launch(
        lambda *refs: mixer_forward_kernel(seqs, count, *refs),
        (bx, by, lines, blocks_i, blocks_r),
        (low, low, full, full, full),
        "mixer_forward",
    )


def mixer_backward_kernel(seqs, head, count, split, dhr, *refs):
    ring_size = dhr.shape[0]
    second = refs[:ring_size]
    bx, by, cx_i, lx_i, lr_i, h_i, lines, blocks_i, blocks_r = refs[ring_size : ring_size + 9]
    dbx_o, dby_o, small_o, dlx_o, dlr_o, dcx_s, dp = refs[ring_size + 9 :]
    skip = bx.shape[1] - split
    soft, gate_soft = lines[count + 3 : count + 4, :], lines[count + 4 : count + 5, :]
    for o in range(ring_size):
        part = lax.dot_general(dhr[o], second[o][skip:, :], NT, preferred_element_type=F32)
        dp[...] = part if o == 0 else dp[...] + part
    total, width = bx.shape
    length = total // seqs
    steps = length // STEP
    rows8 = rows_of((HALF, width))
    soft8 = jnp.broadcast_to(-DECAY_SCALE * soft, (HALF, width))
    zero = jnp.zeros((HALF, width), F32)

    def scan(j, state):
        i = steps - 1 - j
        sums_i, sums_r, sums_d = state[0]
        out = []
        for seq in range(seqs):
            a_after, e_after = state[1][seq]
            base = seq * length + i * STEP
            at = pl.ds(pl.multiple_of(base, STEP), STEP)
            cx16 = cx_i[at, :].astype(F32)
            dby_parts, dlx_parts, dlr_parts = [None, None], [None, None], [None, None]
            for part in (1, 0):
                start = base + part * HALF
                here = pl.ds(pl.multiple_of(start, HALF), HALF)
                cx = cx16[part * HALF : (part + 1) * HALF, :]
                ix = jax.nn.sigmoid(lx_i[here, :])
                ra = jax.nn.sigmoid(lr_i[here, :])
                la = soft8 * ra
                a = jnp.exp(la)
                rest = negative_expm1(2.0 * la, a * a)
                inverse = lax.rsqrt(rest)
                m = rest * inverse
                h = h_i[here, :]
                first = (i == 0) if part == 0 else False
                back = jnp.maximum(start - HALF, 0)
                before = h_i[pl.ds(pl.multiple_of(back, HALF), HALF), :]
                if part == 0:
                    before = jnp.where(i == 0, 0.0, before)
                h_prev = earlier(h, before, 1, rows8)
                gy, slope = gelu_both(by[here, :])
                grad = dp[here, :]
                dby_parts[part] = grad * h * slope
                e = grad * gy
                f = later(a, a_after, 1, rows8)
                for s in (1, 2, 4):
                    keep = rows8 < HALF - s
                    e = e + jnp.where(keep, f * pltpu.roll(e, HALF - s, 0), 0.0)
                    f = jnp.where(keep, f * pltpu.roll(f, HALF - s, 0), f)
                e = e + f * e_after
                e_after = jnp.broadcast_to(e[0:1, :], (HALF, width))
                a_after = a
                eix = e * ix
                dla = (e * h_prev - eix * cx * a * inverse) * a
                dlx = eix * m * cx * (1.0 - ix)
                dlr = dla * la * (1.0 - ra)
                sums_i = sums_i + dlx
                sums_r = sums_r + dlr
                sums_d = sums_d + dla * ra
                dlx_parts[part], dlr_parts[part] = dlx, dlr
                dcx_s[here, :] = eix * m
            dby_o[at, :] = jnp.concatenate(dby_parts, 0).astype(BF16)
            dlx_o[at, :] = jnp.concatenate(dlx_parts, 0).astype(BF16)
            dlr_o[at, :] = jnp.concatenate(dlr_parts, 0).astype(BF16)
            out.append((a_after, e_after))
        return (sums_i, sums_r, sums_d), tuple(out)

    (sums_i, sums_r, sums_d), _ = lax.fori_loop(
        0, steps, scan, ((zero, zero, zero), tuple((zero, zero) for _ in range(seqs)))
    )
    dcx_s[...] += jnp.dot(dlx_o[...], blocks_i[...], preferred_element_type=F32) + jnp.dot(
        dlr_o[...], blocks_r[...], preferred_element_type=F32
    )
    rows16 = rows_of((STEP, width))
    w = [jnp.broadcast_to(lines[k : k + 1, :], (STEP, width)) for k in range(count)]
    zero16 = jnp.zeros((STEP, width), F32)
    sums_t = tuple(zero16 for _ in range(count))
    sums_b = zero16
    for seq in range(seqs):

        def conv(j, state):
            after, tap_sums, shift_sum = state
            at = pl.ds(pl.multiple_of(seq * length + (steps - 1 - j) * STEP, STEP), STEP)
            now = dcx_s[at, :]
            source = bx[at, :]
            grad = w[0] * now
            new_sums = [tap_sums[0] + now * source]
            for k in range(1, count):
                moved = later(now, after, k, rows16)
                grad = grad + w[k] * moved
                new_sums.append(tap_sums[k] + moved * source)
            dbx_o[at, :] = grad.astype(BF16)
            return now, tuple(new_sums), shift_sum + now

        _, sums_t, sums_b = lax.fori_loop(0, steps, conv, (zero16, sums_t, sums_b))
    rows = [jnp.sum(item, 0, keepdims=True) for item in (*sums_t, sums_b, sums_i, sums_r)]
    rows.append(DECAY_SCALE * gate_soft * jnp.sum(sums_d, 0, keepdims=True))
    spare = small_o.shape[0] - 2 * head - SUMS
    if spare:
        rows.append(jnp.zeros((spare, width), F32))
    small_o[2 * head :, :] = jnp.concatenate(rows, 0).astype(BF16)
    lanes = lax.broadcasted_iota(jnp.int32, (head, width), 1)
    for gate, grads in enumerate((dlx_o, dlr_o)):
        whole = lax.dot_general(grads[...], cx_i[...], TN, preferred_element_type=F32)
        picked = whole[:head]
        for i in range(1, width // head):
            picked = jnp.where(lanes < i * head, picked, whole[i * head : (i + 1) * head])
        small_o[gate * head : (gate + 1) * head, :] = picked.astype(BF16)


def mixer_backward(seqs, head, count, split, small_rows, dhr, second, saved, after):
    total, width = saved[0].shape
    low = shaped((total, width), BF16)
    return launch(
        lambda *refs: mixer_backward_kernel(seqs, head, count, split, *refs),
        (dhr, *second, *saved),
        (low, low, shaped((small_rows, width), BF16)),
        "mixer_backward",
        after=after,
        mib=18,
        scratch=[
            pltpu.VMEM((total, width), BF16),
            pltpu.VMEM((total, width), BF16),
            pltpu.VMEM((total, width), F32),
            pltpu.VMEM((total, width), F32),
        ],
    )


def copy_all(pairs, sems):
    copies = [
        pltpu.make_async_copy(source, target, sems.at[i]) for i, (source, target) in enumerate(pairs)
    ]
    for copy in copies:
        copy.start()
    return copies


def pack_two_kernel(split, gelu_w, output, two_o, sems):
    width = gelu_w.shape[0]
    pairs = (
        (gelu_w.at[pl.ds(split, width - split)], two_o.at[pl.ds(0, width - split)]),
        (output, two_o.at[pl.ds(width - split, width)]),
    )
    for copy in copy_all(pairs, sems):
        copy.wait()


def pack_one_kernel(split, gain_one, gain_two, value, gelu_w, one_o, sems):
    width = value.shape[0]
    pairs = (
        (value, one_o.at[pl.ds(0, width)]),
        (gelu_w.at[pl.ds(0, split)], one_o.at[pl.ds(width + 16, split)]),
    )
    copies = copy_all(pairs, sems)
    spare = jnp.zeros((14, value.shape[1]), F32)
    lines = jnp.concatenate([gain_one[...].astype(F32), gain_two[...].astype(F32), spare], 0)
    one_o[width : width + 16, :] = lines.astype(BF16)
    for copy in copies:
        copy.wait()


def pack(split, value, gelu_w, output, gain_one, gain_two):
    width, block = value.shape
    whole = pl.BlockSpec(memory_space=pltpu.VMEM)
    anywhere = pl.BlockSpec(memory_space=pl.ANY)
    value, gelu_w, output = in_hbm(value), in_hbm(gelu_w), in_hbm(output)
    two = launch(
        lambda *refs: pack_two_kernel(split, *refs),
        (gelu_w, output),
        shaped((2 * width - split, block), BF16),
        "pack_two",
        scratch=[pltpu.SemaphoreType.DMA((2,))],
        grid=((), [anywhere, anywhere], whole),
    )
    one = launch(
        lambda *refs: pack_one_kernel(split, *refs),
        (gain_one, gain_two, value, gelu_w),
        shaped((width + 16 + split, block), BF16),
        "pack_one",
        after=(two,),
        scratch=[pltpu.SemaphoreType.DMA((2,))],
        grid=((), [whole, whole, anywhere, anywhere], whole),
    )
    return one, two


def prepare_kernel(scalars, slots, tokens, cotangent, gate_i, gate_r, x_o, g_o, flat_o, r_o, blocks_i, blocks_r):
    ring_size, total, block = x_o.shape
    half = total // 2
    row_count = (scalars.shape[0] - 1) // 2
    length = half // row_count
    rows = lax.broadcasted_iota(jnp.int32, (length, block), 0)
    for place in range(2):
        sub = scalars[0] if place == 0 else 1 - scalars[0]
        for row in range(row_count):
            at = slice(place * half + row * length, place * half + (row + 1) * length)
            source = pl.ds(row * length, length)
            valid = jnp.where(rows < scalars[1 + sub * row_count + row], 1.0, 0.0)
            squares = jnp.zeros((length, block), F32)
            for k in range(ring_size):
                columns = slice(k * block, (k + 1) * block)
                piece = tokens[sub, source, columns]
                wide = piece.astype(F32)
                squares = squares + wide * wide
                x_o[slots[k], at, :] = piece
                masked = (cotangent[sub, source, columns].astype(F32) * valid).astype(BF16)
                g_o[slots[k], at, :] = masked
                flat_o[at, columns] = masked
            mean = jnp.sum(squares, 1, keepdims=True) * (1.0 / (ring_size * block))
            r_o[at, :] = lax.rsqrt(mean + EPSILON)
    head, width = gate_i.shape
    lanes = lax.broadcasted_iota(jnp.int32, (head, width), 1)
    for source, out in ((gate_i, blocks_i), (gate_r, blocks_r)):
        wide = source[...].astype(F32)
        for i in range(width // head):
            inside = (lanes >= i * head) & (lanes < (i + 1) * head)
            out[i * head : (i + 1) * head, :] = jnp.where(inside, wide, 0.0).astype(BF16)


def prepare(scalars, slots, tokens, cotangent, gate_i, gate_r, after):
    subs, half, model = tokens.shape
    total, ring_size, width = subs * half, slots.shape[0], gate_i.shape[1]
    rel = shaped((ring_size, total, model // ring_size), BF16)
    blocks = shaped((width, width), BF16)
    return launch(
        prepare_kernel,
        (scalars, slots, tokens, cotangent, gate_i, gate_r),
        (rel, rel, shaped((total, model), BF16), shaped((total, 1), F32), blocks, blocks),
        "prepare",
        scalars=2,
        after=after,
    )


def project_kernel(offsets, first, width, split, x, r1, *refs):
    count = len(offsets)
    one, two = refs[:count], refs[count : 2 * count]
    rest = refs[2 * count :]
    if not first:
        before = rest[:2]
        rest = rest[2:]
    bx, by, n1_o = rest
    scale = r1[...]
    for i, o in enumerate(offsets):
        gain = one[i][width : width + 16, :].astype(F32)[0:1, :]
        n1 = (x[o].astype(F32) * scale * gain).astype(BF16)
        n1_o[i] = n1
        for out, place, columns, weight in (
            (bx, 0, slice(0, width), one[i][:width, :]),
            (by, 1, slice(0, split), one[i][width + 16 :, :]),
            (by, 1, slice(split, width), two[i][: width - split, :]),
        ):
            part = lax.dot_general(n1, weight, NT, preferred_element_type=F32)
            if i > 0:
                out[:, columns] += part
            elif first:
                out[:, columns] = part
            else:
                out[:, columns] = before[place][:, columns] + part


def project(offsets, x, r1, one, two, before, width, split):
    total, block = x.shape[1:]
    count = len(offsets)
    full = shaped((total, width), F32)
    at = 2 + 2 * count
    return launch(
        lambda *refs: project_kernel(offsets, before is None, width, split, *refs),
        (x, r1, *one, *two, *(before or ())),
        (full, full, shaped((count, total, block), BF16)),
        "project",
        aliases={} if before is None else {at: 0, at + 1: 1},
    )


def mixer_out_kernel(skip, p, *refs):
    own_o, other_o, gains_o = refs[-3:]
    count, half = own_o.shape[:2]
    width = p.shape[1]
    for o in range(count):
        part = jnp.dot(p[...], refs[count + o][skip:, :], preferred_element_type=F32)
        own_o[o] = part[:half]
        other_o[o] = part[half:].astype(BF16)
        gains_o[o] = refs[o][width : width + 16, :].astype(F32)[0:2, :]


def mixer_out(p, one, two, split, after):
    total, width = p.shape
    count, block = len(one), one[0].shape[1]
    shape = (count, total // 2, block)
    return launch(
        lambda *refs: mixer_out_kernel(width - split, *refs),
        (p, *one, *two),
        (shaped(shape, F32), shaped(shape, BF16), shaped((count, 2, block), F32)),
        "mixer_out",
        after=after,
        mib=10,
    )


def input_out_kernel(split, dbx, dby, *refs):
    own_o, other_o = refs[-2:]
    count, half = own_o.shape[:2]
    width = dbx.shape[1]
    for o in range(count):
        one, two = refs[o], refs[count + o]
        part = (
            jnp.dot(dbx[...], one[:width, :], preferred_element_type=F32)
            + jnp.dot(dby[:, :split], one[width + 16 :, :], preferred_element_type=F32)
            + jnp.dot(dby[:, split:], two[: width - split, :], preferred_element_type=F32)
        )
        own_o[o] = part[:half]
        other_o[o] = part[half:].astype(BF16)


def input_out(dbx, dby, one, two, split, after):
    shape = (len(one), dbx.shape[0] // 2, one[0].shape[1])
    return launch(
        lambda *refs: input_out_kernel(split, *refs),
        (dbx, dby, *one, *two),
        (shaped(shape, F32), shaped(shape, BF16)),
        "input_out",
        after=after,
        mib=10,
    )


def pair_kernel(own, got, out):
    out[...] = (own[...] + got[...].astype(F32)).astype(BF16)


def pair_sum(own, got, after):
    return launch(pair_kernel, (own, got), shaped(own.shape, BF16), "pair_sum", after=after)


def relay_kernel(source, out):
    out[...] = source[...]


def relay(source, after):
    return launch(relay_kernel, (source,), shaped(source.shape, source.dtype), "relay", after=after)


def norm_kernel(slots, x, full_gains, *refs):
    h_o, n_o, r_o = refs[-3:]
    ring_size, half, block = h_o.shape
    cut = ring_size // 2 + 1
    groups = [refs[0:2], refs[2:4]]
    squares = jnp.zeros((half, block), F32)
    for o in range(ring_size):
        pair, other = groups[o // cut]
        i = o % cut
        h = x[o, 0:half, :].astype(F32) + (pair[i].astype(F32) + other[i].astype(F32))
        h_o[o] = h
        squares = squares + h * h
    mean = jnp.sum(squares, 1, keepdims=True) * (1.0 / (ring_size * block))
    scale = lax.rsqrt(mean + EPSILON)
    r_o[...] = scale
    for k in range(ring_size):
        o = slots[k]
        gain = full_gains[o, 1:2, :]
        n_o[:, k * block : (k + 1) * block] = (h_o[o] * scale * gain).astype(BF16)


def norm(slots, x, gains, sums, after):
    ring_size, total, block = x.shape
    half = total // 2
    return launch(
        norm_kernel,
        (slots, x, gains, *sums),
        (
            shaped((ring_size, half, block), F32),
            shaped((half, ring_size * block), BF16),
            shaped((half, 1), F32),
        ),
        "norm",
        scalars=1,
        after=after,
    )


def norm_back_kernel(pair, other, h1, r2, gains, g, dh_o, dhr_o, grad_o):
    ring_size, half, block = h1.shape
    dots = jnp.zeros((half, block), F32)
    scale = r2[...]
    for o in range(ring_size):
        product = (pair[o].astype(F32) + other[o].astype(F32)) * h1[o]
        dots = dots + product * gains[o, 1:2, :]
        grad_o[o] = jnp.sum(product * scale, 0, keepdims=True)
    mean = jnp.sum(dots, 1, keepdims=True) * (1.0 / (ring_size * block))
    bend = scale * scale * scale * mean
    for o in range(ring_size):
        grad = pair[o].astype(F32) + other[o].astype(F32)
        dh = g[o, 0:half, :].astype(F32) + scale * (grad * gains[o, 1:2, :]) - h1[o] * bend
        dh_o[o] = dh
        dhr_o[o] = dh.astype(BF16)


def norm_back(pair, other, h1, r2, gains, g, after):
    ring_size, half, block = pair.shape
    return launch(
        norm_back_kernel,
        (pair, other, h1, r2, gains, g),
        (shaped(pair.shape, F32), shaped(pair.shape, BF16), shaped((ring_size, 1, block), F32)),
        "norm_back",
        after=after,
    )


def input_back_kernel(slots, pair, other, x, r1, gains, dh1, second, out_o, grad_o):
    ring_size, half, block = dh1.shape
    dots = jnp.zeros((half, block), F32)
    scale = r1[0:half, :]
    for o in range(ring_size):
        product = (pair[o].astype(F32) + other[o].astype(F32)) * x[o, 0:half, :].astype(F32)
        dots = dots + product * gains[o, 0:1, :]
        grad_o[o, 0:1, :] = jnp.sum(product * scale, 0, keepdims=True)
        grad_o[o, 1:2, :] = second[o]
    mean = jnp.sum(dots, 1, keepdims=True) * (1.0 / (ring_size * block))
    bend = scale * scale * scale * mean
    for k in range(ring_size):
        o = slots[k]
        grad = pair[o].astype(F32) + other[o].astype(F32)
        out_o[:, k * block : (k + 1) * block] = (
            dh1[o] + scale * (grad * gains[o, 0:1, :]) - x[o, 0:half, :].astype(F32) * bend
        )


def input_back(slots, pair, other, x, r1, gains, dh1, second, after):
    ring_size, half, block = pair.shape
    return launch(
        input_back_kernel,
        (slots, pair, other, x, r1, gains, dh1, second),
        (shaped((half, ring_size * block), F32), shaped((ring_size, 2, block), F32)),
        "input_back",
        scalars=1,
        after=after,
    )


def finish_kernel(slots, h1, pair, other, beside, out_o):
    ring_size, half, block = h1.shape
    out_o[0] = beside[...]
    for k in range(ring_size):
        columns = slice(k * block, (k + 1) * block)
        summed = pair[:, columns].astype(F32) + other[:, columns].astype(F32)
        out_o[1, :, columns] = h1[slots[k]] + summed


def finish(slots, h1, pair, other, beside, after):
    return launch(
        finish_kernel,
        (slots, h1, pair, other, beside),
        shaped((2, *beside.shape), F32),
        "finish",
        scalars=1,
        after=after,
        mib=10,
    )


def arrange_kernel(scalars, own, got, *outs):
    core = scalars[0]
    for i, out in enumerate(outs):
        out[core] = own[i]
        out[1 - core] = got[i]


def arrange(scalars, own, got, after):
    out = shaped((2, *own.shape[1:]), own.dtype)
    return launch(
        arrange_kernel, (scalars, own, got), (out,) * own.shape[0], "arrange", scalars=1, after=after, mib=24
    )


def unit_grad_kernel(g, down, dq_o):
    dq_o[...] = lax.dot_general(g[...], down[...], NT, preferred_element_type=F32)


def unit_grad(g, down, after):
    total, model = g.shape
    units = down.shape[0]
    tile = 256
    grid = (
        (units // tile,),
        [pl.BlockSpec((total, model), lambda i: (0, 0)), pl.BlockSpec((tile, model), lambda i: (i, 0))],
        pl.BlockSpec((total, tile), lambda i: (0, i)),
    )
    return launch(unit_grad_kernel, (g, in_hbm(down)), shaped((total, units), F32), "unit_grad", after=after, grid=grid)


def fetch_kernel(gate, up, gate_o, up_o, sems):
    columns = pl.ds(0, gate_o.shape[1])
    copies = [
        pltpu.make_async_copy(source.at[:, columns], target, sems.at[i])
        for i, (source, target) in enumerate(((gate, gate_o), (up, up_o)))
    ]
    for copy in copies:
        copy.start()
    for copy in copies:
        copy.wait()


def fetch(gate, up, after):
    model, units = gate.shape
    whole = pl.BlockSpec(memory_space=pltpu.VMEM)
    anywhere = pl.BlockSpec(memory_space=pl.ANY)
    half = shaped((model, units // 2), BF16)
    return launch(
        fetch_kernel,
        (in_hbm(gate), in_hbm(up)),
        (half, half),
        "fetch",
        after=after,
        scratch=[pltpu.SemaphoreType.DMA((2,))],
        grid=((), [anywhere, anywhere], [whole, whole]),
    )


def unit_products(ga, upward, grad):
    value, slope = gelu_both(ga)
    return value * upward, grad * upward * slope, grad * value


def unit_first_kernel(slots, n2, gate, up, dq, q_o, dga_o, dup_o, rel_o):
    ring_size, total, block = rel_o.shape
    tile = 256
    for i in range(0, gate.shape[1], tile):
        columns = slice(i, i + tile)
        ga = jnp.dot(n2[...], gate[:, columns], preferred_element_type=F32)
        upward = jnp.dot(n2[...], up[:, columns], preferred_element_type=F32)
        for out, item in zip((q_o, dga_o, dup_o), unit_products(ga, upward, dq[:, columns])):
            out[:, columns] = item.astype(BF16)
    for k in range(ring_size):
        rel_o[slots[k]] = n2[:, k * block : (k + 1) * block]


def unit_first(slots, n2, gate, up, dq):
    total, model = n2.shape
    ring_size = slots.shape[0]
    out = shaped((total, gate.shape[1]), BF16)
    return launch(
        unit_first_kernel,
        (slots, n2, gate, up, dq),
        (out, out, out, shaped((ring_size, total, model // ring_size), BF16)),
        "unit_first",
        scalars=1,
        mib=28,
    )


def unit_kernel(n2, gate, up, dq, q_o, dga_o, dup_o):
    ga = jnp.dot(n2[...], gate[...], preferred_element_type=F32)
    upward = jnp.dot(n2[...], up[...], preferred_element_type=F32)
    for out, item in zip((q_o, dga_o, dup_o), unit_products(ga, upward, dq[...])):
        out[...] = item.astype(BF16)


def unit_second(n2, gate, up, dq, after):
    total, model = n2.shape
    share = gate.shape[1] // 2
    tile = 256
    first = share // tile
    wide = pl.BlockSpec((total, tile), lambda i: (0, i))
    tall = pl.BlockSpec((model, tile), lambda i: (0, i + first))
    out = shaped((total, share), BF16)
    grid = (
        (share // tile,),
        [
            pl.BlockSpec((total, model), lambda i: (0, 0)),
            tall,
            tall,
            pl.BlockSpec((total, tile), lambda i: (0, i + first)),
        ],
        [wide, wide, wide],
    )
    return launch(
        unit_kernel,
        (n2, in_hbm(gate), in_hbm(up), dq),
        (out, out, out),
        "unit_second",
        after=after,
        mib=28,
        grid=grid,
    )


def unit_out_kernel(q_a, q_b, down, own_o, other_o):
    half = own_o.shape[0]
    share = q_a.shape[1]
    part = jnp.dot(q_a[...], down[:share, :], preferred_element_type=F32)
    part = part + jnp.dot(q_b[...], down[share:, :], preferred_element_type=F32)
    own_o[...] = part[:half]
    other_o[...] = part[half:].astype(BF16)


def unit_out(q_a, q_b, down, after):
    total, share = q_a.shape
    units, model = down.shape
    half = total // 2
    tile = 256
    out = pl.BlockSpec((half, tile), lambda i: (0, i))
    left = pl.BlockSpec((total, share), lambda i: (0, 0))
    grid = ((model // tile,), [left, left, pl.BlockSpec((units, tile), lambda i: (0, i))], [out, out])
    return launch(
        unit_out_kernel,
        (q_a, q_b, in_hbm(down)),
        (shaped((half, model), F32), shaped((half, model), BF16)),
        "unit_out",
        after=after,
        grid=grid,
    )


def unit_back_kernel(owners, dga_a, dga_b, dup_a, dup_b, gate, up, *refs):
    own_o, other_o = refs[-2:]
    half = other_o.shape[1]
    share = dga_a.shape[1]
    part = None
    for left, right in (
        (dga_a, gate[:, :share]),
        (dga_b, gate[:, share:]),
        (dup_a, up[:, :share]),
        (dup_b, up[:, share:]),
    ):
        term = lax.dot_general(left[...], right, NT, preferred_element_type=F32)
        part = term if part is None else part + term
    own_o[0] = part[:half]
    other_o[0] = part[half:].astype(BF16)


def unit_back(owners, grads, gate, up, after):
    ring_size = owners.shape[0]
    total, share = grads[0].shape
    model, units = gate.shape
    half = total // 2
    block = model // ring_size
    left = pl.BlockSpec((total, share), lambda o, owners: (0, 0))
    weight = pl.BlockSpec((block, units), lambda o, owners: (owners[o], 0))
    out = pl.BlockSpec((1, half, block), lambda o, owners: (o, 0, 0))
    return pl.pallas_call(
        unit_back_kernel,
        grid_spec=pltpu.PrefetchScalarGridSpec(
            num_scalar_prefetch=1,
            grid=(ring_size,),
            in_specs=[left] * 4 + [weight, weight, *[pl.BlockSpec(memory_space=pl.ANY)] * len(after)],
            out_specs=[out, out],
        ),
        out_shape=(shaped((ring_size, half, block), F32), shaped((ring_size, half, block), BF16)),
        compiler_params=pltpu.CompilerParams(vmem_limit_bytes=24 << 20),
        cost_estimate=pl.CostEstimate(flops=1, bytes_accessed=1, transcendentals=0),
        name="unit_back",
    )(owners, *grads, in_hbm(gate), in_hbm(up), *after)


def unit_term_kernel(turns, fold, n2, g, dga, dup, q, *refs):
    share = q.shape[1]
    rest = list(refs)
    outs = rest[len(rest) - len(turns) - (3 if fold else 0) :]
    parts = [slice(i * share, (i + 1) * share) for i in range(3)]

    def terms(o):
        return (
            lax.dot_general(n2[o], dga[...], TN, preferred_element_type=F32),
            lax.dot_general(n2[o], dup[...], TN, preferred_element_type=F32),
        )

    for (o, has), out in zip(turns, outs):
        recv = rest.pop(0) if has else None
        down = lax.dot_general(g[o], q[...], TN, preferred_element_type=F32)
        for grad, columns in zip((*terms(o), down), parts):
            if recv is not None:
                grad = grad + recv[:, columns].astype(F32)
            out[:, columns] = grad.astype(BF16)
    if fold:
        recv = rest.pop(0)
        gate_o, up_o, down_o = outs[len(turns) :]
        for grad, columns, out in zip(terms(0), parts, (gate_o, up_o)):
            out[...] = grad + recv[:, columns].astype(F32)
        down = lax.dot_general(q[...], g[0], TN, preferred_element_type=F32)
        down_o[...] = down + recv[:, parts[2]].astype(F32).T


def unit_term(n2, g, dga, dup, q, turns, fold, after, weight):
    block, share = n2.shape[2], q.shape[1]
    arrived = [item for _, item in turns if item is not None] + ([] if fold is None else [fold])
    plan = [(o, item is not None) for o, item in turns]
    out = [shaped((block, 3 * share), BF16) for _ in turns]
    if fold is not None:
        out += [shaped((block, share), F32), shaped((block, share), F32), shaped((share, block), F32)]
    return launch(
        lambda *refs: unit_term_kernel(plan, fold is not None, *refs),
        (n2, g, dga, dup, q, *arrived),
        tuple(out),
        "unit_term",
        after=after,
        mib=10,
        flops=weight,
    )


def unit_end_kernel(count, *refs):
    own, item, low, outs = refs[:3], refs[3], refs[4 : 4 + count], refs[4 + count :]
    share = own[0].shape[1]
    for i in range(2):
        total = own[i][...] + item[:, i * share : (i + 1) * share].astype(F32)
        if count:
            outs[i][:, :share] = low[i][...]
            outs[i][:, share:] = total
        else:
            outs[i][...] = total
    total = own[2][...] + item[:, 2 * share :].astype(F32).T
    if count:
        outs[2][:share, :] = low[2][...]
        outs[2][share:, :] = total
    else:
        outs[2][...] = total


def unit_end(low, own, item, after):
    block, share = own[0].shape
    wide = 2 if low else 1
    grad = shaped((block, wide * share), F32)
    return launch(
        lambda *refs: unit_end_kernel(len(low), *refs),
        (*own, item, *low),
        (grad, grad, shaped((wide * share, block), F32)),
        "unit_end",
        after=after,
        flops=END_WEIGHT,
    )


def small_pieces(width, block):
    return [slice(i, min(i + block, width)) for i in range(0, width, block)]


def mixer_term_kernel(part, places, groups, split, chunk, turns, fold, owners, *refs):
    n1_all = refs[:groups]
    dhr, grads, p = refs[groups : groups + 3]
    rest = list(refs[groups + 3 :])
    extra = rest.pop(0) if part == 0 else None
    outs = rest[len(rest) - len(turns) - (3 - part if fold else 0) :]
    width, block = grads.shape[1], dhr.shape[2]
    columns = slice(0, split) if part == 0 else slice(split, width)
    size = columns.stop - columns.start
    at = width + size
    pieces = small_pieces(width, block)

    def terms(o, recv):
        group, i = places[o]
        grad = lax.dot_general(grads[...], n1_all[group][i], TN, preferred_element_type=F32)
        out = lax.dot_general(p[:, columns], dhr[o], TN, preferred_element_type=F32)
        if recv is not None:
            grad = grad + recv[:width, :].astype(F32)
            out = out + recv[width:at, :].astype(F32)
        return grad, out

    def small(o, recv):
        own = extra[pl.ds(pl.multiple_of(owners[o] * chunk, 16), chunk), :].astype(F32)
        out = []
        for i, piece in enumerate(pieces):
            total = own[:, piece]
            if recv is not None:
                total = total + recv[at + i * chunk : at + (i + 1) * chunk, : piece.stop - piece.start].astype(F32)
            out.append(total)
        return out

    for (o, has), out_ref in zip(turns, outs):
        recv = rest.pop(0) if has else None
        grad, out = terms(o, recv)
        out_ref[:width, :] = grad.astype(BF16)
        out_ref[width:at, :] = out.astype(BF16)
        if part == 0:
            for i, total in enumerate(small(o, recv)):
                rows = slice(at + i * chunk, at + (i + 1) * chunk)
                wide = total.shape[1]
                out_ref[rows, :wide] = total.astype(BF16)
                if wide < block:
                    out_ref[rows, wide:] = jnp.zeros((chunk, block - wide), BF16)
    if fold:
        recv = rest.pop(0)
        outs[len(turns)][...], outs[len(turns) + 1][...] = terms(0, recv)
        if part == 0:
            for piece, total in zip(pieces, small(0, recv)):
                outs[len(turns) + 2][:, piece] = total


def mixer_term(part, places, split, chunk, owners, n1, dhr, grads, p, extra, turns, fold, after, weight):
    block, width = dhr.shape[2], grads.shape[1]
    size = split if part == 0 else width - split
    arrived = [item for _, item in turns if item is not None] + ([] if fold is None else [fold])
    more = 0 if part == 1 else chunk * len(small_pieces(width, block))
    out = [shaped((width + size + more, block), BF16) for _ in turns]
    if fold is not None:
        out += [shaped((width, block), F32), shaped((size, block), F32)]
        out += [shaped((chunk, width), F32)] if part == 0 else []
    plan = [(o, item is not None) for o, item in turns]
    return launch(
        lambda *refs: mixer_term_kernel(part, places, len(n1), split, chunk, plan, fold is not None, *refs),
        (owners, *n1, dhr, grads, p, *([extra] if part == 0 else []), *arrived),
        tuple(out),
        "mixer_term",
        scalars=1,
        after=after,
        mib=10,
        flops=weight,
    )


def mixer_end_kernel(part, *refs):
    own, item = refs[: 3 - part], refs[3 - part]
    extra, outs = refs[4 - part : 6 - 2 * part], refs[6 - 2 * part :]
    width, block = own[0].shape
    at = width + own[1].shape[0]
    outs[0][...] = own[0][...] + item[:width, :].astype(F32)
    total = own[1][...] + item[width:at, :].astype(F32)
    if part == 1:
        low = extra[0]
        split = low.shape[0]
        outs[1][:split, :] = low[...]
        outs[1][split:, :] = total
        return
    outs[1][...] = total
    chunk = own[2].shape[0]
    for i, piece in enumerate(small_pieces(width, block)):
        rows = slice(at + i * chunk, at + (i + 1) * chunk)
        total = own[2][:, piece] + item[rows, : piece.stop - piece.start].astype(F32)
        outs[2][:chunk, piece] = total.astype(BF16)
    ring_size = extra[0].shape[0]
    lines = jnp.concatenate([extra[0][o] + extra[1][o] for o in range(ring_size)], 0)
    outs[2][chunk:, :block] = lines.astype(BF16)
    outs[2][chunk:, block:] = jnp.zeros((2 * ring_size, width - block), BF16)


def mixer_end(part, extra, own, item, after):
    width, block = own[0].shape
    if part == 0:
        rows = own[2].shape[0] + 2 * extra[0].shape[0]
        shapes = [own[0].shape, own[1].shape, (rows, width)]
    else:
        shapes = [own[0].shape, own[0].shape]
    return launch(
        lambda *refs: mixer_end_kernel(part, *refs),
        (*own, item, *extra),
        tuple(shaped(shape, BF16 if i == 2 else F32) for i, shape in enumerate(shapes)),
        "mixer_end",
        after=after,
        flops=HEAVY,
    )


def spread_kernel(head, owners, *refs):
    ring_size = owners.shape[0]
    gate_i, gate_r, taps, sums, gain_o, whole = refs[ring_size:]
    block = gain_o.shape[1]
    chunk = refs[0].shape[0] - 2 * ring_size
    gain = jnp.zeros((2, block), F32)
    for o in range(ring_size):
        at = pl.ds(pl.multiple_of(owners[o] * chunk, 16), chunk)
        whole[at, :] = refs[o][:chunk, :].astype(F32)
        mine = 2 * ((ring_size - o) % ring_size)
        gain = gain + refs[o][chunk:, :block].astype(F32)[mine : mine + 2, :]
    gate_i[...] = whole[:head, :]
    gate_r[...] = whole[head : 2 * head, :]
    count = taps.shape[0]
    taps[...] = whole[2 * head : 2 * head + count, :]
    sums[...] = whole[2 * head + count : 2 * head + SUMS, :]
    gain_o[...] = gain


def spread(head, count, block, owners, chunks, after):
    ring_size = len(chunks)
    rows, width = chunks[0].shape
    gate = shaped((head, width), F32)
    return launch(
        lambda *refs: spread_kernel(head, *refs),
        (owners, *chunks),
        (gate, gate, shaped((count, width), F32), shaped((SUMS - count, width), F32), shaped((2, block), F32)),
        "spread",
        scalars=1,
        after=after,
        scratch=[pltpu.VMEM(((rows - 2 * ring_size) * ring_size, width), F32)],
    )


def local(
    tokens,
    cotangent,
    row_length,
    first_gain,
    value_weight,
    gelu_weight,
    conv_weight,
    conv_bias,
    input_gate,
    input_bias,
    recur_gate,
    recur_bias,
    decay_param,
    output_weight,
    second_gain,
    mlp_gate,
    mlp_up,
    mlp_down,
):
    ring_size = lax.axis_size("dp")
    middle = ring_size // 2
    ring = [2 * i if i < middle else 2 * (ring_size - 1 - i) + 1 for i in range(ring_size)]
    onward = [(ring[i], ring[(i + 1) % ring_size]) for i in range(ring_size)]
    backward = [(b, a) for a, b in onward]
    me = lax.axis_index("dp")
    core = lax.axis_index("mp") % 2
    core_pair = [(i, i ^ 1) for i in range(4)]
    chip_pair = [(i, i ^ 2) for i in range(4)]
    index = jnp.arange(ring_size, dtype=jnp.int32)

    def spot_of(place):
        return jnp.where(place % 2 == 0, place // 2, ring_size - 1 - place // 2)

    spots = (spot_of(me) + index) % ring_size
    owners = jnp.where(spots < middle, 2 * spots, 2 * (ring_size - 1 - spots) + 1).astype(jnp.int32)
    slots = ((spot_of(index) - spot_of(me) + ring_size) % ring_size).astype(jnp.int32)

    subs, row_count, length, model = tokens.shape
    half = row_count * length
    seqs = subs * row_count
    block = model // ring_size
    width, head = input_gate.shape
    count = conv_weight.shape[0]
    split = width // 2 // 128 * 128
    chunk = -(-(2 * head + SUMS) // (16 * ring_size)) * 16
    small_rows = chunk * ring_size

    def hops(long_way_on):
        return (middle, ring_size - 1 - middle) if long_way_on else (ring_size - 1 - middle, middle)

    token = []

    def mark(*values):
        token[:] = values

    class Gather:
        def __init__(self, shard, long_way_on):
            self.hops = hops(long_way_on)
            self.moving = [shard, shard]
            self.got = [shard] + [None] * (ring_size - 1)

        def step(self, s):
            for d, way in enumerate((onward, backward)):
                if s <= self.hops[d]:
                    self.moving[d] = lax.ppermute(self.moving[d], "dp", way)
                    self.got[ring_size - s if d == 0 else s] = self.moving[d]

    class Scatter:
        def __init__(self, term, end, long_way_on):
            self.term, self.ending = term, end
            self.hops = hops(long_way_on)
            self.moving = [None, None]
            self.own = None

        def step(self, s, weight=HEAVY, apart=False):
            turns, ways, fold = [], [], None
            for d in range(2):
                far = self.hops[d] - s
                if far > 0:
                    turns.append((far if d == 0 else ring_size - far, self.moving[d]))
                    ways.append(d)
                elif far == 0:
                    fold = self.moving[d]
            parts = self.term(turns, None if apart else fold, tuple(token), weight)
            mark(parts[0])
            for d, part in zip(ways, parts):
                self.moving[d] = lax.ppermute(part, "dp", (onward, backward)[d])
            if fold is not None:
                self.own = parts[len(turns) :]
                if apart:
                    self.own = self.term([], fold, tuple(token), weight)
                    mark(self.own[0])

        def end(self, *low):
            last = 0 if self.hops[0] > self.hops[1] else 1
            out = self.ending(low, self.own, self.moving[last], tuple(token))
            mark(out[0])
            return out

    def core_swap(other):
        return lax.ppermute(other, "mp", core_pair)

    def chip_swap(own, got, after):
        pair = pair_sum(own, got, after)
        mark(pair)
        return pair, lax.ppermute(pair, "mp", chip_pair)

    def both_halves(own, dim):
        return jnp.concatenate([own, lax.ppermute(own, "mp", core_pair)], dim)

    scalars = jnp.concatenate([core[None], row_length.reshape(-1)]).astype(jnp.int32)
    shard_one, shard_two = pack(
        split, value_weight.T, gelu_weight.T, output_weight, first_gain[None], second_gain[None]
    )
    ring_one, ring_two = Gather(shard_one, True), Gather(shard_two, False)
    ring_one.step(1)
    ring_two.step(1)

    decay_wide = decay_param.astype(F32)
    lines = jnp.concatenate(
        [
            conv_weight.astype(F32),
            jnp.stack(
                [
                    conv_bias.astype(F32),
                    input_bias.astype(F32),
                    recur_bias.astype(F32),
                    jax.nn.softplus(-decay_wide),
                    jax.nn.sigmoid(-decay_wide),
                ]
            ),
        ]
    )
    x, g, g_flat, r1, blocks_i, blocks_r = prepare(
        scalars,
        slots,
        tokens.reshape(subs, half, model),
        cotangent.reshape(subs, half, model),
        input_gate.T,
        recur_gate.T,
        (lines,),
    )
    x, *moved = lax.optimization_barrier((x, *ring_one.moving, *ring_two.moving))
    ring_one.moving, ring_two.moving = moved[:2], moved[2:]
    for s in range(2, middle + 1):
        ring_one.step(s)
        ring_two.step(s)
    one, two = ring_one.got, ring_two.got

    hop_groups = [[0, 1, ring_size - 1]] + [[s, ring_size - s] for s in range(2, middle)] + [[middle]]
    places, n1, sums_so_far = {}, [], None
    for place, offsets in enumerate(hop_groups):
        bx, by, n1_part = project(
            offsets, x, r1, [one[o] for o in offsets], [two[o] for o in offsets], sums_so_far, width, split
        )
        sums_so_far = (bx, by)
        n1.append(n1_part)
        places |= {o: (place, i) for i, o in enumerate(offsets)}

    p, cx, lx, lr, h = mixer_forward(seqs, count, bx, by, lines, blocks_i, blocks_r)
    cut = ring_size // 2 + 1
    own_a, other_a, gains_a = mixer_out(p, one[:cut], two[:cut], split, ())
    got_a = core_swap(other_a)
    own_b, other_b, gains_b = mixer_out(p, one[cut:], two[cut:], split, (own_a,))
    sums_a = chip_swap(own_a, got_a, (own_b,))
    sums_b = chip_swap(own_b, core_swap(other_b), tuple(token))
    gains = jnp.concatenate([gains_a, gains_b])
    dq = unit_grad(g_flat, mlp_down, tuple(token))
    fetched = fetch(mlp_gate, mlp_up, (dq,))
    h1, n2_own, r2 = norm(slots, x, gains, (*sums_a, *sums_b), (fetched[0],))
    n2 = both_halves(n2_own, 0)
    q_a, dga_a, dup_a, n2_rel = unit_first(slots, n2, *fetched, dq)
    unit_a = Scatter(lambda *a: unit_term(n2_rel, g, dga_a, dup_a, q_a, *a), unit_end, True)
    unit_a.step(0)
    q_b, dga_b, dup_b = unit_second(n2, mlp_gate, mlp_up, dq, tuple(token))
    unit_b = Scatter(lambda *a: unit_term(n2_rel, g, dga_b, dup_b, q_b, *a), unit_end, False)
    unit_b.step(0, 1)
    last = middle - 1

    def now():
        return tuple(token)

    own, other = unit_back(owners, (dga_a, dga_b, dup_a, dup_b), mlp_gate, mlp_up, now())
    mark(own)
    got = core_swap(other)
    for s in range(1, max(last - 1, 1)):
        unit_a.step(s)
        if s == 1:
            pair, other = chip_swap(own, got, now())
        unit_b.step(s)
    unit_a.step(last - 1)
    dh1, dhr_own, second_grad = norm_back(pair, other, h1, r2, gains, g, now())
    mark(dhr_own)
    dhr = both_halves(dhr_own, 1)
    unit_b.step(last - 1)
    dbx, dby, small = mixer_backward(
        seqs, head, count, split, small_rows, dhr, two, (bx, by, cx, lx, lr, h, lines, blocks_i, blocks_r), now()
    )
    mark(dbx)
    half_split = width // 2 // 128 * 128
    mixer_a = Scatter(
        lambda *a: mixer_term(0, places, half_split, chunk, owners, n1, dhr, dbx, p, small, *a),
        lambda *a: mixer_end(0, *a),
        True,
    )
    mixer_b = Scatter(
        lambda *a: mixer_term(1, places, half_split, chunk, owners, n1, dhr, dby, p, None, *a),
        lambda *a: mixer_end(1, *a),
        False,
    )
    mixer_a.step(0)
    unit_a.step(last)
    out_own, out_other = unit_out(q_a, q_b, mlp_down, now())
    mark(out_own)
    layer_pair = pair_sum(out_own, core_swap(out_other), now())
    mark(layer_pair)
    own, other = input_out(dbx, dby, one, two, split, now())
    mark(own)
    got = core_swap(other)
    unit_b.step(last)
    pair, other = chip_swap(own, got, now())
    mixer_a.step(1)
    low = unit_a.end()
    mixer_b.step(0, 1)
    gate_grad, up_grad, down_grad = unit_b.end(*low)
    input_own, gain_grads = input_back(slots, pair, other, x, r1, gains, dh1, second_grad, now())
    mark(input_own)
    layer_pair = relay(layer_pair, now())
    mark(layer_pair)
    layer_other = lax.ppermute(layer_pair, "mp", chip_pair)
    gain_got = core_swap(gain_grads)
    for s in range(2, middle):
        mixer_a.step(s)
        if s == middle - 1:
            both_own = finish(slots, h1, layer_pair, layer_other, input_own, now())
            mark(both_own)
        mixer_b.step(s - 1)
    input_grad, layer_out = arrange(scalars, both_own, core_swap(both_own), now())
    mark(layer_out)
    value_grad, output_low, small = mixer_a.end(gain_grads, gain_got)
    small_ring = Gather(small, True)
    mixer_b.step(last, 1, True)
    for s in range(1, middle + 1):
        small_ring.step(s)
    gelu_grad, output_grad = mixer_b.end(output_low)
    gate_i, gate_r, taps_grad, sums, gain_grads = spread(head, count, block, owners, small_ring.got, now())

    return (
        layer_out.reshape(tokens.shape),
        input_grad.reshape(tokens.shape),
        gain_grads[0],
        value_grad.T,
        gelu_grad.T,
        taps_grad,
        sums[0],
        gate_i.T,
        sums[1],
        gate_r.T,
        sums[2],
        sums[3],
        output_grad,
        gain_grads[1],
        gate_grad,
        up_grad,
        down_grad,
    )


def solution(mesh):
    placed = (
        P(None, "dp", None, None),
        P(None, "dp", None, None),
        P(None, "dp"),
        P("dp"),
        P("dp", "mp"),
        P("dp", "mp"),
        P(None, "mp"),
        P("mp"),
        P("mp", None),
        P("mp"),
        P("mp", None),
        P("mp"),
        P("mp"),
        P("mp", "dp"),
        P("dp"),
        P(None, "mp"),
        P(None, "mp"),
        P("mp", None),
    )
    return jax.shard_map(
        local,
        mesh=mesh,
        in_specs=placed,
        out_specs=(
            P(None, "dp", None, None),
            P(None, "dp", None, None),
            P("dp"),
            P("dp", "mp"),
            P("dp", "mp"),
            P(None, "mp"),
            P("mp"),
            P("mp", None),
            P("mp"),
            P("mp", None),
            P("mp"),
            P("mp"),
            P("mp", "dp"),
            P("dp"),
            P("dp", "mp"),
            P("dp", "mp"),
            P("mp", "dp"),
        ),
        check_vma=False,
    )
```

```python
import jax
import jax.numpy as jnp
from jax import lax
from jax.experimental import pallas as pl
from jax.experimental.pallas import tpu as pltpu
from jax.sharding import PartitionSpec as P

EPSILON = 1e-06
DECAY_SCALE = 8.0
GELU_A = 0.7978845608028654
GELU_B = 0.044715
BF16 = jnp.bfloat16
F32 = jnp.float32
STEP = 16
HALF = 8
SUMS = 8
HEAVY = 100 * 10**9
END_WEIGHT = 1
TN = (((0,), (0,)), ((), ()))
NT = (((1,), (1,)), ((), ()))


def gelu(v):
    return 0.5 * v * (1.0 + jnp.tanh(GELU_A * (v + GELU_B * v * v * v)))


def gelu_both(v):
    squared = v * v
    bent = jnp.tanh(GELU_A * v * (1.0 + GELU_B * squared))
    value = 0.5 * v * (1.0 + bent)
    slope = 0.5 * (1.0 + bent) + 0.5 * v * (1.0 - bent * bent) * GELU_A * (
        1.0 + 3.0 * GELU_B * squared
    )
    return value, slope


def negative_expm1(z, exp_z):
    series = 1.0 + z * (1.0 / 7.0)
    for k in (6.0, 5.0, 4.0, 3.0, 2.0):
        series = 1.0 + z * (1.0 / k) * series
    return jnp.where(z > -0.25, -z * series, 1.0 - exp_z)


def rows_of(shape):
    return lax.broadcasted_iota(jnp.int32, shape, 0)


def earlier(now, before, k, rows):
    return jnp.where(rows < k, pltpu.roll(before, k, 0), pltpu.roll(now, k, 0))


def later(now, after, k, rows):
    size = now.shape[0]
    return jnp.where(
        rows >= size - k, pltpu.roll(after, size - k, 0), pltpu.roll(now, size - k, 0)
    )


def shaped(shape, dtype):
    return jax.ShapeDtypeStruct(shape, dtype)


def launch(
    kernel, inputs, out_shape, name, scalars=0, after=(), mib=10, scratch=(), aliases=None, grid=None, flops=1
):
    count, extra = len(inputs), len(after)
    waits = [pl.BlockSpec(memory_space=pl.ANY)] * extra
    in_specs = [pl.BlockSpec(memory_space=pltpu.SMEM)] * scalars
    more = {}
    if grid is None:
        in_specs += [pl.BlockSpec(memory_space=pltpu.VMEM)] * (count - scalars)
    else:
        in_specs += grid[1]
        more = {"grid": grid[0], "out_specs": grid[2]}
    return pl.pallas_call(
        lambda *refs: kernel(*refs[:count], *refs[count + extra :]),
        in_specs=in_specs + waits,
        out_shape=out_shape,
        scratch_shapes=list(scratch),
        input_output_aliases=aliases or {},
        compiler_params=pltpu.CompilerParams(vmem_limit_bytes=mib << 20),
        cost_estimate=pl.CostEstimate(flops=flops, bytes_accessed=1, transcendentals=0),
        name=name,
        **more,
    )(*inputs, *after)


def in_hbm(array):
    return pltpu.with_memory_space_constraint(array, pltpu.HBM)


def mixer_forward_kernel(
    seqs, count, bx, by, lines, blocks_i, blocks_r, p_o, cx_o, lx_o, lr_o, h_o
):
    total, width = bx.shape
    length = total // seqs
    steps = length // STEP
    rows16 = rows_of((STEP, width))
    w = [jnp.broadcast_to(lines[k : k + 1, :], (STEP, width)) for k in range(count)]
    shift = jnp.broadcast_to(lines[count : count + 1, :], (STEP, width))
    bias_i, bias_r = lines[count + 1 : count + 2, :], lines[count + 2 : count + 3, :]
    soft = lines[count + 3 : count + 4, :]
    for seq in range(seqs):

        def conv(i, before):
            at = pl.ds(pl.multiple_of(seq * length + i * STEP, STEP), STEP)
            now = bx[at, :]
            mixed = shift + w[0] * now
            for k in range(1, count):
                mixed = mixed + w[k] * earlier(now, before, k, rows16)
            cx_o[at, :] = mixed.astype(BF16)
            return now

        lax.fori_loop(0, steps, conv, jnp.zeros((STEP, width), F32), unroll=2)
    lx_o[...] = lax.dot_general(cx_o[...], blocks_i[...], NT, preferred_element_type=F32) + bias_i
    lr_o[...] = lax.dot_general(cx_o[...], blocks_r[...], NT, preferred_element_type=F32) + bias_r
    rows8 = rows_of((HALF, width))
    soft8 = jnp.broadcast_to(-DECAY_SCALE * soft, (HALF, width))

    def scan(i, carries):
        out = []
        for seq in range(seqs):
            carry = carries[seq]
            base = seq * length + i * STEP
            at = pl.ds(pl.multiple_of(base, STEP), STEP)
            cx16 = cx_o[at, :].astype(F32)
            products = []
            for part in range(STEP // HALF):
                here = pl.ds(pl.multiple_of(base + part * HALF, HALF), HALF)
                cx = cx16[part * HALF : (part + 1) * HALF, :]
                ix = jax.nn.sigmoid(lx_o[here, :])
                la = soft8 * jax.nn.sigmoid(lr_o[here, :])
                a = jnp.exp(la)
                rest = negative_expm1(2.0 * la, a * a)
                m = jnp.where(rest > 0.0, rest * lax.rsqrt(rest), 0.0)
                u = m * ix * cx
                for s in (1, 2, 4):
                    keep = rows8 >= s
                    u = u + jnp.where(keep, a * pltpu.roll(u, s, 0), 0.0)
                    a = jnp.where(keep, a * pltpu.roll(a, s, 0), a)
                h = u + a * carry
                carry = jnp.broadcast_to(h[HALF - 1 : HALF, :], (HALF, width))
                h_o[here, :] = h
                products.append(h * gelu(by[here, :]))
            p_o[at, :] = jnp.concatenate(products, 0).astype(BF16)
            out.append(carry)
        return tuple(out)

    lax.fori_loop(0, steps, scan, tuple(jnp.zeros((HALF, width), F32) for _ in range(seqs)), unroll=4)


def mixer_forward(seqs, count, bx, by, lines, blocks_i, blocks_r):
    low, full = shaped(bx.shape, BF16), shaped(bx.shape, F32)
    return launch(
        lambda *refs: mixer_forward_kernel(seqs, count, *refs),
        (bx, by, lines, blocks_i, blocks_r),
        (low, low, full, full, full),
        "mixer_forward",
    )


def mixer_backward_kernel(seqs, head, count, split, dhr, *refs):
    ring_size = dhr.shape[0]
    second = refs[:ring_size]
    bx, by, cx_i, lx_i, lr_i, h_i, lines, blocks_i, blocks_r = refs[ring_size : ring_size + 9]
    dbx_o, dby_o, small_o, dlx_o, dlr_o, dcx_s, dp = refs[ring_size + 9 :]
    skip = bx.shape[1] - split
    soft, gate_soft = lines[count + 3 : count + 4, :], lines[count + 4 : count + 5, :]
    for o in range(ring_size):
        part = lax.dot_general(dhr[o], second[o][skip:, :], NT, preferred_element_type=F32)
        dp[...] = part if o == 0 else dp[...] + part
    total, width = bx.shape
    length = total // seqs
    steps = length // STEP
    rows8 = rows_of((HALF, width))
    soft8 = jnp.broadcast_to(-DECAY_SCALE * soft, (HALF, width))
    zero = jnp.zeros((HALF, width), F32)

    def scan(j, state):
        i = steps - 1 - j
        sums_i, sums_r, sums_d = state[0]
        out = []
        for seq in range(seqs):
            a_after, e_after = state[1][seq]
            base = seq * length + i * STEP
            at = pl.ds(pl.multiple_of(base, STEP), STEP)
            cx16 = cx_i[at, :].astype(F32)
            dby_parts, dlx_parts, dlr_parts = [None, None], [None, None], [None, None]
            for part in (1, 0):
                start = base + part * HALF
                here = pl.ds(pl.multiple_of(start, HALF), HALF)
                cx = cx16[part * HALF : (part + 1) * HALF, :]
                ix = jax.nn.sigmoid(lx_i[here, :])
                ra = jax.nn.sigmoid(lr_i[here, :])
                la = soft8 * ra
                a = jnp.exp(la)
                rest = negative_expm1(2.0 * la, a * a)
                inverse = lax.rsqrt(rest)
                m = rest * inverse
                h = h_i[here, :]
                first = (i == 0) if part == 0 else False
                back = jnp.maximum(start - HALF, 0)
                before = h_i[pl.ds(pl.multiple_of(back, HALF), HALF), :]
                if part == 0:
                    before = jnp.where(i == 0, 0.0, before)
                h_prev = earlier(h, before, 1, rows8)
                gy, slope = gelu_both(by[here, :])
                grad = dp[here, :]
                dby_parts[part] = grad * h * slope
                e = grad * gy
                f = later(a, a_after, 1, rows8)
                for s in (1, 2, 4):
                    keep = rows8 < HALF - s
                    e = e + jnp.where(keep, f * pltpu.roll(e, HALF - s, 0), 0.0)
                    f = jnp.where(keep, f * pltpu.roll(f, HALF - s, 0), f)
                e = e + f * e_after
                e_after = jnp.broadcast_to(e[0:1, :], (HALF, width))
                a_after = a
                eix = e * ix
                dla = (e * h_prev - eix * cx * a * inverse) * a
                dlx = eix * m * cx * (1.0 - ix)
                dlr = dla * la * (1.0 - ra)
                sums_i = sums_i + dlx
                sums_r = sums_r + dlr
                sums_d = sums_d + dla * ra
                dlx_parts[part], dlr_parts[part] = dlx, dlr
                dcx_s[here, :] = eix * m
            dby_o[at, :] = jnp.concatenate(dby_parts, 0).astype(BF16)
            dlx_o[at, :] = jnp.concatenate(dlx_parts, 0).astype(BF16)
            dlr_o[at, :] = jnp.concatenate(dlr_parts, 0).astype(BF16)
            out.append((a_after, e_after))
        return (sums_i, sums_r, sums_d), tuple(out)

    (sums_i, sums_r, sums_d), _ = lax.fori_loop(
        0, steps, scan, ((zero, zero, zero), tuple((zero, zero) for _ in range(seqs)))
    )
    dcx_s[...] += jnp.dot(dlx_o[...], blocks_i[...], preferred_element_type=F32) + jnp.dot(
        dlr_o[...], blocks_r[...], preferred_element_type=F32
    )
    rows16 = rows_of((STEP, width))
    w = [jnp.broadcast_to(lines[k : k + 1, :], (STEP, width)) for k in range(count)]
    zero16 = jnp.zeros((STEP, width), F32)
    sums_t = tuple(zero16 for _ in range(count))
    sums_b = zero16
    for seq in range(seqs):

        def conv(j, state):
            after, tap_sums, shift_sum = state
            at = pl.ds(pl.multiple_of(seq * length + (steps - 1 - j) * STEP, STEP), STEP)
            now = dcx_s[at, :]
            source = bx[at, :]
            grad = w[0] * now
            new_sums = [tap_sums[0] + now * source]
            for k in range(1, count):
                moved = later(now, after, k, rows16)
                grad = grad + w[k] * moved
                new_sums.append(tap_sums[k] + moved * source)
            dbx_o[at, :] = grad.astype(BF16)
            return now, tuple(new_sums), shift_sum + now

        _, sums_t, sums_b = lax.fori_loop(0, steps, conv, (zero16, sums_t, sums_b))
    rows = [jnp.sum(item, 0, keepdims=True) for item in (*sums_t, sums_b, sums_i, sums_r)]
    rows.append(DECAY_SCALE * gate_soft * jnp.sum(sums_d, 0, keepdims=True))
    spare = small_o.shape[0] - 2 * head - SUMS
    if spare:
        rows.append(jnp.zeros((spare, width), F32))
    small_o[2 * head :, :] = jnp.concatenate(rows, 0).astype(BF16)
    lanes = lax.broadcasted_iota(jnp.int32, (head, width), 1)
    for gate, grads in enumerate((dlx_o, dlr_o)):
        whole = lax.dot_general(grads[...], cx_i[...], TN, preferred_element_type=F32)
        picked = whole[:head]
        for i in range(1, width // head):
            picked = jnp.where(lanes < i * head, picked, whole[i * head : (i + 1) * head])
        small_o[gate * head : (gate + 1) * head, :] = picked.astype(BF16)


def mixer_backward(seqs, head, count, split, small_rows, dhr, second, saved, after):
    total, width = saved[0].shape
    low = shaped((total, width), BF16)
    return launch(
        lambda *refs: mixer_backward_kernel(seqs, head, count, split, *refs),
        (dhr, *second, *saved),
        (low, low, shaped((small_rows, width), BF16)),
        "mixer_backward",
        after=after,
        mib=18,
        scratch=[
            pltpu.VMEM((total, width), BF16),
            pltpu.VMEM((total, width), BF16),
            pltpu.VMEM((total, width), F32),
            pltpu.VMEM((total, width), F32),
        ],
    )


def copy_all(pairs, sems):
    copies = [
        pltpu.make_async_copy(source, target, sems.at[i]) for i, (source, target) in enumerate(pairs)
    ]
    for copy in copies:
        copy.start()
    return copies


def pack_two_kernel(split, gelu_w, output, two_o, sems):
    width = gelu_w.shape[0]
    pairs = (
        (gelu_w.at[pl.ds(split, width - split)], two_o.at[pl.ds(0, width - split)]),
        (output, two_o.at[pl.ds(width - split, width)]),
    )
    for copy in copy_all(pairs, sems):
        copy.wait()


def pack_one_kernel(split, gain_one, gain_two, value, gelu_w, one_o, sems):
    width = value.shape[0]
    pairs = (
        (value, one_o.at[pl.ds(0, width)]),
        (gelu_w.at[pl.ds(0, split)], one_o.at[pl.ds(width + 16, split)]),
    )
    copies = copy_all(pairs, sems)
    spare = jnp.zeros((14, value.shape[1]), F32)
    lines = jnp.concatenate([gain_one[...].astype(F32), gain_two[...].astype(F32), spare], 0)
    one_o[width : width + 16, :] = lines.astype(BF16)
    for copy in copies:
        copy.wait()


def pack(split, value, gelu_w, output, gain_one, gain_two):
    width, block = value.shape
    whole = pl.BlockSpec(memory_space=pltpu.VMEM)
    anywhere = pl.BlockSpec(memory_space=pl.ANY)
    value, gelu_w, output = in_hbm(value), in_hbm(gelu_w), in_hbm(output)
    two = launch(
        lambda *refs: pack_two_kernel(split, *refs),
        (gelu_w, output),
        shaped((2 * width - split, block), BF16),
        "pack_two",
        scratch=[pltpu.SemaphoreType.DMA((2,))],
        grid=((), [anywhere, anywhere], whole),
    )
    one = launch(
        lambda *refs: pack_one_kernel(split, *refs),
        (gain_one, gain_two, value, gelu_w),
        shaped((width + 16 + split, block), BF16),
        "pack_one",
        after=(two,),
        scratch=[pltpu.SemaphoreType.DMA((2,))],
        grid=((), [whole, whole, anywhere, anywhere], whole),
    )
    return one, two


def prepare_kernel(scalars, slots, tokens, cotangent, gate_i, gate_r, x_o, g_o, flat_o, r_o, blocks_i, blocks_r):
    ring_size, total, block = x_o.shape
    half = total // 2
    row_count = (scalars.shape[0] - 1) // 2
    length = half // row_count
    rows = lax.broadcasted_iota(jnp.int32, (length, block), 0)
    for place in range(2):
        sub = scalars[0] if place == 0 else 1 - scalars[0]
        for row in range(row_count):
            at = slice(place * half + row * length, place * half + (row + 1) * length)
            source = pl.ds(row * length, length)
            valid = jnp.where(rows < scalars[1 + sub * row_count + row], 1.0, 0.0)
            squares = jnp.zeros((length, block), F32)
            for k in range(ring_size):
                columns = slice(k * block, (k + 1) * block)
                piece = tokens[sub, source, columns]
                wide = piece.astype(F32)
                squares = squares + wide * wide
                x_o[slots[k], at, :] = piece
                masked = (cotangent[sub, source, columns].astype(F32) * valid).astype(BF16)
                g_o[slots[k], at, :] = masked
                flat_o[at, columns] = masked
            mean = jnp.sum(squares, 1, keepdims=True) * (1.0 / (ring_size * block))
            r_o[at, :] = lax.rsqrt(mean + EPSILON)
    head, width = gate_i.shape
    lanes = lax.broadcasted_iota(jnp.int32, (head, width), 1)
    for source, out in ((gate_i, blocks_i), (gate_r, blocks_r)):
        wide = source[...].astype(F32)
        for i in range(width // head):
            inside = (lanes >= i * head) & (lanes < (i + 1) * head)
            out[i * head : (i + 1) * head, :] = jnp.where(inside, wide, 0.0).astype(BF16)


def prepare(scalars, slots, tokens, cotangent, gate_i, gate_r, after):
    subs, half, model = tokens.shape
    total, ring_size, width = subs * half, slots.shape[0], gate_i.shape[1]
    rel = shaped((ring_size, total, model // ring_size), BF16)
    blocks = shaped((width, width), BF16)
    return launch(
        prepare_kernel,
        (scalars, slots, tokens, cotangent, gate_i, gate_r),
        (rel, rel, shaped((total, model), BF16), shaped((total, 1), F32), blocks, blocks),
        "prepare",
        scalars=2,
        after=after,
    )


def project_kernel(offsets, first, width, split, x, r1, *refs):
    count = len(offsets)
    one, two = refs[:count], refs[count : 2 * count]
    rest = refs[2 * count :]
    if not first:
        before = rest[:2]
        rest = rest[2:]
    bx, by, n1_o = rest
    scale = r1[...]
    for i, o in enumerate(offsets):
        gain = one[i][width : width + 16, :].astype(F32)[0:1, :]
        n1 = (x[o].astype(F32) * scale * gain).astype(BF16)
        n1_o[i] = n1
        for out, place, columns, weight in (
            (bx, 0, slice(0, width), one[i][:width, :]),
            (by, 1, slice(0, split), one[i][width + 16 :, :]),
            (by, 1, slice(split, width), two[i][: width - split, :]),
        ):
            part = lax.dot_general(n1, weight, NT, preferred_element_type=F32)
            if i > 0:
                out[:, columns] += part
            elif first:
                out[:, columns] = part
            else:
                out[:, columns] = before[place][:, columns] + part


def project(offsets, x, r1, one, two, before, width, split):
    total, block = x.shape[1:]
    count = len(offsets)
    full = shaped((total, width), F32)
    at = 2 + 2 * count
    return launch(
        lambda *refs: project_kernel(offsets, before is None, width, split, *refs),
        (x, r1, *one, *two, *(before or ())),
        (full, full, shaped((count, total, block), BF16)),
        "project",
        aliases={} if before is None else {at: 0, at + 1: 1},
    )


def mixer_out_kernel(skip, p, *refs):
    own_o, other_o, gains_o = refs[-3:]
    count, half = own_o.shape[:2]
    width = p.shape[1]
    for o in range(count):
        part = jnp.dot(p[...], refs[count + o][skip:, :], preferred_element_type=F32)
        own_o[o] = part[:half]
        other_o[o] = part[half:].astype(BF16)
        gains_o[o] = refs[o][width : width + 16, :].astype(F32)[0:2, :]


def mixer_out(p, one, two, split, after):
    total, width = p.shape
    count, block = len(one), one[0].shape[1]
    shape = (count, total // 2, block)
    return launch(
        lambda *refs: mixer_out_kernel(width - split, *refs),
        (p, *one, *two),
        (shaped(shape, F32), shaped(shape, BF16), shaped((count, 2, block), F32)),
        "mixer_out",
        after=after,
        mib=10,
    )


def input_out_kernel(split, dbx, dby, *refs):
    own_o, other_o = refs[-2:]
    count, half = own_o.shape[:2]
    width = dbx.shape[1]
    for o in range(count):
        one, two = refs[o], refs[count + o]
        part = (
            jnp.dot(dbx[...], one[:width, :], preferred_element_type=F32)
            + jnp.dot(dby[:, :split], one[width + 16 :, :], preferred_element_type=F32)
            + jnp.dot(dby[:, split:], two[: width - split, :], preferred_element_type=F32)
        )
        own_o[o] = part[:half]
        other_o[o] = part[half:].astype(BF16)


def input_out(dbx, dby, one, two, split, after):
    shape = (len(one), dbx.shape[0] // 2, one[0].shape[1])
    return launch(
        lambda *refs: input_out_kernel(split, *refs),
        (dbx, dby, *one, *two),
        (shaped(shape, F32), shaped(shape, BF16)),
        "input_out",
        after=after,
        mib=10,
    )


def pair_kernel(own, got, out):
    out[...] = (own[...] + got[...].astype(F32)).astype(BF16)


def pair_sum(own, got, after):
    return launch(pair_kernel, (own, got), shaped(own.shape, BF16), "pair_sum", after=after)


def relay_kernel(source, out):
    out[...] = source[...]


def relay(source, after):
    return launch(relay_kernel, (source,), shaped(source.shape, source.dtype), "relay", after=after)


def norm_kernel(slots, x, full_gains, *refs):
    h_o, n_o, r_o = refs[-3:]
    ring_size, half, block = h_o.shape
    cut = ring_size // 2 + 1
    groups = [refs[0:2], refs[2:4]]
    squares = jnp.zeros((half, block), F32)
    for o in range(ring_size):
        pair, other = groups[o // cut]
        i = o % cut
        h = x[o, 0:half, :].astype(F32) + (pair[i].astype(F32) + other[i].astype(F32))
        h_o[o] = h
        squares = squares + h * h
    mean = jnp.sum(squares, 1, keepdims=True) * (1.0 / (ring_size * block))
    scale = lax.rsqrt(mean + EPSILON)
    r_o[...] = scale
    for k in range(ring_size):
        o = slots[k]
        gain = full_gains[o, 1:2, :]
        n_o[:, k * block : (k + 1) * block] = (h_o[o] * scale * gain).astype(BF16)


def norm(slots, x, gains, sums, after):
    ring_size, total, block = x.shape
    half = total // 2
    return launch(
        norm_kernel,
        (slots, x, gains, *sums),
        (
            shaped((ring_size, half, block), F32),
            shaped((half, ring_size * block), BF16),
            shaped((half, 1), F32),
        ),
        "norm",
        scalars=1,
        after=after,
    )


def norm_back_kernel(pair, other, h1, r2, gains, g, dh_o, dhr_o, grad_o):
    ring_size, half, block = h1.shape
    dots = jnp.zeros((half, block), F32)
    scale = r2[...]
    for o in range(ring_size):
        product = (pair[o].astype(F32) + other[o].astype(F32)) * h1[o]
        dots = dots + product * gains[o, 1:2, :]
        grad_o[o] = jnp.sum(product * scale, 0, keepdims=True)
    mean = jnp.sum(dots, 1, keepdims=True) * (1.0 / (ring_size * block))
    bend = scale * scale * scale * mean
    for o in range(ring_size):
        grad = pair[o].astype(F32) + other[o].astype(F32)
        dh = g[o, 0:half, :].astype(F32) + scale * (grad * gains[o, 1:2, :]) - h1[o] * bend
        dh_o[o] = dh
        dhr_o[o] = dh.astype(BF16)


def norm_back(pair, other, h1, r2, gains, g, after):
    ring_size, half, block = pair.shape
    return launch(
        norm_back_kernel,
        (pair, other, h1, r2, gains, g),
        (shaped(pair.shape, F32), shaped(pair.shape, BF16), shaped((ring_size, 1, block), F32)),
        "norm_back",
        after=after,
    )


def input_back_kernel(slots, pair, other, x, r1, gains, dh1, second, out_o, grad_o):
    ring_size, half, block = dh1.shape
    dots = jnp.zeros((half, block), F32)
    scale = r1[0:half, :]
    for o in range(ring_size):
        product = (pair[o].astype(F32) + other[o].astype(F32)) * x[o, 0:half, :].astype(F32)
        dots = dots + product * gains[o, 0:1, :]
        grad_o[o, 0:1, :] = jnp.sum(product * scale, 0, keepdims=True)
        grad_o[o, 1:2, :] = second[o]
    mean = jnp.sum(dots, 1, keepdims=True) * (1.0 / (ring_size * block))
    bend = scale * scale * scale * mean
    for k in range(ring_size):
        o = slots[k]
        grad = pair[o].astype(F32) + other[o].astype(F32)
        out_o[:, k * block : (k + 1) * block] = (
            dh1[o] + scale * (grad * gains[o, 0:1, :]) - x[o, 0:half, :].astype(F32) * bend
        )


def input_back(slots, pair, other, x, r1, gains, dh1, second, after):
    ring_size, half, block = pair.shape
    return launch(
        input_back_kernel,
        (slots, pair, other, x, r1, gains, dh1, second),
        (shaped((half, ring_size * block), F32), shaped((ring_size, 2, block), F32)),
        "input_back",
        scalars=1,
        after=after,
    )


def finish_kernel(slots, h1, pair, other, beside, out_o):
    ring_size, half, block = h1.shape
    out_o[0] = beside[...]
    for k in range(ring_size):
        columns = slice(k * block, (k + 1) * block)
        summed = pair[:, columns].astype(F32) + other[:, columns].astype(F32)
        out_o[1, :, columns] = h1[slots[k]] + summed


def finish(slots, h1, pair, other, beside, after):
    return launch(
        finish_kernel,
        (slots, h1, pair, other, beside),
        shaped((2, *beside.shape), F32),
        "finish",
        scalars=1,
        after=after,
        mib=10,
    )


def arrange_kernel(scalars, own, got, *outs):
    core = scalars[0]
    for i, out in enumerate(outs):
        out[core] = own[i]
        out[1 - core] = got[i]


def arrange(scalars, own, got, after):
    out = shaped((2, *own.shape[1:]), own.dtype)
    return launch(
        arrange_kernel, (scalars, own, got), (out,) * own.shape[0], "arrange", scalars=1, after=after, mib=24
    )


def unit_grad_kernel(g, down, dq_o):
    dq_o[...] = lax.dot_general(g[...], down[...], NT, preferred_element_type=F32)


def unit_grad(g, down, after):
    total, model = g.shape
    units = down.shape[0]
    tile = 256
    grid = (
        (units // tile,),
        [pl.BlockSpec((total, model), lambda i: (0, 0)), pl.BlockSpec((tile, model), lambda i: (i, 0))],
        pl.BlockSpec((total, tile), lambda i: (0, i)),
    )
    return launch(unit_grad_kernel, (g, in_hbm(down)), shaped((total, units), F32), "unit_grad", after=after, grid=grid)


def fetch_kernel(gate, up, gate_o, up_o, sems):
    columns = pl.ds(0, gate_o.shape[1])
    copies = [
        pltpu.make_async_copy(source.at[:, columns], target, sems.at[i])
        for i, (source, target) in enumerate(((gate, gate_o), (up, up_o)))
    ]
    for copy in copies:
        copy.start()
    for copy in copies:
        copy.wait()


def fetch(gate, up, after):
    model, units = gate.shape
    whole = pl.BlockSpec(memory_space=pltpu.VMEM)
    anywhere = pl.BlockSpec(memory_space=pl.ANY)
    half = shaped((model, units // 2), BF16)
    return launch(
        fetch_kernel,
        (in_hbm(gate), in_hbm(up)),
        (half, half),
        "fetch",
        after=after,
        scratch=[pltpu.SemaphoreType.DMA((2,))],
        grid=((), [anywhere, anywhere], [whole, whole]),
    )


def unit_products(ga, upward, grad):
    value, slope = gelu_both(ga)
    return value * upward, grad * upward * slope, grad * value


def unit_first_kernel(slots, n2, gate, up, dq, q_o, dga_o, dup_o, rel_o):
    ring_size, total, block = rel_o.shape
    tile = 256
    for i in range(0, gate.shape[1], tile):
        columns = slice(i, i + tile)
        ga = jnp.dot(n2[...], gate[:, columns], preferred_element_type=F32)
        upward = jnp.dot(n2[...], up[:, columns], preferred_element_type=F32)
        for out, item in zip((q_o, dga_o, dup_o), unit_products(ga, upward, dq[:, columns])):
            out[:, columns] = item.astype(BF16)
    for k in range(ring_size):
        rel_o[slots[k]] = n2[:, k * block : (k + 1) * block]


def unit_first(slots, n2, gate, up, dq):
    total, model = n2.shape
    ring_size = slots.shape[0]
    out = shaped((total, gate.shape[1]), BF16)
    return launch(
        unit_first_kernel,
        (slots, n2, gate, up, dq),
        (out, out, out, shaped((ring_size, total, model // ring_size), BF16)),
        "unit_first",
        scalars=1,
        mib=28,
    )


def unit_kernel(n2, gate, up, dq, q_o, dga_o, dup_o):
    ga = jnp.dot(n2[...], gate[...], preferred_element_type=F32)
    upward = jnp.dot(n2[...], up[...], preferred_element_type=F32)
    for out, item in zip((q_o, dga_o, dup_o), unit_products(ga, upward, dq[...])):
        out[...] = item.astype(BF16)


def unit_second(n2, gate, up, dq, after):
    total, model = n2.shape
    share = gate.shape[1] // 2
    tile = 256
    first = share // tile
    wide = pl.BlockSpec((total, tile), lambda i: (0, i))
    tall = pl.BlockSpec((model, tile), lambda i: (0, i + first))
    out = shaped((total, share), BF16)
    grid = (
        (share // tile,),
        [
            pl.BlockSpec((total, model), lambda i: (0, 0)),
            tall,
            tall,
            pl.BlockSpec((total, tile), lambda i: (0, i + first)),
        ],
        [wide, wide, wide],
    )
    return launch(
        unit_kernel,
        (n2, in_hbm(gate), in_hbm(up), dq),
        (out, out, out),
        "unit_second",
        after=after,
        mib=28,
        grid=grid,
    )


def unit_out_kernel(q_a, q_b, down, own_o, other_o):
    half = own_o.shape[0]
    share = q_a.shape[1]
    part = jnp.dot(q_a[...], down[:share, :], preferred_element_type=F32)
    part = part + jnp.dot(q_b[...], down[share:, :], preferred_element_type=F32)
    own_o[...] = part[:half]
    other_o[...] = part[half:].astype(BF16)


def unit_out(q_a, q_b, down, after):
    total, share = q_a.shape
    units, model = down.shape
    half = total // 2
    tile = 256
    out = pl.BlockSpec((half, tile), lambda i: (0, i))
    left = pl.BlockSpec((total, share), lambda i: (0, 0))
    grid = ((model // tile,), [left, left, pl.BlockSpec((units, tile), lambda i: (0, i))], [out, out])
    return launch(
        unit_out_kernel,
        (q_a, q_b, in_hbm(down)),
        (shaped((half, model), F32), shaped((half, model), BF16)),
        "unit_out",
        after=after,
        grid=grid,
    )


def unit_back_kernel(owners, dga_a, dga_b, dup_a, dup_b, gate, up, *refs):
    own_o, other_o = refs[-2:]
    half = other_o.shape[1]
    share = dga_a.shape[1]
    part = None
    for left, right in (
        (dga_a, gate[:, :share]),
        (dga_b, gate[:, share:]),
        (dup_a, up[:, :share]),
        (dup_b, up[:, share:]),
    ):
        term = lax.dot_general(left[...], right, NT, preferred_element_type=F32)
        part = term if part is None else part + term
    own_o[0] = part[:half]
    other_o[0] = part[half:].astype(BF16)


def unit_back(owners, grads, gate, up, after):
    ring_size = owners.shape[0]
    total, share = grads[0].shape
    model, units = gate.shape
    half = total // 2
    block = model // ring_size
    left = pl.BlockSpec((total, share), lambda o, owners: (0, 0))
    weight = pl.BlockSpec((block, units), lambda o, owners: (owners[o], 0))
    out = pl.BlockSpec((1, half, block), lambda o, owners: (o, 0, 0))
    return pl.pallas_call(
        unit_back_kernel,
        grid_spec=pltpu.PrefetchScalarGridSpec(
            num_scalar_prefetch=1,
            grid=(ring_size,),
            in_specs=[left] * 4 + [weight, weight, *[pl.BlockSpec(memory_space=pl.ANY)] * len(after)],
            out_specs=[out, out],
        ),
        out_shape=(shaped((ring_size, half, block), F32), shaped((ring_size, half, block), BF16)),
        compiler_params=pltpu.CompilerParams(vmem_limit_bytes=24 << 20),
        cost_estimate=pl.CostEstimate(flops=1, bytes_accessed=1, transcendentals=0),
        name="unit_back",
    )(owners, *grads, in_hbm(gate), in_hbm(up), *after)


def unit_term_kernel(turns, fold, n2, g, dga, dup, q, *refs):
    share = q.shape[1]
    rest = list(refs)
    outs = rest[len(rest) - len(turns) - (3 if fold else 0) :]
    parts = [slice(i * share, (i + 1) * share) for i in range(3)]

    def terms(o):
        return (
            lax.dot_general(n2[o], dga[...], TN, preferred_element_type=F32),
            lax.dot_general(n2[o], dup[...], TN, preferred_element_type=F32),
        )

    for (o, has), out in zip(turns, outs):
        recv = rest.pop(0) if has else None
        down = lax.dot_general(g[o], q[...], TN, preferred_element_type=F32)
        for grad, columns in zip((*terms(o), down), parts):
            if recv is not None:
                grad = grad + recv[:, columns].astype(F32)
            out[:, columns] = grad.astype(BF16)
    if fold:
        recv = rest.pop(0)
        gate_o, up_o, down_o = outs[len(turns) :]
        for grad, columns, out in zip(terms(0), parts, (gate_o, up_o)):
            out[...] = grad + recv[:, columns].astype(F32)
        down = lax.dot_general(q[...], g[0], TN, preferred_element_type=F32)
        down_o[...] = down + recv[:, parts[2]].astype(F32).T


def unit_term(n2, g, dga, dup, q, turns, fold, after, weight):
    block, share = n2.shape[2], q.shape[1]
    arrived = [item for _, item in turns if item is not None] + ([] if fold is None else [fold])
    plan = [(o, item is not None) for o, item in turns]
    out = [shaped((block, 3 * share), BF16) for _ in turns]
    if fold is not None:
        out += [shaped((block, share), F32), shaped((block, share), F32), shaped((share, block), F32)]
    return launch(
        lambda *refs: unit_term_kernel(plan, fold is not None, *refs),
        (n2, g, dga, dup, q, *arrived),
        tuple(out),
        "unit_term",
        after=after,
        mib=10,
        flops=weight,
    )


def unit_end_kernel(count, *refs):
    own, item, low, outs = refs[:3], refs[3], refs[4 : 4 + count], refs[4 + count :]
    share = own[0].shape[1]
    for i in range(2):
        total = own[i][...] + item[:, i * share : (i + 1) * share].astype(F32)
        if count:
            outs[i][:, :share] = low[i][...]
            outs[i][:, share:] = total
        else:
            outs[i][...] = total
    total = own[2][...] + item[:, 2 * share :].astype(F32).T
    if count:
        outs[2][:share, :] = low[2][...]
        outs[2][share:, :] = total
    else:
        outs[2][...] = total


def unit_end(low, own, item, after):
    block, share = own[0].shape
    wide = 2 if low else 1
    grad = shaped((block, wide * share), F32)
    return launch(
        lambda *refs: unit_end_kernel(len(low), *refs),
        (*own, item, *low),
        (grad, grad, shaped((wide * share, block), F32)),
        "unit_end",
        after=after,
        flops=END_WEIGHT,
    )


def small_pieces(width, block):
    return [slice(i, min(i + block, width)) for i in range(0, width, block)]


def mixer_term_kernel(part, places, groups, split, chunk, turns, fold, owners, *refs):
    n1_all = refs[:groups]
    dhr, grads, p = refs[groups : groups + 3]
    rest = list(refs[groups + 3 :])
    extra = rest.pop(0) if part == 0 else None
    outs = rest[len(rest) - len(turns) - (3 - part if fold else 0) :]
    width, block = grads.shape[1], dhr.shape[2]
    columns = slice(0, split) if part == 0 else slice(split, width)
    size = columns.stop - columns.start
    at = width + size
    pieces = small_pieces(width, block)

    def terms(o, recv):
        group, i = places[o]
        grad = lax.dot_general(grads[...], n1_all[group][i], TN, preferred_element_type=F32)
        out = lax.dot_general(p[:, columns], dhr[o], TN, preferred_element_type=F32)
        if recv is not None:
            grad = grad + recv[:width, :].astype(F32)
            out = out + recv[width:at, :].astype(F32)
        return grad, out

    def small(o, recv):
        own = extra[pl.ds(pl.multiple_of(owners[o] * chunk, 16), chunk), :].astype(F32)
        out = []
        for i, piece in enumerate(pieces):
            total = own[:, piece]
            if recv is not None:
                total = total + recv[at + i * chunk : at + (i + 1) * chunk, : piece.stop - piece.start].astype(F32)
            out.append(total)
        return out

    for (o, has), out_ref in zip(turns, outs):
        recv = rest.pop(0) if has else None
        grad, out = terms(o, recv)
        out_ref[:width, :] = grad.astype(BF16)
        out_ref[width:at, :] = out.astype(BF16)
        if part == 0:
            for i, total in enumerate(small(o, recv)):
                rows = slice(at + i * chunk, at + (i + 1) * chunk)
                wide = total.shape[1]
                out_ref[rows, :wide] = total.astype(BF16)
                if wide < block:
                    out_ref[rows, wide:] = jnp.zeros((chunk, block - wide), BF16)
    if fold:
        recv = rest.pop(0)
        outs[len(turns)][...], outs[len(turns) + 1][...] = terms(0, recv)
        if part == 0:
            for piece, total in zip(pieces, small(0, recv)):
                outs[len(turns) + 2][:, piece] = total


def mixer_term(part, places, split, chunk, owners, n1, dhr, grads, p, extra, turns, fold, after, weight):
    block, width = dhr.shape[2], grads.shape[1]
    size = split if part == 0 else width - split
    arrived = [item for _, item in turns if item is not None] + ([] if fold is None else [fold])
    more = 0 if part == 1 else chunk * len(small_pieces(width, block))
    out = [shaped((width + size + more, block), BF16) for _ in turns]
    if fold is not None:
        out += [shaped((width, block), F32), shaped((size, block), F32)]
        out += [shaped((chunk, width), F32)] if part == 0 else []
    plan = [(o, item is not None) for o, item in turns]
    return launch(
        lambda *refs: mixer_term_kernel(part, places, len(n1), split, chunk, plan, fold is not None, *refs),
        (owners, *n1, dhr, grads, p, *([extra] if part == 0 else []), *arrived),
        tuple(out),
        "mixer_term",
        scalars=1,
        after=after,
        mib=10,
        flops=weight,
    )


def mixer_end_kernel(part, *refs):
    own, item = refs[: 3 - part], refs[3 - part]
    extra, outs = refs[4 - part : 6 - 2 * part], refs[6 - 2 * part :]
    width, block = own[0].shape
    at = width + own[1].shape[0]
    outs[0][...] = own[0][...] + item[:width, :].astype(F32)
    total = own[1][...] + item[width:at, :].astype(F32)
    if part == 1:
        low = extra[0]
        split = low.shape[0]
        outs[1][:split, :] = low[...]
        outs[1][split:, :] = total
        return
    outs[1][...] = total
    chunk = own[2].shape[0]
    for i, piece in enumerate(small_pieces(width, block)):
        rows = slice(at + i * chunk, at + (i + 1) * chunk)
        total = own[2][:, piece] + item[rows, : piece.stop - piece.start].astype(F32)
        outs[2][:chunk, piece] = total.astype(BF16)
    ring_size = extra[0].shape[0]
    lines = [extra[0][o] + extra[1][o] for o in range(ring_size)]
    for g in range(2):
        gain = jnp.concatenate([line[g : g + 1, :] for line in lines], 0)
        outs[2][chunk:, g * block : (g + 1) * block] = gain.astype(BF16)
    outs[2][chunk:, 2 * block :] = jnp.zeros((ring_size, width - 2 * block), BF16)


def mixer_end(part, extra, own, item, after):
    width, block = own[0].shape
    if part == 0:
        rows = own[2].shape[0] + extra[0].shape[0]
        shapes = [own[0].shape, own[1].shape, (rows, width)]
    else:
        shapes = [own[0].shape, own[0].shape]
    return launch(
        lambda *refs: mixer_end_kernel(part, *refs),
        (*own, item, *extra),
        tuple(shaped(shape, BF16 if i == 2 else F32) for i, shape in enumerate(shapes)),
        "mixer_end",
        after=after,
        flops=HEAVY,
    )


def spread_kernel(head, owners, *refs):
    ring_size = owners.shape[0]
    gate_i, gate_r, taps, sums, gain_o, whole = refs[ring_size:]
    block = gain_o.shape[1]
    chunk = refs[0].shape[0] - ring_size
    gains = [jnp.zeros((1, block), F32) for _ in range(2)]
    for o in range(ring_size):
        at = pl.ds(pl.multiple_of(owners[o] * chunk, 16), chunk)
        whole[at, :] = refs[o][:chunk, :].astype(F32)
        mine = (ring_size - o) % ring_size
        lines = refs[o][chunk:, : 2 * block].astype(F32)[mine : mine + 1, :]
        gains = [gains[g] + lines[:, g * block : (g + 1) * block] for g in range(2)]
    gate_i[...] = whole[:head, :]
    gate_r[...] = whole[head : 2 * head, :]
    count = taps.shape[0]
    taps[...] = whole[2 * head : 2 * head + count, :]
    sums[...] = whole[2 * head + count : 2 * head + SUMS, :]
    gain_o[...] = jnp.concatenate(gains, 0)


def spread(head, count, block, owners, chunks, after):
    ring_size = len(chunks)
    rows, width = chunks[0].shape
    gate = shaped((head, width), F32)
    return launch(
        lambda *refs: spread_kernel(head, *refs),
        (owners, *chunks),
        (gate, gate, shaped((count, width), F32), shaped((SUMS - count, width), F32), shaped((2, block), F32)),
        "spread",
        scalars=1,
        after=after,
        scratch=[pltpu.VMEM(((rows - ring_size) * ring_size, width), F32)],
    )


def local(
    tokens,
    cotangent,
    row_length,
    first_gain,
    value_weight,
    gelu_weight,
    conv_weight,
    conv_bias,
    input_gate,
    input_bias,
    recur_gate,
    recur_bias,
    decay_param,
    output_weight,
    second_gain,
    mlp_gate,
    mlp_up,
    mlp_down,
):
    ring_size = lax.axis_size("dp")
    middle = ring_size // 2
    ring = [2 * i if i < middle else 2 * (ring_size - 1 - i) + 1 for i in range(ring_size)]
    onward = [(ring[i], ring[(i + 1) % ring_size]) for i in range(ring_size)]
    backward = [(b, a) for a, b in onward]
    me = lax.axis_index("dp")
    core = lax.axis_index("mp") % 2
    core_pair = [(i, i ^ 1) for i in range(4)]
    chip_pair = [(i, i ^ 2) for i in range(4)]
    index = jnp.arange(ring_size, dtype=jnp.int32)

    def spot_of(place):
        return jnp.where(place % 2 == 0, place // 2, ring_size - 1 - place // 2)

    spots = (spot_of(me) + index) % ring_size
    owners = jnp.where(spots < middle, 2 * spots, 2 * (ring_size - 1 - spots) + 1).astype(jnp.int32)
    slots = ((spot_of(index) - spot_of(me) + ring_size) % ring_size).astype(jnp.int32)

    subs, row_count, length, model = tokens.shape
    half = row_count * length
    seqs = subs * row_count
    block = model // ring_size
    width, head = input_gate.shape
    count = conv_weight.shape[0]
    split = width // 2 // 128 * 128
    chunk = -(-(2 * head + SUMS) // (16 * ring_size)) * 16
    small_rows = chunk * ring_size

    def hops(long_way_on):
        return (middle, ring_size - 1 - middle) if long_way_on else (ring_size - 1 - middle, middle)

    token = []

    def mark(*values):
        token[:] = values

    class Gather:
        def __init__(self, shard, long_way_on):
            self.hops = hops(long_way_on)
            self.moving = [shard, shard]
            self.got = [shard] + [None] * (ring_size - 1)

        def step(self, s):
            for d, way in enumerate((onward, backward)):
                if s <= self.hops[d]:
                    self.moving[d] = lax.ppermute(self.moving[d], "dp", way)
                    self.got[ring_size - s if d == 0 else s] = self.moving[d]

    class Scatter:
        def __init__(self, term, end, long_way_on):
            self.term, self.ending = term, end
            self.hops = hops(long_way_on)
            self.moving = [None, None]
            self.own = None

        def step(self, s, weight=HEAVY, apart=False):
            turns, ways, fold = [], [], None
            for d in range(2):
                far = self.hops[d] - s
                if far > 0:
                    turns.append((far if d == 0 else ring_size - far, self.moving[d]))
                    ways.append(d)
                elif far == 0:
                    fold = self.moving[d]
            parts = self.term(turns, None if apart else fold, tuple(token), weight)
            mark(parts[0])
            for d, part in zip(ways, parts):
                self.moving[d] = lax.ppermute(part, "dp", (onward, backward)[d])
            if fold is not None:
                self.own = parts[len(turns) :]
                if apart:
                    self.own = self.term([], fold, tuple(token), weight)
                    mark(self.own[0])

        def end(self, *low):
            last = 0 if self.hops[0] > self.hops[1] else 1
            out = self.ending(low, self.own, self.moving[last], tuple(token))
            mark(out[0])
            return out

    def core_swap(other):
        return lax.ppermute(other, "mp", core_pair)

    def chip_swap(own, got, after):
        pair = pair_sum(own, got, after)
        mark(pair)
        return pair, lax.ppermute(pair, "mp", chip_pair)

    def both_halves(own, dim):
        return jnp.concatenate([own, lax.ppermute(own, "mp", core_pair)], dim)

    scalars = jnp.concatenate([core[None], row_length.reshape(-1)]).astype(jnp.int32)
    shard_one, shard_two = pack(
        split, value_weight.T, gelu_weight.T, output_weight, first_gain[None], second_gain[None]
    )
    ring_one, ring_two = Gather(shard_one, True), Gather(shard_two, False)
    ring_one.step(1)
    ring_two.step(1)

    decay_wide = decay_param.astype(F32)
    lines = jnp.concatenate(
        [
            conv_weight.astype(F32),
            jnp.stack(
                [
                    conv_bias.astype(F32),
                    input_bias.astype(F32),
                    recur_bias.astype(F32),
                    jax.nn.softplus(-decay_wide),
                    jax.nn.sigmoid(-decay_wide),
                ]
            ),
        ]
    )
    x, g, g_flat, r1, blocks_i, blocks_r = prepare(
        scalars,
        slots,
        tokens.reshape(subs, half, model),
        cotangent.reshape(subs, half, model),
        input_gate.T,
        recur_gate.T,
        (lines,),
    )
    x, *moved = lax.optimization_barrier((x, *ring_one.moving, *ring_two.moving))
    ring_one.moving, ring_two.moving = moved[:2], moved[2:]
    for s in range(2, middle + 1):
        ring_one.step(s)
        ring_two.step(s)
    one, two = ring_one.got, ring_two.got

    hop_groups = [[0, 1, ring_size - 1]] + [[s, ring_size - s] for s in range(2, middle)] + [[middle]]
    places, n1, sums_so_far = {}, [], None
    for place, offsets in enumerate(hop_groups):
        bx, by, n1_part = project(
            offsets, x, r1, [one[o] for o in offsets], [two[o] for o in offsets], sums_so_far, width, split
        )
        sums_so_far = (bx, by)
        n1.append(n1_part)
        places |= {o: (place, i) for i, o in enumerate(offsets)}

    p, cx, lx, lr, h = mixer_forward(seqs, count, bx, by, lines, blocks_i, blocks_r)
    cut = ring_size // 2 + 1
    own_a, other_a, gains_a = mixer_out(p, one[:cut], two[:cut], split, ())
    got_a = core_swap(other_a)
    own_b, other_b, gains_b = mixer_out(p, one[cut:], two[cut:], split, (own_a,))
    sums_a = chip_swap(own_a, got_a, (own_b,))
    sums_b = chip_swap(own_b, core_swap(other_b), tuple(token))
    gains = jnp.concatenate([gains_a, gains_b])
    dq = unit_grad(g_flat, mlp_down, tuple(token))
    fetched = fetch(mlp_gate, mlp_up, (dq,))
    h1, n2_own, r2 = norm(slots, x, gains, (*sums_a, *sums_b), (fetched[0],))
    n2 = both_halves(n2_own, 0)
    q_a, dga_a, dup_a, n2_rel = unit_first(slots, n2, *fetched, dq)
    unit_a = Scatter(lambda *a: unit_term(n2_rel, g, dga_a, dup_a, q_a, *a), unit_end, True)
    unit_a.step(0)
    q_b, dga_b, dup_b = unit_second(n2, mlp_gate, mlp_up, dq, tuple(token))
    unit_b = Scatter(lambda *a: unit_term(n2_rel, g, dga_b, dup_b, q_b, *a), unit_end, False)
    unit_b.step(0, 1)
    last = middle - 1

    def now():
        return tuple(token)

    own, other = unit_back(owners, (dga_a, dga_b, dup_a, dup_b), mlp_gate, mlp_up, now())
    mark(own)
    got = core_swap(other)
    for s in range(1, max(last - 1, 1)):
        unit_a.step(s)
        if s == 1:
            pair, other = chip_swap(own, got, now())
        unit_b.step(s)
    unit_a.step(last - 1)
    dh1, dhr_own, second_grad = norm_back(pair, other, h1, r2, gains, g, now())
    mark(dhr_own)
    dhr = both_halves(dhr_own, 1)
    unit_b.step(last - 1)
    dbx, dby, small = mixer_backward(
        seqs, head, count, split, small_rows, dhr, two, (bx, by, cx, lx, lr, h, lines, blocks_i, blocks_r), now()
    )
    mark(dbx)
    half_split = width // 2 // 128 * 128
    mixer_a = Scatter(
        lambda *a: mixer_term(0, places, half_split, chunk, owners, n1, dhr, dbx, p, small, *a),
        lambda *a: mixer_end(0, *a),
        True,
    )
    mixer_b = Scatter(
        lambda *a: mixer_term(1, places, half_split, chunk, owners, n1, dhr, dby, p, None, *a),
        lambda *a: mixer_end(1, *a),
        False,
    )
    mixer_a.step(0)
    unit_a.step(last)
    out_own, out_other = unit_out(q_a, q_b, mlp_down, now())
    mark(out_own)
    layer_pair = pair_sum(out_own, core_swap(out_other), now())
    mark(layer_pair)
    own, other = input_out(dbx, dby, one, two, split, now())
    mark(own)
    got = core_swap(other)
    unit_b.step(last)
    pair, other = chip_swap(own, got, now())
    mixer_a.step(1)
    low = unit_a.end()
    mixer_b.step(0, 1)
    gate_grad, up_grad, down_grad = unit_b.end(*low)
    input_own, gain_grads = input_back(slots, pair, other, x, r1, gains, dh1, second_grad, now())
    mark(input_own)
    layer_pair = relay(layer_pair, now())
    mark(layer_pair)
    layer_other = lax.ppermute(layer_pair, "mp", chip_pair)
    gain_got = core_swap(gain_grads)
    for s in range(2, middle):
        mixer_a.step(s)
        if s == middle - 1:
            both_own = finish(slots, h1, layer_pair, layer_other, input_own, now())
            mark(both_own)
        mixer_b.step(s - 1)
    input_grad, layer_out = arrange(scalars, both_own, core_swap(both_own), now())
    mark(layer_out)
    value_grad, output_low, small = mixer_a.end(gain_grads, gain_got)
    small_ring = Gather(small, True)
    mixer_b.step(last, 1, True)
    for s in range(1, middle + 1):
        small_ring.step(s)
    gelu_grad, output_grad = mixer_b.end(output_low)
    gate_i, gate_r, taps_grad, sums, gain_grads = spread(head, count, block, owners, small_ring.got, now())

    return (
        layer_out.reshape(tokens.shape),
        input_grad.reshape(tokens.shape),
        gain_grads[0],
        value_grad.T,
        gelu_grad.T,
        taps_grad,
        sums[0],
        gate_i.T,
        sums[1],
        gate_r.T,
        sums[2],
        sums[3],
        output_grad,
        gain_grads[1],
        gate_grad,
        up_grad,
        down_grad,
    )


def solution(mesh):
    placed = (
        P(None, "dp", None, None),
        P(None, "dp", None, None),
        P(None, "dp"),
        P("dp"),
        P("dp", "mp"),
        P("dp", "mp"),
        P(None, "mp"),
        P("mp"),
        P("mp", None),
        P("mp"),
        P("mp", None),
        P("mp"),
        P("mp"),
        P("mp", "dp"),
        P("dp"),
        P(None, "mp"),
        P(None, "mp"),
        P("mp", None),
    )
    return jax.shard_map(
        local,
        mesh=mesh,
        in_specs=placed,
        out_specs=(
            P(None, "dp", None, None),
            P(None, "dp", None, None),
            P("dp"),
            P("dp", "mp"),
            P("dp", "mp"),
            P(None, "mp"),
            P("mp"),
            P("mp", None),
            P("mp"),
            P("mp", None),
            P("mp"),
            P("mp"),
            P("mp", "dp"),
            P("dp"),
            P("dp", "mp"),
            P("dp", "mp"),
            P("mp", "dp"),
        ),
        check_vma=False,
    )
```
